32 devices in a mesh: fsdp: 8 (over z, y), seq: 4 (over x, core).
Axes of the slice: x: 2, y: 2, z: 4, core: 2. Of those that a mesh axis runs over, the one named last changes fastest.
Arguments:
- tokens: bfloat16 [16, 1024, 1024], P('fsdp', 'seq'), may hold values from -6 to 6
- cotangent: bfloat16 [16, 1024, 1024], P('fsdp', 'seq'), may hold values from -6 to 6
- lengths: int32 [16], P('fsdp'), may hold values from 256 to 1024, as said below
- first_gain: bfloat16 [1024], P('fsdp'), may hold values from 0.25 to 1.75
- first_shift: bfloat16 [1024], P('fsdp'), may hold values from -3 to 3
- qkv_weight: bfloat16 [1024, 3072], P('fsdp'), may hold values from -0.1875 to 0.1875
- qv_bias: bfloat16 [2, 1024], P(None, 'fsdp'), may hold values from -3 to 3
- out_weight: bfloat16 [1024, 1024], P('fsdp'), may hold values from -0.375 to 0.375
- out_bias: bfloat16 [1024], P('fsdp'), may hold values from -2 to 2
- second_gain: bfloat16 [1024], P('fsdp'), may hold values from 0.25 to 1.75
- second_shift: bfloat16 [1024], P('fsdp'), may hold values from -3 to 3
- up_weight: bfloat16 [1024, 4096], P('fsdp'), may hold values from -0.1875 to 0.1875
- up_bias: bfloat16 [4096], P('fsdp'), may hold values from -3 to 3
- down_weight: bfloat16 [4096, 1024], P('fsdp'), may hold values from -0.09375 to 0.09375
- down_bias: bfloat16 [1024], P('fsdp'), may hold values from -2 to 2
Outputs:
- block_out: bfloat16 [16, 1024, 1024], P('fsdp', 'seq')
- tokens_grad: bfloat16 [16, 1024, 1024], P('fsdp', 'seq')
- first_gain_grad: float32 [1024], P(('fsdp', 'seq'))
- first_shift_grad: float32 [1024], P(('fsdp', 'seq'))
- qkv_weight_grad: float32 [1024, 3072], P(('fsdp', 'seq'))
- qv_bias_grad: float32 [2, 1024], P(None, ('fsdp', 'seq'))
- out_weight_grad: float32 [1024, 1024], P(('fsdp', 'seq'))
- out_bias_grad: float32 [1024], P(('fsdp', 'seq'))
- second_gain_grad: float32 [1024], P(('fsdp', 'seq'))
- second_shift_grad: float32 [1024], P(('fsdp', 'seq'))
- up_weight_grad: float32 [1024, 4096], P(('fsdp', 'seq'))
- up_bias_grad: float32 [4096], P(('fsdp', 'seq'))
- down_weight_grad: float32 [4096, 1024], P(('fsdp', 'seq'))
- down_bias_grad: float32 [1024], P(('fsdp', 'seq'))
The draws below stay inside these ranges and needn't reach their ends.
Inputs may be any that keep to these rules, and one draw needn't show every extreme that they name: `lengths`: at least a quarter of 1024; in every draw some sequence has all 1024 slots valid.
All inputs are finite; a program needn't handle non-finite values.
Results may differ from the reference program's by a relative error of at most 0.011.
Values may be sent and summed in bfloat16 or wider, within the bound.
No kernel may reach another device: no remote copies, remote signals or barrier semaphores. Data moves between devices by JAX's collectives and lax.ppermute only.
A program may use at most 256 MiB of HBM per device.

```python
import math
import jax
import jax.numpy as jnp
from jax import lax

D = 1024
H = 16
FF = 4096
L = 1024
SEQS = 16


def draw_lengths(key, part):
    key_values, key_place = jax.random.split(key)
    values = jax.random.randint(key_values, (SEQS,), L // 4, L + 1)
    fullest = jax.random.randint(key_place, (), 0, SEQS)
    return jnp.where(jnp.arange(SEQS) == fullest, L, values).astype(jnp.int32)


def strengthened(array, rng, source, target, blocks, factor):
    owner, partner = [(jnp.arange(array.shape[axis_at]) // (array.shape[axis_at] // blocks)).reshape([-1 if axis == axis_at else 1 for axis in range(array.ndim)]) for axis_at in (source, target)]
    chosen = jax.random.permutation(rng, blocks)[partner]
    strong = (owner == chosen) | (owner == (partner + blocks // 2) % blocks)
    return jnp.where(strong, factor * array, array)


def shard_levels(key, dims, shards, low, high):
    gain = 1.0
    for axis_at, parts in shards:
        draws = jax.random.uniform(jax.random.fold_in(jax.random.fold_in(key, 6), axis_at), (parts,), jnp.float32, low / len(shards), high / len(shards))
        gain = gain * jnp.repeat(jnp.exp(draws), dims[axis_at] // parts).reshape((-1,) + (1,) * (len(dims) - 1 - axis_at))
    return gain


def noise(own_key, extent, spread, reach, cuts=(), held_as=jnp.bfloat16):
    drawn = jax.random.normal(own_key, extent, jnp.float32) * spread
    if len(cuts) > 0:
        drawn = shard_levels(own_key, extent, cuts, -0.22, 0.18) * drawn
    return jnp.clip(drawn, min=-reach, max=reach).astype(held_as)


def heavy_noise(stream_key, dims, deviation, bound, cuts, heavy, kind=jnp.bfloat16):
    values = deviation * jax.random.normal(stream_key, dims, jnp.float32)
    if cuts:
        values = values * shard_levels(stream_key, dims, cuts, -0.22, 0.18)
    return jnp.clip(strengthened(values, jax.random.fold_in(stream_key, 3), *heavy), -bound, bound).astype(kind)


def setup_inputs(seed: int = 0) -> dict:
    seeds = jax.random.split(jax.random.key(seed), 16)
    tokens = noise(seeds[0], (SEQS, L, D), 1.0, 6.0, ((0, 8), (1, 4)))
    cotangent = heavy_noise(seeds[1], (SEQS, L, D), 1.0, 6.0, ((0, 8), (1, 4)), (1, 2, 4, 2.0))
    lengths = draw_lengths(jax.random.fold_in(seeds[15], 71), 0)
    first_gain = jnp.clip(1.0 + 0.15 * jax.random.normal(seeds[3], (D,), jnp.float32), 0.25, 1.75).astype(jnp.bfloat16)
    first_shift = noise(seeds[4], (D,), 0.5, 3.0, ((0, 8),))
    qkv_weight = noise(seeds[5], (D, 3 * D), D ** -0.5, 0.1875, ((0, 8),))
    qv_bias = noise(seeds[6], (2, D), 0.5, 3.0, ((1, 8),))
    out_weight = noise(seeds[7], (D, D), (D // 4) ** -0.5, 0.375, ((0, 8),))
    out_bias = noise(seeds[8], (D,), 0.3, 2.0, ((0, 8),))
    second_gain = jnp.clip(1.0 + 0.15 * jax.random.normal(seeds[9], (D,), jnp.float32), 0.25, 1.75).astype(jnp.bfloat16)
    second_shift = noise(seeds[10], (D,), 0.5, 3.0, ((0, 8),))
    up_weight = noise(seeds[11], (D, FF), D ** -0.5, 0.1875, ((0, 8),))
    up_bias = noise(seeds[12], (FF,), 0.5, 3.0, ((0, 8),))
    down_weight = noise(seeds[13], (FF, D), FF ** -0.5, 0.09375, ((0, 8),))
    down_bias = noise(seeds[14], (D,), 0.3, 2.0, ((0, 8),))
    return {"tokens": tokens, "cotangent": cotangent, "lengths": lengths, "first_gain": first_gain, "first_shift": first_shift, "qkv_weight": qkv_weight, "qv_bias": qv_bias, "out_weight": out_weight, "out_bias": out_bias, "second_gain": second_gain, "second_shift": second_shift, "up_weight": up_weight, "up_bias": up_bias, "down_weight": down_weight, "down_bias": down_bias}


@jax.custom_vjp
def low(v):
    return lax.optimization_barrier(v.astype(jnp.bfloat16)).astype(jnp.float32)

@jax.custom_vjp
def low_back(v):
    return v

def low_keep(v):
    return (low(v), None)

def low_pass(kept, grad):
    return (grad,)

def back_keep(v):
    return (v, None)

def back_low(kept, grad):
    return (low(grad),)
low.defvjp(low_keep, low_pass)
low_back.defvjp(back_keep, back_low)
highest = lax.Precision.HIGHEST
epsilon = 1e-05

def matmul(left_side, right_side):
    return jnp.dot(left_side, right_side, preferred_element_type=jnp.float32, precision=highest)

def layer_norm(values, norm_gain, norm_shift):
    row_mean = lax.optimization_barrier(jnp.mean(values, axis=-1, keepdims=True))
    centered = values - row_mean
    variance = lax.optimization_barrier(jnp.mean(centered * centered, axis=-1, keepdims=True))
    return centered * lax.rsqrt(variance + epsilon) * norm_gain + norm_shift

def attention(queries, key_rows, value_rows, length):
    head_count, seq_len, head_size = queries.shape
    block_size = math.gcd(512, seq_len)
    score_scale = head_size ** (-0.5)
    slopes = jnp.exp2(-(jnp.arange(head_count, dtype=jnp.float32) + 1.0) * 8.0 / head_count)
    columns = jnp.arange(seq_len).astype(jnp.int32)

    def one_block(start_row):
        row_index = start_row + jnp.arange(block_size).astype(jnp.int32)
        query_block = lax.dynamic_slice_in_dim(queries, start_row, block_size, 1)
        products = jnp.einsum('hqd,hkd->hqk', query_block, key_rows, precision=highest)
        distance = (columns[None, :] - row_index[:, None]).astype(jnp.float32)
        scores = low_back(products * score_scale + slopes[:, None, None] * distance)
        allowed = (columns[None, :] <= row_index[:, None]) & (columns[None, :] < length)
        scores = jnp.where(allowed[None], scores, -jnp.inf)
        largest = lax.optimization_barrier(jnp.max(scores, axis=-1, keepdims=True))
        weights = jnp.exp(scores - largest)
        attention_probs = low(weights / lax.optimization_barrier(jnp.sum(weights, axis=-1, keepdims=True)))
        return jnp.einsum('hqk,hkd->hqd', attention_probs, value_rows, precision=highest)
    starts = (jnp.arange(seq_len // block_size) * block_size).astype(jnp.int32)
    blocks = lax.map(jax.checkpoint(one_block), starts)
    return jnp.moveaxis(blocks, 0, 1).reshape(head_count, seq_len, head_size)

def forward(token_rows, length, params):
    first_gain, first_shift, qkv_weight, qv_bias, out_weight, out_bias, second_gain, second_shift, up_weight, up_bias, down_weight, down_bias = params
    seq_len, model_width = token_rows.shape
    head_size = model_width // H
    valid_mask = (jnp.arange(seq_len).astype(jnp.int32) < length).astype(jnp.float32)[:, None]
    normed = low(layer_norm(token_rows, first_gain, first_shift))
    bias_columns = jnp.stack([qv_bias[0].reshape(H, head_size), jnp.zeros((H, head_size), jnp.float32), qv_bias[1].reshape(H, head_size)], axis=1).reshape(3 * model_width)
    projected = low(low_back(matmul(normed, qkv_weight) + bias_columns)).reshape(seq_len, H, 3, head_size)
    by_head = jnp.moveaxis(projected, 0, 2)
    mixed_heads = attention(by_head[:, 0], by_head[:, 1], by_head[:, 2], length)
    mixed_rows = low(low_back(jnp.moveaxis(mixed_heads, 0, 1).reshape(seq_len, model_width)))
    middle = token_rows + low_back(matmul(mixed_rows, out_weight) + out_bias)
    normed_two = low(layer_norm(middle, second_gain, second_shift))
    hidden_pre = low_back(matmul(normed_two, up_weight) + up_bias)
    activation = low(jax.nn.gelu(hidden_pre, approximate=True))
    return valid_mask * (middle + matmul(activation, down_weight) + down_bias)

def reference(tokens, cotangent, lengths, first_gain, first_shift, qkv_weight, qv_bias, out_weight, out_bias, second_gain, second_shift, up_weight, up_bias, down_weight, down_bias):
    params = tuple((member.astype(jnp.float32) for member in (first_gain, first_shift, qkv_weight, qv_bias, out_weight, out_bias, second_gain, second_shift, up_weight, up_bias, down_weight, down_bias)))
    totals = tuple((jnp.zeros_like(member) for member in params))

    def per_sequence(carried, inputs):
        token_rows, grad_rows, length = inputs

        def run_layer(row_values, param_values):
            return forward(row_values, length, param_values)
        outputs, pull_back = jax.vjp(run_layer, token_rows.astype(jnp.float32), params)
        row_grad, param_grads = pull_back(grad_rows.astype(jnp.float32))
        carried = tuple((left_term + right_term for left_term, right_term in zip(carried, param_grads)))
        return (carried, (outputs.astype(jnp.bfloat16), row_grad.astype(jnp.bfloat16)))
    totals, (block_out, tokens_grad) = lax.scan(per_sequence, totals, (tokens, cotangent, lengths))
    return (block_out, tokens_grad, totals[0], totals[1], totals[2], totals[3], totals[4], totals[5], totals[6], totals[7], totals[8], totals[9], totals[10], totals[11])
```

```python
from functools import partial
import math

import jax
import jax.numpy as jnp
from jax import lax
from jax.experimental import pallas as pl
from jax.experimental.pallas import tpu as pltpu
from jax.sharding import PartitionSpec as P

H = 16


epsilon = 1e-05
f32 = jnp.float32
bf16 = jnp.bfloat16


def layer_norm(values, norm_gain, norm_shift):
    row_mean = jnp.mean(values, axis=-1, keepdims=True)
    centered = values - row_mean
    variance = jnp.mean(centered * centered, axis=-1, keepdims=True)
    return centered * lax.rsqrt(variance + epsilon) * norm_gain + norm_shift


def product(left_side, right_side):
    return jnp.dot(left_side, right_side, preferred_element_type=f32)


def contract_rows(left_side, right_side):
    return lax.dot_general(
        left_side, right_side, (((0,), (0,)), ((), ())), preferred_element_type=f32
    )


def against(left_side, right_side):
    return lax.dot_general(
        left_side, right_side, (((1,), (1,)), ((), ())), preferred_element_type=f32
    )


def head_scores(query_block, key_rows, start_row, slopes, length, score_scale):
    block_size = query_block.shape[1]
    seq_len = key_rows.shape[1]
    row_index = start_row + jnp.arange(block_size)
    columns = jnp.arange(seq_len)
    products = jnp.einsum("hqd,hkd->hqk", query_block, key_rows, preferred_element_type=f32)
    distance = (columns[None, :] - row_index[:, None]).astype(f32)
    allowed = (columns[None, :] <= row_index[:, None]) & (columns[None, :] < length)
    return jnp.where(
        allowed[None], products * score_scale + slopes[:, None, None] * distance, -jnp.inf
    )


def attend(queries, key_rows, value_rows, length, slopes, score_scale):
    head_count, seq_len, head_size = queries.shape
    block_size = math.gcd(512, seq_len)

    def one_block(start_row):
        query_block = lax.dynamic_slice_in_dim(queries, start_row, block_size, 1)
        scores = head_scores(query_block, key_rows, start_row, slopes, length, score_scale)
        largest = jnp.max(scores, axis=-1, keepdims=True)
        log_total = largest + jnp.log(jnp.sum(jnp.exp(scores - largest), axis=-1, keepdims=True))
        attention_probs = jnp.exp(scores - log_total).astype(bf16)
        mixed_rows = jnp.einsum(
            "hqk,hkd->hqd", attention_probs, value_rows, preferred_element_type=f32
        )
        return (mixed_rows.astype(bf16), log_total[..., 0])

    starts = jnp.arange(seq_len // block_size, dtype=jnp.int32) * block_size
    mixed_rows, log_totals = lax.map(one_block, starts)
    return (
        jnp.moveaxis(mixed_rows, 0, 1).reshape(head_count, seq_len, head_size),
        jnp.moveaxis(log_totals, 0, 1).reshape(head_count, seq_len),
    )


def attend_back(queries, key_rows, value_rows, grad_mixed, log_totals, length, slopes, score_scale):
    head_count, seq_len, head_size = queries.shape
    block_size = math.gcd(512, seq_len)

    def one_block(carried, start_row):
        key_sum, value_sum = carried
        query_block = lax.dynamic_slice_in_dim(queries, start_row, block_size, 1)
        grad_block = lax.dynamic_slice_in_dim(grad_mixed, start_row, block_size, 1)
        total_block = lax.dynamic_slice_in_dim(log_totals, start_row, block_size, 1)
        scores = head_scores(query_block, key_rows, start_row, slopes, length, score_scale)
        attention_probs = jnp.exp(scores - total_block[..., None])
        grad_probs = jnp.einsum(
            "hqd,hkd->hqk", grad_block, value_rows, preferred_element_type=f32
        )
        row_inner = jnp.sum(attention_probs * grad_probs, axis=-1, keepdims=True)
        grad_scores = (attention_probs * (grad_probs - row_inner)).astype(bf16)
        query_grad = (
            jnp.einsum("hqk,hkd->hqd", grad_scores, key_rows, preferred_element_type=f32)
            * score_scale
        ).astype(bf16)
        key_sum = (
            key_sum
            + jnp.einsum("hqk,hqd->hkd", grad_scores, query_block, preferred_element_type=f32)
            * score_scale
        )
        value_sum = value_sum + jnp.einsum(
            "hqk,hqd->hkd",
            attention_probs.astype(bf16),
            grad_block,
            preferred_element_type=f32,
        )
        return ((key_sum, value_sum), query_grad)

    starts = jnp.arange(seq_len // block_size, dtype=jnp.int32) * block_size
    empty = jnp.zeros(queries.shape, f32)
    (key_sum, value_sum), query_grads = lax.scan(one_block, (empty, empty), starts)
    query_grad = jnp.moveaxis(query_grads, 0, 1).reshape(head_count, seq_len, head_size)
    return (query_grad, key_sum.astype(bf16), value_sum.astype(bf16))


ACROSS = ((1,), (1,))
PLAIN = ((1,), (0,))
DOWN = ((0,), (0,))

def mm(left_side, right_side, dims):
    return lax.dot_general(left_side, right_side, (dims, ((), ())), preferred_element_type=f32)


def set_bias(length, head, su):
    rows = su.shape[1]
    u = lax.broadcasted_iota(jnp.int32, (rows, 128), 0)
    for h in range(2):
        power = jnp.full((rows, 128), head + (h + 1), jnp.int32).astype(f32)
        slope = jnp.exp2(power * (-8.0 / H))
        su[h] = jnp.where(u < length, u.astype(f32) * slope, -jnp.inf)


def half(value, h):
    lane = lax.broadcasted_iota(jnp.int32, value.shape, 1)
    return jnp.where((lane // 64) == h, value, jnp.zeros_like(value))


def scores(k_ref, q, h, su, nk, block):
    st = mm(k_ref[:nk], half(q, h) * jnp.asarray(0.125, bf16), ACROSS)
    st = st + jnp.concatenate([su[h, :nk]] * (block // 128), axis=1)
    keep = lax.broadcasted_iota(jnp.int32, (block, block), 0) <= lax.broadcasted_iota(
        jnp.int32, (block, block), 1
    )
    tail = jnp.where(keep, st[nk - block :], -jnp.inf)
    return tail if nk == block else jnp.concatenate([st[: nk - block], tail], axis=0)


def exchange(value, axis, bit):
    return lax.ppermute(value, axis, [(i, i ^ bit) for i in range(lax.axis_size(axis))])


def is_set(axis, bit):
    return (lax.axis_index(axis) // bit) % 2


def place(bit):
    return (0 if bit[0] == "fsdp" else 1, -bit[1])


def powers(size):
    return [1 << i for i in range(size.bit_length() - 1)]


def gather_bits(unit, order):
    held, buffer = [], unit
    for bit in order:
        received = exchange(buffer, *bit)
        second = is_set(*bit) == 1
        at = sum(1 for other in held if place(other) < place(bit))
        buffer = jnp.stack(
            [jnp.where(second, received, buffer), jnp.where(second, buffer, received)], axis=at
        )
        held.append(bit)
    return buffer


def scatter_bits(partial_sum, held, order):
    held, buffer = list(held), partial_sum
    for bit in order:
        at, mine = held.index(bit), is_set(*bit)
        sent = lax.dynamic_index_in_dim(buffer, 1 - mine, at, keepdims=False).astype(bf16)
        kept = lax.dynamic_index_in_dim(buffer, mine, at, keepdims=False).astype(f32)
        buffer = kept + exchange(sent, *bit).astype(f32)
        held.remove(bit)
    return buffer


def in_order(pieces, own):
    pieces = list(pieces)
    for bit in powers(len(pieces)):
        second = (own // bit) % 2 == 1
        pieces = [
            jnp.where(second, pieces[i ^ bit], pieces[i]) for i in range(len(pieces))
        ]
    return pieces


class Team:
    def __init__(self, micro_count):
        self.shards = lax.axis_size("seq")
        self.size = self.shards // micro_count
        self.micro_count = micro_count
        self.member = lax.axis_index("seq") % self.size
        self.which = lax.axis_index("seq") // self.size
        self.team_bits = [("seq", bit) for bit in powers(self.size)]
        self.pair_bits = [("seq", self.size * bit) for bit in powers(micro_count)]

    def to_sequences(self, pieces):
        arrived = []
        for offset in range(self.micro_count):
            sent = lax.dynamic_index_in_dim(pieces, self.which ^ offset, 0, keepdims=False)
            arrived.append(sent if offset == 0 else exchange(sent, "seq", offset * self.size))
        return jnp.stack(in_order(arrived, self.which))

    def share(self, own):
        arrived = [own if e == 0 else exchange(own, "seq", e) for e in range(self.size)]
        return jnp.stack(in_order(arrived, self.member), axis=1)

    def swap(self, pieces, axis, onto):
        arrived = []
        for e in range(self.size):
            sent = lax.dynamic_index_in_dim(pieces, self.member ^ e, axis, keepdims=False)
            arrived.append(sent if e == 0 else exchange(sent, "seq", e))
        return jnp.stack(in_order(arrived, self.member), axis=onto)

    def reduce(self, partial_sum):
        total = lax.dynamic_index_in_dim(partial_sum, self.member, 1, keepdims=False)
        for e in range(1, self.size):
            sent = lax.dynamic_index_in_dim(partial_sum, self.member ^ e, 1, keepdims=False)
            total = total + exchange(sent.astype(bf16), "seq", e).astype(f32)
        return total


def general_program(
    tokens,
    cotangent,
    lengths,
    first_gain,
    first_shift,
    qkv_weight,
    qv_bias,
    out_weight,
    out_bias,
    second_gain,
    second_shift,
    up_weight,
    up_bias,
    down_weight,
    down_bias,
):
    micro_count, block_rows, width = tokens.shape
    team = Team(micro_count)
    size, member, which = team.size, team.member, team.which
    shards = team.shards
    fsdp_shards = lax.axis_size("fsdp")
    seq_len = block_rows * shards
    head_size = width // H
    own_heads = H // size
    own_width = own_heads * head_size
    hidden = up_weight.shape[1]
    own_hidden = hidden // size
    fsdp_bits = [("fsdp", bit) for bit in powers(fsdp_shards)]
    line_bits = fsdp_bits[1:] + fsdp_bits[:1]
    pair_bits, team_bits = team.pair_bits, team.team_bits
    rows_first = lambda bits: sorted(bits, key=place)
    split = lambda bits: (2,) * len(bits)

    packed = jnp.concatenate(
        [
            first_gain,
            first_shift,
            second_gain,
            second_shift,
            out_bias,
            down_bias,
            qv_bias[0],
            qv_bias[1],
            up_bias,
        ]
    )
    packed = gather_bits(packed, line_bits).reshape(fsdp_shards, -1).astype(f32)
    part = width // fsdp_shards
    vectors = [packed[:, i * part : (i + 1) * part].reshape(width) for i in range(8)]
    gain_one, shift_one, gain_two, shift_two, bias_out, bias_down, bias_q, bias_v = vectors
    bias_up = packed[:, 8 * part :].reshape(hidden // (size * (hidden // (fsdp_shards * shards))), size, -1)
    bias_up = lax.dynamic_index_in_dim(bias_up, member, 1, keepdims=False).reshape(own_hidden)

    def part_rows(weight, bits, parts_of):
        rows = weight.shape[0] // parts_of
        index = jnp.int32(0)
        for bit in rows_first(bits):
            index = index * 2 + is_set(*bit)
        return lax.dynamic_slice_in_dim(weight, index * rows, rows, 0)

    qkv_own = lax.dynamic_slice_in_dim(qkv_weight, member * 3 * own_width, 3 * own_width, 1)
    qkv_own = jnp.swapaxes(qkv_own.reshape(-1, own_heads, 3, head_size), 1, 2).reshape(-1, 3 * own_width)
    whole_qkv = gather_bits(
        part_rows(qkv_own, pair_bits, micro_count), line_bits + pair_bits
    ).reshape(width, 3 * own_width)
    whole_out = gather_bits(
        part_rows(out_weight, pair_bits + team_bits, shards), line_bits + pair_bits + team_bits
    ).reshape(width, width)
    unit = hidden // (fsdp_shards * shards)
    up_own = lax.dynamic_index_in_dim(
        up_weight.reshape(width // fsdp_shards, hidden // (size * unit), size, unit),
        member,
        2,
        keepdims=False,
    ).reshape(width // fsdp_shards, own_hidden)
    whole_up = gather_bits(up_own, line_bits).reshape(width, own_hidden)
    down_own = lax.dynamic_index_in_dim(
        down_weight.reshape(micro_count, size, unit, width), member, 1, keepdims=False
    ).reshape(micro_count * unit, width)
    whole_down = gather_bits(
        part_rows(down_own, pair_bits, micro_count), line_bits + pair_bits
    ).reshape(own_hidden, width)

    length = lax.dynamic_index_in_dim(lengths, which, 0, keepdims=False)
    own_tokens = team.to_sequences(tokens)
    all_tokens = team.share(own_tokens).reshape(seq_len, width).astype(f32)
    own_rows = micro_count * block_rows
    own_tokens = own_tokens.reshape(own_rows, width).astype(f32)
    own_positions = (
        (jnp.arange(micro_count)[:, None] * size + member) * block_rows
        + jnp.arange(block_rows)[None, :]
    ).reshape(own_rows)
    valid_mask = (own_positions < length).astype(f32)[:, None]
    slopes = jnp.exp2(-((member * own_heads + jnp.arange(own_heads)).astype(f32) + 1.0) * 8.0 / H)
    score_scale = head_size ** (-0.5)

    by_member = (micro_count, size, block_rows)

    normed = layer_norm(all_tokens, gain_one, shift_one).astype(bf16)
    own_bias = lambda vector: lax.dynamic_slice_in_dim(vector, member * own_width, own_width, 0)
    bias_columns = jnp.concatenate([own_bias(bias_q), jnp.zeros((own_width,), f32), own_bias(bias_v)])
    projected = (product(normed, whole_qkv) + bias_columns).astype(bf16)
    split_heads = lambda value: jnp.moveaxis(value.reshape(seq_len, -1, head_size), 1, 0)
    join_heads = lambda value: jnp.moveaxis(value, 0, 1).reshape(seq_len, -1)
    queries, key_rows, value_rows = [
        split_heads(projected[:, i * own_width : (i + 1) * own_width]) for i in range(3)
    ]
    mixed, log_totals = attend(queries, key_rows, value_rows, length, slopes, score_scale)
    mixed = join_heads(mixed)
    mixed_rows = team.swap(mixed.reshape(by_member + (own_width,)), 1, 2).reshape(own_rows, width)
    middle = own_tokens + (product(mixed_rows, whole_out) + bias_out)
    normed_two_own = layer_norm(middle, gain_two, shift_two).astype(bf16)
    normed_two = team.share(normed_two_own.reshape(micro_count, block_rows, width)).reshape(
        seq_len, width
    )
    hidden_pre = product(normed_two, whole_up) + bias_up
    activation = jax.nn.gelu(hidden_pre, approximate=True).astype(bf16)
    fed = team.reduce(product(activation, whole_down).reshape(by_member + (width,)))
    block_own = (valid_mask * (middle + fed.reshape(own_rows, width) + bias_down)).astype(bf16)
    block_out = team.to_sequences(block_own.reshape(micro_count, block_rows, width))

    own_grad = team.to_sequences(cotangent)
    own_grad = jnp.where(
        (valid_mask > 0).reshape(micro_count, block_rows, 1), own_grad, jnp.zeros_like(own_grad)
    )
    grad_low = team.share(own_grad).reshape(seq_len, width)
    grad_out = own_grad.reshape(own_rows, width).astype(f32)
    down_bias_grad = jnp.sum(grad_out, axis=0)
    down_grad = contract_rows(activation, grad_low)
    grad_act = against(grad_low, whole_down)
    gelu_pull = jax.vjp(partial(jax.nn.gelu, approximate=True), hidden_pre)[1]
    grad_pre = gelu_pull(grad_act)[0].astype(bf16)
    up_grad = contract_rows(normed_two, grad_pre)
    up_bias_grad = jnp.sum(grad_pre.astype(f32), axis=0)
    grad_normed_two = team.reduce(
        against(grad_pre, whole_up).reshape(by_member + (width,))
    ).reshape(own_rows, width)
    norm_pull = jax.vjp(layer_norm, middle, gain_two, shift_two)[1]
    middle_part, second_gain_grad, second_shift_grad = norm_pull(grad_normed_two)
    grad_middle = grad_out + middle_part
    grad_branch = grad_middle.astype(bf16)
    out_bias_grad = jnp.sum(grad_branch.astype(f32), axis=0)
    out_grad = contract_rows(mixed_rows, grad_branch)
    grad_mixed_own = against(grad_branch, whole_out).astype(bf16)
    grad_mixed = team.swap(
        grad_mixed_own.reshape(micro_count, block_rows, size, own_width), 2, 1
    ).reshape(seq_len, own_width)
    backs = attend_back(
        queries,
        key_rows,
        value_rows,
        split_heads(grad_mixed),
        log_totals,
        length,
        slopes,
        score_scale,
    )
    grad_qkv = jnp.concatenate([join_heads(back) for back in backs], axis=1)
    qkv_grad = contract_rows(normed, grad_qkv)
    column_sums = jnp.sum(grad_qkv.astype(f32), axis=0).reshape(3, own_width)
    grad_normed = team.reduce(
        against(grad_qkv, whole_qkv).reshape(by_member + (width,))
    ).reshape(own_rows, width)
    first_pull = jax.vjp(layer_norm, own_tokens, gain_one, shift_one)[1]
    token_part, first_gain_grad, first_shift_grad = first_pull(grad_normed)
    row_grad = (grad_middle + token_part).astype(bf16)
    tokens_grad = team.to_sequences(row_grad.reshape(micro_count, block_rows, width))

    row_bits = rows_first(fsdp_bits + pair_bits)
    pair_first = pair_bits + fsdp_bits[:1] + fsdp_bits[:0:-1]
    pair_second = fsdp_bits[:1] + pair_bits + fsdp_bits[:0:-1]
    down_sum = scatter_bits(
        down_grad.reshape(split(row_bits) + (unit, width)), row_bits, pair_first
    )

    def by_columns(grad, order):
        total = scatter_bits(
            grad.reshape(split(row_bits) + (size, -1) + grad.shape[1:]), row_bits, order
        )
        return team.swap(total, 0, 1)

    up_sum = by_columns(up_grad, pair_second)
    up_sum = jnp.swapaxes(up_sum.reshape(-1, size, hidden // (size * unit), unit), 1, 2)
    up_sum = up_sum.reshape(-1, hidden)
    qkv_sum = by_columns(qkv_grad, pair_first).reshape(-1, size, 3, own_heads, head_size)
    qkv_sum = jnp.swapaxes(qkv_sum, 2, 3).reshape(-1, 3 * width)
    all_bits = rows_first(fsdp_bits + pair_bits + team_bits)
    out_sum = scatter_bits(
        out_grad.reshape(split(all_bits) + (-1, width)), all_bits, team_bits[::-1] + pair_first
    )

    devices = fsdp_shards * shards

    def spread(own, count):
        at_member = jnp.arange(size).reshape(1, size, 1) == member
        return jnp.where(at_member, own.reshape(count, 1, -1), 0.0)

    up_vector = spread(up_bias_grad, hidden // (size * unit)).reshape(devices, unit)
    by_team = lambda own: spread(own.reshape(1, own_width), 1).reshape(width)
    vectors = [
        first_gain_grad,
        first_shift_grad,
        second_gain_grad,
        second_shift_grad,
        out_bias_grad,
        down_bias_grad,
        by_team(column_sums[0]),
        by_team(column_sums[2]),
    ]
    buffer = jnp.concatenate([v.reshape(devices, -1) for v in vectors] + [up_vector], axis=1)
    buffer = buffer.reshape(split(all_bits) + (-1,))
    held = list(all_bits)
    for bit in team_bits + pair_first:
        at, mine = held.index(bit), is_set(*bit)
        sent = lax.dynamic_index_in_dim(buffer, 1 - mine, at, keepdims=False)
        kept = lax.dynamic_index_in_dim(buffer, mine, at, keepdims=False)
        buffer = kept + exchange(sent, *bit)
        held.remove(bit)
    each = width // devices
    sums = [buffer[i * each : (i + 1) * each] for i in range(8)]
    return (
        block_out,
        tokens_grad,
        sums[0],
        sums[1],
        qkv_sum,
        jnp.stack([sums[6], sums[7]]),
        out_sum,
        sums[4],
        sums[2],
        sums[3],
        up_sum,
        buffer[8 * each :],
        down_sum,
        sums[5],
    )


BRIEF = pl.CostEstimate(flops=1, bytes_accessed=1, transcendentals=0)


def whole_block(array):
    return pl.BlockSpec(array.shape, lambda *_: (0,) * array.ndim, pipeline_mode=pl.Buffered(1))


def lanes(ref, block):
    return ref[:, pl.ds(pl.multiple_of(block * 128, 128), 128)]


def member_of(order):
    return order[1] & 1


def pair_of(order):
    return order[1] >> 1


def owner(order, i):
    return order[0] ^ ((i & 3) * 2 + (i >> 2))


def mixed_block(order, i):
    return owner(order, i) ^ (member_of(order) * 4 + pair_of(order) * 2)


def picked(ref, order, first, block_of=owner):
    return jnp.concatenate([lanes(ref, block_of(order, first + i)) for i in range(4)], axis=1)


def flat(ref, start):
    value = ref[start : start + 4, :128]
    return value.reshape(512, value.shape[-1])


class Weight:
    def __init__(self, *parts):
        self.parts = parts

    def slabs(self):
        found = []
        for pair in self.parts:
            for array, _, columns, which in pair:
                if not any(array is a and (columns, which) == b for a, b in found):
                    found.append((array, (columns, which)))
        return found

    def inputs(self):
        result = []
        for array, (columns, which) in self.slabs():
            spec = pl.BlockSpec(
                array.shape[:2] + (columns,),
                lambda *_, which=which: (0, 0, which),
                pipeline_mode=pl.Buffered(1),
            )
            result.append((array, spec))
        return result

    def views(self, refs):
        slabs = self.slabs()

        def find(view):
            array, first, columns, which = view
            at = [array is a and (columns, which) == b for a, b in slabs].index(True)
            return refs[at], first

        return [(find(pair[0]), find(pair[1])) for pair in self.parts]


def grid_call(name, kernel, order, grid, inputs, outputs, scratch=(), limit=48):
    return pl.pallas_call(
        kernel,
        name=name,
        grid_spec=pltpu.PrefetchScalarGridSpec(
            num_scalar_prefetch=1,
            grid=grid,
            in_specs=[spec for _, spec in inputs],
            out_specs=[spec for _, spec in outputs],
            scratch_shapes=list(scratch),
        ),
        out_shape=[shape for shape, _ in outputs],
        compiler_params=pltpu.CompilerParams(vmem_limit_bytes=limit << 20),
        cost_estimate=BRIEF,
    )(order, *[a for a, _ in inputs])


def shape_of(shape, dtype):
    return jax.ShapeDtypeStruct(shape, dtype)


def normalized(values):
    row_mean = jnp.mean(values, axis=-1, keepdims=True)
    centered = values - row_mean
    rstd = lax.rsqrt(jnp.mean(centered * centered, axis=-1, keepdims=True) + epsilon)
    return centered * rstd, rstd


def first_norm(order, tokens, came, other_mine, other_came, vectors):
    _, block, width = tokens.shape

    def kernel(order, mine_ref, came_ref, other_mine_ref, other_came_ref, vec_ref, out_ref):
        def write(ref):
            xhat, _ = normalized(ref[...].astype(f32))
            out_ref[...] = (xhat * vec_ref[0:1] + vec_ref[1:2]).astype(bf16)

        at = pl.program_id(0)
        for i, ref in enumerate((mine_ref.at[0], came_ref, other_mine_ref, other_came_ref)):
            pl.when(at == i)(partial(write, ref))

    def place(i, o):
        return (((i % 2) ^ pair_of(o)) * 2 + ((i // 2) ^ member_of(o)), 0)

    return grid_call(
        "first_norm",
        kernel,
        order,
        (4,),
        [(tokens, pl.BlockSpec((1, block, width), lambda i, o: (pair_of(o), 0, 0)))]
        + [(a, whole_block(a)) for a in (came, other_mine, other_came, vectors)],
        [(shape_of((4 * block, width), bf16), pl.BlockSpec((block, width), place))],
    )[0]


def project(order, normed, bias, part, weight, block=256):
    rows, width = normed.shape
    columns = bias.shape[1]
    step = columns // len(weight.parts)

    def kernel(order, lhs_ref, bias_ref, *rest):
        out_ref = rest[-1]
        left = [picked(lhs_ref, order, 0), picked(lhs_ref, order, 4)]
        for at, views in enumerate(weight.views(rest[:-1])):
            total = sum(mm(l, flat(*view), PLAIN) for l, view in zip(left, views))
            here = slice(at * step, (at + 1) * step)
            out_ref[:, here] = (total + bias_ref[part : part + 1, here]).astype(bf16)

    return grid_call(
        "project",
        kernel,
        order,
        (rows // block,),
        [(normed, pl.BlockSpec((block, width), lambda i, o: (i, 0))), (bias, whole_block(bias))]
        + weight.inputs(),
        [(shape_of((rows, columns), bf16), pl.BlockSpec((block, columns), lambda i, o: (i, 0)))],
    )[0]


def out_and_norm(order, mixed, tokens, vectors, weight, block=256):
    rows, width = mixed.shape

    def kernel(order, lhs_ref, tok_ref, vec_ref, *rest):
        middle_ref, norm_ref = rest[-2:]
        left = [picked(lhs_ref, order, i, mixed_block) for i in (0, 4)]
        for at, views in enumerate(weight.views(rest[:-2])):
            total = sum(mm(l, flat(*view), PLAIN) for l, view in zip(left, views))
            start = pl.multiple_of((member_of(order) ^ at) * (width // 2), 128)
            middle_ref[:, pl.ds(start, width // 2)] = total
        middle = tok_ref[...].astype(f32) + (middle_ref[...] + vec_ref[4:5])
        middle_ref[...] = middle
        xhat, _ = normalized(middle)
        norm_ref[...] = (xhat * vec_ref[2:3] + vec_ref[3:4]).astype(bf16)

    row = pl.BlockSpec((block, width), lambda i, o: (i, 0))
    return grid_call(
        "out_and_norm",
        kernel,
        order,
        (rows // block,),
        [(mixed, row), (tokens, row)]
        + [(vectors, whole_block(vectors))]
        + weight.inputs(),
        [(shape_of((rows, width), f32), row), (shape_of((rows, width), bf16), row)],
    )


def both(block, width):
    return (
        pl.BlockSpec((block, width), lambda i, o: (jnp.minimum(i, 1), 0)),
        pl.BlockSpec((block, width), lambda i, o: (jnp.maximum(i - 2, 0), 0)),
    )


def either(own_ref, other_ref, run):
    at = pl.program_id(0)
    pl.when(at < 2)(lambda: run(own_ref, True))
    pl.when(at >= 2)(lambda: run(other_ref, False))


ROOT = math.sqrt(2.0 / math.pi)


def gelu_and_slope(z):
    inner = jnp.tanh(ROOT * (z + 0.044715 * (z * z * z)))
    half_up = 0.5 * (1.0 + inner)
    slope = half_up + 0.5 * z * (1.0 - inner * inner) * (ROOT * (1.0 + 3 * 0.044715 * (z * z)))
    return z * half_up, slope


def feed_up(order, own, other, bias, part, weight):
    rows, width = own.shape
    block = rows // 2
    columns = bias.shape[1]

    def kernel(order, own_ref, other_ref, bias_ref, *rest):
        act_ref, slope_ref = rest[-2:]

        def run(lhs_ref, _):
            left = [picked(lhs_ref, order, 0), picked(lhs_ref, order, 4)]
            (views,) = weight.views(rest[:-2])
            total = sum(mm(l, flat(*view), PLAIN) for l, view in zip(left, views))
            act, slope = gelu_and_slope(total + bias_ref[part : part + 1])
            act_ref[...] = act.astype(bf16)
            slope_ref[...] = slope.astype(bf16)

        either(own_ref, other_ref, run)

    row = pl.BlockSpec((block, columns), lambda i, o: (i, 0))
    return grid_call(
        "feed_up",
        kernel,
        order,
        (4,),
        list(zip((own, other), both(block, width)))
        + [(bias, whole_block(bias))]
        + weight.inputs(),
        [(shape_of((2 * rows, columns), bf16), row)] * 2,
    )


def own_and_sent(rows, width):
    block = rows // 2
    return list(
        zip(
            (shape_of((rows, width), f32), shape_of((rows, width), bf16)),
            both(block, width),
        )
    )


def feed_down(order, acts, weight):
    rows, columns = acts[0].shape
    width = 1024
    block = rows // 4
    count = len(acts)

    def kernel(order, *rest):
        own_ref, sent_ref = rest[-2:]
        total = 0.0
        for part, views in zip(rest[:count], weight.views(rest[count:-2])):
            for half, view in enumerate(views):
                total = total + mm(picked(part, order, 4 * half), flat(*view), PLAIN)

        def save(ref, _):
            ref[...] = total.astype(ref.dtype)

        either(own_ref, sent_ref, save)

    return grid_call(
        "feed_down",
        kernel,
        order,
        (4,),
        [(act, pl.BlockSpec((block, columns), lambda i, o: (i, 0))) for act in acts]
        + weight.inputs(),
        own_and_sent(rows // 2, width),
    )


def feed_down_back(order, own, other, slope, weight):
    rows, width = own.shape
    columns = slope.shape[1]
    block = rows // 2
    step = columns // len(weight.parts)

    def kernel(order, own_ref, other_ref, slope_ref, *rest):
        out_ref, sum_ref = rest[-2:]

        @pl.when(pl.program_id(0) == 0)
        def _():
            sum_ref[...] = jnp.zeros_like(sum_ref)

        def run(lhs_ref, _):
            left = lhs_ref[...]
            for at, views in enumerate(weight.views(rest[:-2])):
                for half, view in enumerate(views):
                    total = mm(left, flat(*view), ACROSS)
                    for k in range(4):
                        start = at * step + owner(order, 4 * half + k) * 128
                        here = pl.ds(pl.multiple_of(start, 128), 128)
                        value = total[:, 128 * k : 128 * (k + 1)] * slope_ref[:, here].astype(f32)
                        low = value.astype(bf16)
                        out_ref[:, here] = low
                        sum_ref[:, here] += jnp.sum(
                            low.astype(f32).reshape(block // 8, 8, 128), axis=0
                        )

        either(own_ref, other_ref, run)

    row = pl.BlockSpec((block, columns), lambda i, o: (i, 0))
    return grid_call(
        "feed_down_back",
        kernel,
        order,
        (4,),
        list(zip((own, other), both(block, width)))
        + [(slope, row)]
        + weight.inputs(),
        [
            (shape_of((2 * rows, columns), bf16), row),
            (shape_of((8, columns), f32), pl.BlockSpec((8, columns), lambda i, o: (0, 0))),
        ],
    )


def feed_up_back(order, grads, weight):
    rows, columns = grads[0].shape
    width = 1024
    block = rows // 4
    count = len(grads)

    def kernel(order, *rest):
        own_ref, sent_ref = rest[-2:]

        def save(ref, _):
            views = weight.views(rest[count:-2])
            for half in range(2):
                total = 0.0
                for grad_ref, pair in zip(rest[:count], views):
                    total = total + mm(grad_ref[...], flat(*pair[half]), ACROSS)
                for k in range(4):
                    here = pl.ds(pl.multiple_of(owner(order, 4 * half + k) * 128, 128), 128)
                    ref[:, here] = total[:, 128 * k : 128 * (k + 1)].astype(ref.dtype)

        either(own_ref, sent_ref, save)

    return grid_call(
        "feed_up_back",
        kernel,
        order,
        (4,),
        [(grad, pl.BlockSpec((block, columns), lambda i, o: (i, 0))) for grad in grads]
        + weight.inputs(),
        own_and_sent(rows // 2, width),
    )


def rows_of_eight(value):
    return jnp.sum(value.reshape(value.shape[0] // 8, 8, value.shape[1]), axis=0)


def norm_back(xhat, rstd, grad_norm, gain):
    scaled = grad_norm * gain
    return rstd * (
        scaled
        - jnp.mean(scaled, axis=-1, keepdims=True)
        - xhat * jnp.mean(scaled * xhat, axis=-1, keepdims=True)
    )


def middle_back(order, own, came, middle, grad_out, vectors, weight, block=256):
    rows, width = middle.shape
    half_width = width // 2

    def kernel(order, own_ref, came_ref, middle_ref, dy_ref, vec_ref, *rest):
        grad_ref, low_ref, keep_ref, sent_ref, sum_ref, tmp = rest[-6:]

        @pl.when(pl.program_id(0) == 0)
        def _():
            sum_ref[...] = jnp.zeros_like(sum_ref)

        grad_norm = own_ref[...] + came_ref[...].astype(f32)
        xhat, rstd = normalized(middle_ref[...])
        grad_out = dy_ref[...].astype(f32)
        grad_middle = grad_out + norm_back(xhat, rstd, grad_norm, vec_ref[2:3])
        grad_ref[...] = grad_middle
        low = grad_middle.astype(bf16)
        low_ref[...] = low
        sum_ref[0] += rows_of_eight(grad_norm * xhat)
        sum_ref[1] += rows_of_eight(grad_norm)
        sum_ref[2] += rows_of_eight(low.astype(f32))
        sum_ref[3] += rows_of_eight(grad_out)
        views = weight.views(rest[:-6])
        member = member_of(order)
        for half in range(2):
            total = 0.0
            for at, pair in enumerate(views):
                start = pl.multiple_of((member ^ at) * half_width, 128)
                total = total + mm(low_ref[:, pl.ds(start, half_width)], flat(*pair[half]), ACROSS)
            for k in range(4):
                here = pl.ds(pl.multiple_of(mixed_block(order, 4 * half + k) * 128, 128), 128)
                tmp[:, here] = total[:, 128 * k : 128 * (k + 1)].astype(bf16)
        keep_ref[...] = tmp[:, :half_width]
        sent_ref[...] = tmp[:, half_width:]

    row = pl.BlockSpec((block, width), lambda i, o: (i, 0))
    part = pl.BlockSpec((block, half_width), lambda i, o: (i, 0))
    return grid_call(
        "middle_back",
        kernel,
        order,
        (rows // block,),
        [(own, row), (came, row), (middle, row), (grad_out, row), (vectors, whole_block(vectors))]
        + weight.inputs(),
        [
            (shape_of((rows, width), f32), row),
            (shape_of((rows, width), bf16), row),
            (shape_of((rows, half_width), bf16), part),
            (shape_of((rows, half_width), bf16), part),
            (shape_of((4, 8, width), f32), pl.BlockSpec((4, 8, width), lambda i, o: (0, 0, 0))),
        ],
        scratch=[pltpu.VMEM((block, width), bf16)],
    )


def project_back(order, grads, weight):
    rows = grads[0][0].shape[0]
    block = rows // 4
    width = 1024
    given = [g for half in grads for g in half]

    def kernel(order, *rest):
        parts = rest[:6]
        own_ref, sent_ref = rest[-2:]

        def save(ref, _):
            views = weight.views(rest[6:-2])
            lefts = [
                jnp.concatenate([r[...] for r in parts[3 * i : 3 * i + 3]], axis=1) for i in range(2)
            ]
            for half in range(2):
                total = 0.0
                for left, pair in zip(lefts, views):
                    total = total + mm(left, flat(*pair[half]), ACROSS)
                for k in range(4):
                    here = pl.ds(pl.multiple_of(owner(order, 4 * half + k) * 128, 128), 128)
                    ref[:, here] = total[:, 128 * k : 128 * (k + 1)].astype(ref.dtype)

        either(own_ref, sent_ref, save)

    row = pl.BlockSpec(
        (block, given[0].shape[1]), lambda i, o: (((i % 2) ^ pair_of(o)) * 2 + ((i // 2) ^ member_of(o)), 0)
    )
    return grid_call(
        "project_back",
        kernel,
        order,
        (4,),
        [(g, row) for g in given] + weight.inputs(),
        own_and_sent(rows // 2, width),
    )


def first_back(order, own, came, tokens, grad_middle, vectors, block=256):
    rows, width = own.shape

    def kernel(order, own_ref, came_ref, tok_ref, mid_ref, vec_ref, out_ref, sum_ref):
        @pl.when(pl.program_id(0) == 0)
        def _():
            sum_ref[...] = jnp.zeros_like(sum_ref)

        grad_norm = own_ref[...] + came_ref[...].astype(f32)
        xhat, rstd = normalized(tok_ref[...].astype(f32))
        total = mid_ref[...] + norm_back(xhat, rstd, grad_norm, vec_ref[0:1])
        out_ref[...] = total.astype(bf16)
        sum_ref[0] += rows_of_eight(grad_norm * xhat)
        sum_ref[1] += rows_of_eight(grad_norm)

    row = pl.BlockSpec((block, width), lambda i, o: (i, 0))
    return grid_call(
        "first_back",
        kernel,
        order,
        (rows // block,),
        [(own, row), (came, row), (tokens, row), (grad_middle, row), (vectors, whole_block(vectors))],
        [
            (shape_of((rows, width), bf16), row),
            (shape_of((2, 8, width), f32), pl.BlockSpec((2, 8, width), lambda i, o: (0, 0, 0))),
        ],
    )


def weight_grad(order, first, count, lefts, rights, block_of=owner):
    pieces = [r for right in rights for r in right]
    wide = sum(r.shape[1] for r in rights[0])
    together = 2

    def kernel(order, *rest):
        left_refs, right_refs, out_ref = rest[: len(lefts)], rest[len(lefts) : -1], rest[-1]
        at = first + together * pl.program_id(0)
        left = [
            jnp.concatenate([lanes(ref, block_of(order, at + k)) for k in range(together)], axis=1)
            for ref in left_refs
        ]
        each = len(rights[0])
        start = 0
        for j in range(each):
            total = 0.0
            for i in range(len(lefts)):
                total = total + mm(left[i], right_refs[i * each + j][...], DOWN)
            width = total.shape[1]
            out_ref[:, :, start : start + width] = total.reshape(together, 128, width).astype(bf16)
            start += width

    return grid_call(
        "weight_grad",
        kernel,
        order,
        (count // together,),
        [(a, whole_block(a)) for a in lefts] + [(a, whole_block(a)) for a in pieces],
        [
            (
                shape_of((count, 128, wide), bf16),
                pl.BlockSpec((together, 128, wide), lambda i, o: (i, 0, 0)),
            )
        ],
    )[0]


def head_of(order, part):
    return member_of(order) * 8 + (pair_of(order) ^ part) * 4 + 2 * pl.program_id(0)


def team_attend_kernel(part, order, q_ref, k_ref, v_ref, o_ref, total_ref, vt, su):
    at = pl.program_id(1)
    block = q_ref.shape[0]

    @pl.when(at == 0)
    def _():
        vt[...] = v_ref[...].T
        set_bias(order[2], head_of(order, part), su)

    def branch(b):
        nk = (b + 1) * block
        q = q_ref[...]
        outs, totals = [], []
        for h in range(2):
            st = scores(k_ref, q, h, su, nk, block)
            m = jnp.max(st, axis=0, keepdims=True)
            p = jnp.exp(st - m)
            l = jnp.sum(p, axis=0, keepdims=True)
            ot = mm(vt[64 * h : 64 * h + 64, :nk], p.astype(bf16), PLAIN)
            outs.append(ot / l)
            totals.append(m + jnp.log(l))
        o_ref[...] = jnp.concatenate(outs, axis=0).T.astype(bf16)
        total_ref[0] = jnp.concatenate(totals + [jnp.zeros((6, block), f32)], axis=0)

    for b in range(k_ref.shape[0] // block):
        pl.when(at == b)(partial(branch, b))


def kept_place(i, o):
    return ((i % 2) ^ member_of(o)) * 2 + ((i // 2) ^ pair_of(o))


def team_attend(order, qkv, part, block):
    rows = qkv.shape[0]
    whole = lambda kind: pl.BlockSpec((rows, 128), lambda p, i, o: (0, 2 * kind + p))
    return pl.pallas_call(
        partial(team_attend_kernel, part),
        name="team_attend",
        grid_spec=pltpu.PrefetchScalarGridSpec(
            num_scalar_prefetch=1,
            grid=(2, rows // block),
            in_specs=[pl.BlockSpec((block, 128), lambda p, i, o: (i, p)), whole(1), whole(2)],
            out_specs=[
                pl.BlockSpec((block, 128), lambda p, i, o: (kept_place(i, o), p)),
                pl.BlockSpec((1, 8, block), lambda p, i, o: (p, 0, i)),
            ],
            scratch_shapes=[pltpu.VMEM((128, rows), bf16), pltpu.VMEM((2, rows, 128), f32)],
        ),
        out_shape=[shape_of((rows, 256), bf16), shape_of((2, 8, rows), f32)],
        compiler_params=pltpu.CompilerParams(vmem_limit_bytes=40 << 20),
        cost_estimate=BRIEF,
    )(order, qkv, qkv, qkv)


def team_back_kernel(
    part, order, q_ref, k_ref, v_ref, g_ref, total_ref, dq_ref, dk_ref, dv_ref, sum_ref,
    kt, su, dk, dv
):
    at = pl.program_id(1)
    block = q_ref.shape[0]
    blocks = k_ref.shape[0] // block

    @pl.when(at == 0)
    def _():
        kt[...] = k_ref[...].T
        set_bias(order[2], head_of(order, part), su)
        dk[...] = jnp.zeros_like(dk)
        dv[...] = jnp.zeros_like(dv)
        sum_ref[...] = jnp.zeros_like(sum_ref)

    def branch(b):
        nk = (b + 1) * block
        q, g = q_ref[...], g_ref[...]
        outs, dks, dvs = [], [], []
        for h in range(2):
            st = scores(k_ref, q, h, su, nk, block)
            p = jnp.exp(st - total_ref[0, h : h + 1])
            gm = half(g, h)
            dp = mm(v_ref[:nk], gm, ACROSS)
            inner = jnp.sum(p * dp, axis=0, keepdims=True)
            ds = (p * (dp - inner)).astype(bf16)
            outs.append(mm(kt[64 * h : 64 * h + 64, :nk], ds, PLAIN))
            dks.append(mm(ds, half(q, h), PLAIN))
            dvs.append(mm(p.astype(bf16), gm, PLAIN))
        low = (jnp.concatenate(outs, axis=0).T * 0.125).astype(bf16)
        dq_ref[...] = low
        sum_ref[0, 0] += rows_of_eight(low.astype(f32))
        dk[:nk] += dks[0] + dks[1]
        dv[:nk] += dvs[0] + dvs[1]

    for b in range(blocks):
        pl.when(at == b)(partial(branch, b))

    @pl.when(at == blocks - 1)
    def _():
        dk_ref[...] = (dk[...] * 0.125).astype(bf16)
        low = dv[...].astype(bf16)
        dv_ref[...] = low
        sum_ref[0, 1] = rows_of_eight(low.astype(f32))


def team_back(order, qkv, grad, totals, part, block):
    rows = qkv.shape[0]
    whole = lambda kind: pl.BlockSpec((rows, 128), lambda p, i, o: (0, 2 * kind + p))
    by_rows = pl.BlockSpec((block, 128), lambda p, i, o: (i, p))
    by_head = pl.BlockSpec((rows, 128), lambda p, i, o: (0, p))
    return pl.pallas_call(
        partial(team_back_kernel, part),
        name="team_back",
        grid_spec=pltpu.PrefetchScalarGridSpec(
            num_scalar_prefetch=1,
            grid=(2, rows // block),
            in_specs=[
                by_rows,
                whole(1),
                whole(2),
                pl.BlockSpec((block, 128), lambda p, i, o: (kept_place(i, o), 2 * part + p)),
                pl.BlockSpec((1, 8, block), lambda p, i, o: (p, 0, i)),
            ],
            out_specs=[
                by_rows,
                by_head,
                by_head,
                pl.BlockSpec((1, 2, 8, 128), lambda p, i, o: (p, 0, 0, 0)),
            ],
            scratch_shapes=[
                pltpu.VMEM((128, rows), bf16),
                pltpu.VMEM((2, rows, 128), f32),
                pltpu.VMEM((rows, 128), f32),
                pltpu.VMEM((rows, 128), f32),
            ],
        ),
        out_shape=[shape_of((rows, 256), bf16)] * 3 + [shape_of((2, 2, 8, 128), f32)],
        compiler_params=pltpu.CompilerParams(vmem_limit_bytes=48 << 20),
        cost_estimate=BRIEF,
    )(order, qkv, qkv, qkv, grad, totals)


def joined(arrays, rows=None):
    rows = rows or arrays[0].shape[0]
    width = arrays[0].shape[1]
    count = len(arrays)

    def kernel(*refs):
        for i in range(count):
            refs[-1][i] = refs[i][:rows]

    return pl.pallas_call(
        kernel,
        name="joined",
        out_shape=shape_of((count, rows, width), arrays[0].dtype),
        compiler_params=pltpu.CompilerParams(vmem_limit_bytes=32 << 20),
        cost_estimate=BRIEF,
    )(*arrays)


def units(order, qkv_weight, out_weight, up_weight, down_weight, packed):
    def kernel(order, qkv_ref, out_ref, up_ref, down_ref, packed_ref, q_unit, o_unit, u_first, u_second, d_unit):
        c, x = member_of(order), pair_of(order)
        heads = qkv_ref[:, pl.ds(pl.multiple_of((c * 2 + x) * 768, 128), 768)]
        q_unit[:128] = jnp.concatenate(
            [
                heads[:, n * 192 + kind * 64 : n * 192 + kind * 64 + 64]
                for kind in range(3)
                for n in range(4)
            ],
            axis=1,
        )
        q_unit[128:] = jnp.concatenate([packed_ref[...], jnp.zeros((16, 640), bf16)], axis=1)
        o_unit[...] = out_ref[:, pl.ds(pl.multiple_of(c * 512, 128), 512)]
        for i in range(8):
            u_first[:, 128 * i : 128 * i + 128] = lanes(up_ref, i * 4 + x * 2 + c)
            u_second[:, 128 * i : 128 * i + 128] = lanes(up_ref, i * 4 + (1 - x) * 2 + c)
        d_unit[...] = down_ref[...]

    shapes = [(144, 768), (128, 512), (128, 1024), (128, 1024), (128, 1024)]
    return grid_call(
        "units",
        kernel,
        order,
        (1,),
        [(a, whole_block(a)) for a in (qkv_weight, out_weight, up_weight)]
        + [(down_weight, pl.BlockSpec((128, 1024), lambda i, o: (o[1], 0)))]
        + [(packed, whole_block(packed))],
        [(shape_of(s, bf16), pl.BlockSpec(s, lambda i, o: (0, 0))) for s in shapes],
    )


def unpacked(order, mine, came):
    def kernel(order, mine_ref, came_ref, vec_ref, qkv_ref, up_ref, tmp):
        c, x = member_of(order), pair_of(order)
        for i in range(8):
            values = (mine_ref if i < 4 else came_ref)[i % 4].astype(f32)
            start = owner(order, i) * 128
            vec_ref[:, pl.ds(pl.multiple_of(start, 128), 128)] = values
            tmp[i] = values
            for part in range(2):
                row = tmp[i, pl.ds(8 + (x ^ part) * 2 + c, 1)]
                up_ref[part : part + 1, pl.ds(pl.multiple_of(start, 128), 128)] = row
        for part in range(2):
            here = pl.ds(pl.multiple_of(c * 512 + (x ^ part) * 256, 128), 256)
            qkv_ref[part : part + 1] = jnp.concatenate(
                [vec_ref[6:7, here], jnp.zeros((1, 256), f32), vec_ref[7:8, here]], axis=1
            )

    spec = pl.BlockSpec((4, 16, 128), lambda i, o: (0, 8, 0))
    shapes = [(16, 1024), (2, 768), (2, 1024)]
    return grid_call(
        "unpacked",
        kernel,
        order,
        (1,),
        [(mine, spec), (came, spec)],
        [(shape_of(s, f32), pl.BlockSpec(s, lambda i, o: (0, 0))) for s in shapes],
        scratch=[pltpu.VMEM((8, 16, 128), f32)],
    )


def one_of(pair, index):
    return lax.dynamic_index_in_dim(pair, index, 0, keepdims=False)


def flipped(pair, index):
    return jnp.where(index == 0, pair, pair[::-1])


def after(value, *earlier):
    return lax.optimization_barrier((value,) + earlier)[0]


def team_program(
    tokens,
    cotangent,
    lengths,
    first_gain,
    first_shift,
    qkv_weight,
    qv_bias,
    out_weight,
    out_bias,
    second_gain,
    second_shift,
    up_weight,
    up_bias,
    down_weight,
    down_bias,
):
    _, block, width = tokens.shape
    own_rows = 2 * block
    f, s = lax.axis_index("fsdp"), lax.axis_index("seq")
    x, c = s // 2, s % 2
    over_core = lambda v: exchange(v, "seq", 1)
    over_x = lambda v: exchange(v, "seq", 2)
    over_y = lambda v: exchange(v, "fsdp", 1)
    over_z = lambda v, k: exchange(v, "fsdp", 2 * k)
    along_z = lambda v: joined([v] + [over_z(v, k) for k in (1, 2, 3)])

    length = one_of(lengths, x)
    order = jnp.stack([f, s, length]).astype(jnp.int32)

    packed = jnp.concatenate(
        [
            first_gain, first_shift, second_gain, second_shift, out_bias, down_bias,
            qv_bias[0], qv_bias[1], up_bias, jnp.zeros((512,), bf16),
        ]
    ).reshape(16, 128)
    order = [jnp.stack([f, s, length]).astype(jnp.int32)]

    def wait_for(*values):
        order[0] = after(order[0], *values)

    def run(kernel, *operands, **options):
        result = kernel(order[0], *operands, **options)
        wait_for(result[0] if isinstance(result, (list, tuple)) else result)
        return result

    def along_z(unit):
        pieces = [unit] + [over_z(unit, k) for k in (1, 2, 3)]
        result = joined([after(pieces[0], order[0])] + pieces[1:])
        wait_for(result)
        return result

    full = lambda a, b: ((a, 0, a.shape[2], 0), (b, 0, b.shape[2], 0))

    unit_qkv, unit_out, unit_up, unit_up_other, unit_down = run(
        units, qkv_weight, out_weight, up_weight, down_weight, packed
    )
    tokens_came = over_x(one_of(tokens, 1 - x))
    other_mine = over_core(one_of(tokens, x))
    other_came = over_core(tokens_came)
    own_tokens = jnp.concatenate([one_of(tokens, x), tokens_came])
    z_qkv = along_z(unit_qkv)
    y_qkv, xz_qkv = over_y(z_qkv), over_x(z_qkv)
    xy_qkv = over_x(y_qkv)
    qkv_own, qkv_other = full(z_qkv, y_qkv), full(xz_qkv, xy_qkv)
    z_out = along_z(after(unit_out, z_qkv))
    y_out = over_y(z_out)
    out = Weight(full(z_out, y_out), full(over_core(z_out), over_core(y_out)))
    vectors, bias_qkv, bias_up = run(unpacked, z_qkv, y_qkv)

    blocks_at = (jnp.arange(2) ^ x) * 2 + c
    valid = ((blocks_at[:, None] * block + jnp.arange(block)) < length).reshape(own_rows, 1)
    normed = run(first_norm, tokens, tokens_came, other_mine, other_came, vectors)
    projected = [None, None]
    mixed, totals = [None, None], [None, None]
    projected[0] = run(project, normed, bias_qkv, 0, Weight(qkv_own))
    z_up = along_z(after(unit_up, z_out))
    y_up = over_y(z_up)
    mixed[0], totals[0] = run(team_attend, projected[0], 0, block)
    projected[1] = run(project, normed, bias_qkv, 1, Weight(qkv_other))
    mixed[1], totals[1] = run(team_attend, projected[1], 1, block)
    z_down = along_z(after(unit_down, z_up))
    y_down, xz_down = over_y(z_down), over_x(z_down)
    down = [full(z_down, y_down), full(xz_down, over_x(y_down))]
    sent = jnp.concatenate([m[own_rows:] for m in mixed], axis=1)
    mixed_rows = jnp.concatenate([m[:own_rows] for m in mixed] + [over_core(sent)], axis=1)
    middle, norm_own = run(out_and_norm, mixed_rows, own_tokens, vectors, out)
    norm_other = over_core(norm_own)
    grad_came = over_x(one_of(after(cotangent, xy_qkv), 1 - x))
    grad_own = jnp.concatenate([one_of(cotangent, x), grad_came])
    grad_own = jnp.where(valid, grad_own, jnp.zeros_like(grad_own))
    grad_other = over_core(grad_own)
    grad_all = jnp.concatenate([grad_own, grad_other])
    norm_all = jnp.concatenate([norm_own, norm_other])

    act, slope, grad_pre, pre_sums = ([None, None] for _ in range(4))
    up_sent, up_kept, up_came = ([None, None] for _ in range(3))

    def hidden_grad(part):
        up_sent[part] = run(weight_grad, 4, 4, [norm_all], [[grad_pre[part]]])
        up_came[part] = over_y(up_sent[part])

    act[0], slope[0] = run(feed_up, norm_own, norm_other, bias_up, 0, Weight(full(z_up, y_up)))
    down_kept = run(weight_grad, 0, 8, [act[0]], [[grad_all]])
    z_up_other = along_z(after(unit_up_other, z_down))
    y_up_other = over_y(z_up_other)
    up = [full(z_up, y_up), full(z_up_other, y_up_other)]
    grad_pre[0], pre_sums[0] = run(feed_down_back, grad_own, grad_other, slope[0], Weight(down[0]))
    hidden_grad(0)
    up_kept[0] = run(weight_grad, 0, 4, [norm_all], [[grad_pre[0]]])
    act[1], slope[1] = run(feed_up, norm_own, norm_other, bias_up, 1, Weight(up[1]))
    down_sent = [None, None]
    for i in (1, 0):
        down_sent[i] = run(weight_grad, 4 * i, 4, [act[1]], [[grad_all]])
    down_came = [over_x(sent) for sent in down_sent]
    grad_pre[1], pre_sums[1] = run(feed_down_back, grad_own, grad_other, slope[1], Weight(down[1]))
    hidden_grad(1)
    back_own, back_sent = run(feed_up_back, grad_pre, Weight(*up))
    back_came = over_core(back_sent)
    up_kept[1] = run(weight_grad, 0, 4, [norm_all], [[grad_pre[1]]])
    grad_middle, branch, mixed_kept, mixed_sent, middle_sums = run(
        middle_back, back_own, back_came, middle, grad_own, vectors, out
    )
    grad_mixed = jnp.concatenate([mixed_kept, over_core(mixed_sent)])

    def out_grad(i):
        columns = lax.dynamic_slice(branch, (0, i * 512), (own_rows, 512))
        return run(weight_grad, 0, 8, [mixed_rows], [[columns]], block_of=mixed_block)

    out_sent = out_grad(1 - c)
    out_came = over_core(out_sent)
    out_kept = out_grad(c)

    def added(kept, came):
        return kept.astype(f32) + came.astype(f32)

    def low_sum(kept, came):
        return added(kept, came).astype(bf16)

    def z_pieces(total):
        return [total[k].astype(bf16) for k in (1, 2, 3)]

    def sum_z(total, pieces):
        result = total[0]
        for k, piece in enumerate(pieces):
            result = result + over_z(piece, k + 1).astype(f32)
        return result

    up_x = low_sum(up_kept[1], up_came[1])
    up_x_came = over_x(up_x)
    down_y = low_sum(down_kept[4:], down_came[1])
    down_y_came = over_y(down_y)
    out_total = jnp.swapaxes(added(out_kept, out_came).reshape(2, 4, 128, 512), 0, 1)
    out_pieces = z_pieces(out_total)
    wait_for(up_x, down_y, *out_pieces)
    *heads_other, sums_other = run(team_back, projected[1], grad_mixed, totals[1], 1, block)
    other_sent = run(weight_grad, 4, 4, [normed], [heads_other])
    other_y_came = over_y(other_sent)
    other_kept = run(weight_grad, 0, 4, [normed], [heads_other])
    out_y = sum_z(out_total, out_pieces)
    out_y_sent = out_y[1].astype(bf16)
    wait_for(out_y_sent)
    *heads_own, sums_own = run(team_back, projected[0], grad_mixed, totals[0], 0, block)
    own_sent = run(weight_grad, 4, 4, [normed], [heads_own])
    own_y_came = over_y(own_sent)
    down_total = added(low_sum(down_kept[:4], down_came[0]), down_y_came)
    down_pieces = z_pieces(down_total)
    wait_for(*down_pieces)
    first_own, first_sent = run(
        project_back, [heads_own, heads_other], Weight(qkv_own, qkv_other)
    )
    first_came = over_core(first_sent)
    other_x = low_sum(other_kept, other_y_came)
    up_total = added(low_sum(up_kept[0], up_came[0]), up_x_came)
    up_pieces = z_pieces(up_total)
    wait_for(other_x, *up_pieces)
    own_kept = run(weight_grad, 0, 4, [normed], [heads_own])
    row_grad, first_sums = run(first_back, first_own, first_came, own_tokens, grad_middle, vectors)
    fed_own, fed_sent = run(feed_down, act, Weight(*down))
    block_own = jnp.where(
        valid, middle + (fed_own + over_core(fed_sent).astype(f32)) + vectors[5:6], 0.0
    ).astype(bf16)

    def to_devices(rows):
        return flipped(jnp.stack([rows[:block], over_x(rows[block:])]), x)

    tokens_grad = to_devices(row_grad)
    block_out = to_devices(block_own)

    def over_pair(total):
        pieces = total.reshape(2, 64, -1)
        rows = flipped(jnp.stack([one_of(pieces, x), over_x(one_of(pieces, 1 - x))]), x)
        return jnp.swapaxes(rows, 0, 1)

    def over_team(total):
        pieces = total.reshape((2, 32) + total.shape[1:])
        rows = flipped(jnp.stack([one_of(pieces, c), over_core(one_of(pieces, 1 - c))]), c)
        return jnp.swapaxes(rows, 0, 1)

    down_sum = sum_z(down_total, down_pieces)
    up_sum = over_team(over_pair(sum_z(up_total, up_pieces)))
    up_sum = up_sum.reshape(32, 2, 2, 8, 128).transpose(0, 3, 2, 1, 4).reshape(32, 4096)
    out_x = added(out_y[0], over_y(out_y_sent)).reshape(2, 64, 512)
    out_sum = added(one_of(out_x, x), over_x(one_of(out_x, 1 - x).astype(bf16)))
    out_sum = over_team(out_sum).reshape(32, width)
    qkv_total = added(own_kept, own_y_came) + over_x(other_x).astype(f32)
    qkv_sum = over_team(over_pair(sum_z(qkv_total, z_pieces(qkv_total))))
    qkv_sum = qkv_sum.reshape(32, 2, 2, 3, 4, 64)
    qkv_sum = jnp.transpose(qkv_sum, (0, 1, 2, 4, 3, 5)).reshape(32, 3 * width)

    places = f ^ jnp.array([0, 2, 4, 6, 1, 3, 5, 7], jnp.int32)

    def sum_vectors(buffer):
        buffer = buffer.reshape(8, 2, 2, -1)
        at_core = jnp.moveaxis(buffer, 2, 0)
        buffer = one_of(at_core, c) + over_core(one_of(at_core, 1 - c))
        at_x = jnp.moveaxis(buffer, 1, 0)
        buffer = one_of(at_x, x) + over_x(one_of(at_x, 1 - x))
        buffer = jnp.take(buffer, places, axis=0)
        buffer = buffer[:4] + over_y(buffer[4:])
        total = buffer[0]
        for k in (1, 2, 3):
            total = total + over_z(buffer[k], k)
        return total

    at_member = jnp.arange(2) == c
    up_vector = flipped(jnp.sum(jnp.stack(pre_sums), axis=1).reshape(2, 8, 128), x)
    up_vector = jnp.where(
        at_member[None, None, :, None], jnp.swapaxes(up_vector, 0, 1)[:, :, None], 0.0
    ).reshape(32, 128)
    middle_sums = jnp.sum(middle_sums, axis=1)
    early = sum_vectors(
        jnp.concatenate([middle_sums[i].reshape(32, 32) for i in range(4)] + [up_vector], axis=1)
    )
    head_sums = flipped(jnp.sum(jnp.stack([sums_own, sums_other]), axis=3), x)

    def head_vector(kind):
        return jnp.where(at_member[:, None], head_sums[:, :, kind].reshape(1, 512), 0.0).reshape(32, 32)

    first_sums = jnp.sum(first_sums, axis=1)
    late = sum_vectors(
        jnp.concatenate(
            [first_sums[i].reshape(32, 32) for i in range(2)] + [head_vector(0), head_vector(1)],
            axis=1,
        )
    )
    return (
        block_out,
        tokens_grad,
        late[:32],
        late[32:64],
        qkv_sum,
        jnp.stack([late[64:96], late[96:]]),
        out_sum,
        early[64:96],
        early[:32],
        early[32:64],
        up_sum,
        early[128:],
        down_sum,
        early[96:128],
    )


def local(tokens, *others):
    width = tokens.shape[2]
    shards = (lax.axis_size("fsdp"), lax.axis_size("seq"))
    hidden = others[10].shape[1]
    if tokens.shape[0] == 2 and tokens.shape[1] % 256 == 0 and shards == (8, 4) and tokens.shape[1] * 4 <= 1024 and (width, hidden) == (1024, 4096):
        return team_program(tokens, *others)
    return general_program(tokens, *others)


def solution(mesh):
    return jax.shard_map(
        local,
        mesh=mesh,
        in_specs=(
            P("fsdp", "seq", None),
            P("fsdp", "seq", None),
            P("fsdp"),
            P("fsdp"),
            P("fsdp"),
            P("fsdp", None),
            P(None, "fsdp"),
            P("fsdp", None),
            P("fsdp"),
            P("fsdp"),
            P("fsdp"),
            P("fsdp", None),
            P("fsdp"),
            P("fsdp", None),
            P("fsdp"),
        ),
        out_specs=(
            P("fsdp", "seq", None),
            P("fsdp", "seq", None),
            P(("fsdp", "seq")),
            P(("fsdp", "seq")),
            P(("fsdp", "seq"), None),
            P(None, ("fsdp", "seq")),
            P(("fsdp", "seq"), None),
            P(("fsdp", "seq")),
            P(("fsdp", "seq")),
            P(("fsdp", "seq")),
            P(("fsdp", "seq"), None),
            P(("fsdp", "seq")),
            P(("fsdp", "seq"), None),
            P(("fsdp", "seq")),
        ),
        check_vma=False,
    )
```

```python
from functools import partial
import math

import jax
import jax.numpy as jnp
from jax import lax
from jax.experimental import pallas as pl
from jax.experimental.pallas import tpu as pltpu
from jax.sharding import PartitionSpec as P

H = 16


epsilon = 1e-05
f32 = jnp.float32
bf16 = jnp.bfloat16


def layer_norm(values, norm_gain, norm_shift):
    row_mean = jnp.mean(values, axis=-1, keepdims=True)
    centered = values - row_mean
    variance = jnp.mean(centered * centered, axis=-1, keepdims=True)
    return centered * lax.rsqrt(variance + epsilon) * norm_gain + norm_shift


def product(left_side, right_side):
    return jnp.dot(left_side, right_side, preferred_element_type=f32)


def contract_rows(left_side, right_side):
    return lax.dot_general(
        left_side, right_side, (((0,), (0,)), ((), ())), preferred_element_type=f32
    )


def against(left_side, right_side):
    return lax.dot_general(
        left_side, right_side, (((1,), (1,)), ((), ())), preferred_element_type=f32
    )


def head_scores(query_block, key_rows, start_row, slopes, length, score_scale):
    block_size = query_block.shape[1]
    seq_len = key_rows.shape[1]
    row_index = start_row + jnp.arange(block_size)
    columns = jnp.arange(seq_len)
    products = jnp.einsum("hqd,hkd->hqk", query_block, key_rows, preferred_element_type=f32)
    distance = (columns[None, :] - row_index[:, None]).astype(f32)
    allowed = (columns[None, :] <= row_index[:, None]) & (columns[None, :] < length)
    return jnp.where(
        allowed[None], products * score_scale + slopes[:, None, None] * distance, -jnp.inf
    )


def attend(queries, key_rows, value_rows, length, slopes, score_scale):
    head_count, seq_len, head_size = queries.shape
    block_size = math.gcd(512, seq_len)

    def one_block(start_row):
        query_block = lax.dynamic_slice_in_dim(queries, start_row, block_size, 1)
        scores = head_scores(query_block, key_rows, start_row, slopes, length, score_scale)
        largest = jnp.max(scores, axis=-1, keepdims=True)
        log_total = largest + jnp.log(jnp.sum(jnp.exp(scores - largest), axis=-1, keepdims=True))
        attention_probs = jnp.exp(scores - log_total).astype(bf16)
        mixed_rows = jnp.einsum(
            "hqk,hkd->hqd", attention_probs, value_rows, preferred_element_type=f32
        )
        return (mixed_rows.astype(bf16), log_total[..., 0])

    starts = jnp.arange(seq_len // block_size, dtype=jnp.int32) * block_size
    mixed_rows, log_totals = lax.map(one_block, starts)
    return (
        jnp.moveaxis(mixed_rows, 0, 1).reshape(head_count, seq_len, head_size),
        jnp.moveaxis(log_totals, 0, 1).reshape(head_count, seq_len),
    )


def attend_back(queries, key_rows, value_rows, grad_mixed, log_totals, length, slopes, score_scale):
    head_count, seq_len, head_size = queries.shape
    block_size = math.gcd(512, seq_len)

    def one_block(carried, start_row):
        key_sum, value_sum = carried
        query_block = lax.dynamic_slice_in_dim(queries, start_row, block_size, 1)
        grad_block = lax.dynamic_slice_in_dim(grad_mixed, start_row, block_size, 1)
        total_block = lax.dynamic_slice_in_dim(log_totals, start_row, block_size, 1)
        scores = head_scores(query_block, key_rows, start_row, slopes, length, score_scale)
        attention_probs = jnp.exp(scores - total_block[..., None])
        grad_probs = jnp.einsum(
            "hqd,hkd->hqk", grad_block, value_rows, preferred_element_type=f32
        )
        row_inner = jnp.sum(attention_probs * grad_probs, axis=-1, keepdims=True)
        grad_scores = (attention_probs * (grad_probs - row_inner)).astype(bf16)
        query_grad = (
            jnp.einsum("hqk,hkd->hqd", grad_scores, key_rows, preferred_element_type=f32)
            * score_scale
        ).astype(bf16)
        key_sum = (
            key_sum
            + jnp.einsum("hqk,hqd->hkd", grad_scores, query_block, preferred_element_type=f32)
            * score_scale
        )
        value_sum = value_sum + jnp.einsum(
            "hqk,hqd->hkd",
            attention_probs.astype(bf16),
            grad_block,
            preferred_element_type=f32,
        )
        return ((key_sum, value_sum), query_grad)

    starts = jnp.arange(seq_len // block_size, dtype=jnp.int32) * block_size
    empty = jnp.zeros(queries.shape, f32)
    (key_sum, value_sum), query_grads = lax.scan(one_block, (empty, empty), starts)
    query_grad = jnp.moveaxis(query_grads, 0, 1).reshape(head_count, seq_len, head_size)
    return (query_grad, key_sum.astype(bf16), value_sum.astype(bf16))


ACROSS = ((1,), (1,))
PLAIN = ((1,), (0,))
DOWN = ((0,), (0,))

def mm(left_side, right_side, dims):
    return lax.dot_general(left_side, right_side, (dims, ((), ())), preferred_element_type=f32)


def set_bias(length, head, su):
    rows = su.shape[1]
    u = lax.broadcasted_iota(jnp.int32, (rows, 128), 0)
    for h in range(2):
        power = jnp.full((rows, 128), head + (h + 1), jnp.int32).astype(f32)
        slope = jnp.exp2(power * (-8.0 / H))
        su[h] = jnp.where(u < length, u.astype(f32) * slope, -jnp.inf)


def half(value, h):
    lane = lax.broadcasted_iota(jnp.int32, value.shape, 1)
    return jnp.where((lane // 64) == h, value, jnp.zeros_like(value))


def scores(k_ref, q, h, su, nk, block):
    st = mm(k_ref[:nk], half(q, h) * jnp.asarray(0.125, bf16), ACROSS)
    st = st + jnp.concatenate([su[h, :nk]] * (block // 128), axis=1)
    keep = lax.broadcasted_iota(jnp.int32, (block, block), 0) <= lax.broadcasted_iota(
        jnp.int32, (block, block), 1
    )
    tail = jnp.where(keep, st[nk - block :], -jnp.inf)
    return tail if nk == block else jnp.concatenate([st[: nk - block], tail], axis=0)


def exchange(value, axis, bit):
    return lax.ppermute(value, axis, [(i, i ^ bit) for i in range(lax.axis_size(axis))])


def is_set(axis, bit):
    return (lax.axis_index(axis) // bit) % 2


def place(bit):
    return (0 if bit[0] == "fsdp" else 1, -bit[1])


def powers(size):
    return [1 << i for i in range(size.bit_length() - 1)]


def gather_bits(unit, order):
    held, buffer = [], unit
    for bit in order:
        received = exchange(buffer, *bit)
        second = is_set(*bit) == 1
        at = sum(1 for other in held if place(other) < place(bit))
        buffer = jnp.stack(
            [jnp.where(second, received, buffer), jnp.where(second, buffer, received)], axis=at
        )
        held.append(bit)
    return buffer


def scatter_bits(partial_sum, held, order):
    held, buffer = list(held), partial_sum
    for bit in order:
        at, mine = held.index(bit), is_set(*bit)
        sent = lax.dynamic_index_in_dim(buffer, 1 - mine, at, keepdims=False).astype(bf16)
        kept = lax.dynamic_index_in_dim(buffer, mine, at, keepdims=False).astype(f32)
        buffer = kept + exchange(sent, *bit).astype(f32)
        held.remove(bit)
    return buffer


def in_order(pieces, own):
    pieces = list(pieces)
    for bit in powers(len(pieces)):
        second = (own // bit) % 2 == 1
        pieces = [
            jnp.where(second, pieces[i ^ bit], pieces[i]) for i in range(len(pieces))
        ]
    return pieces


class Team:
    def __init__(self, micro_count):
        self.shards = lax.axis_size("seq")
        self.size = self.shards // micro_count
        self.micro_count = micro_count
        self.member = lax.axis_index("seq") % self.size
        self.which = lax.axis_index("seq") // self.size
        self.team_bits = [("seq", bit) for bit in powers(self.size)]
        self.pair_bits = [("seq", self.size * bit) for bit in powers(micro_count)]

    def to_sequences(self, pieces):
        arrived = []
        for offset in range(self.micro_count):
            sent = lax.dynamic_index_in_dim(pieces, self.which ^ offset, 0, keepdims=False)
            arrived.append(sent if offset == 0 else exchange(sent, "seq", offset * self.size))
        return jnp.stack(in_order(arrived, self.which))

    def share(self, own):
        arrived = [own if e == 0 else exchange(own, "seq", e) for e in range(self.size)]
        return jnp.stack(in_order(arrived, self.member), axis=1)

    def swap(self, pieces, axis, onto):
        arrived = []
        for e in range(self.size):
            sent = lax.dynamic_index_in_dim(pieces, self.member ^ e, axis, keepdims=False)
            arrived.append(sent if e == 0 else exchange(sent, "seq", e))
        return jnp.stack(in_order(arrived, self.member), axis=onto)

    def reduce(self, partial_sum):
        total = lax.dynamic_index_in_dim(partial_sum, self.member, 1, keepdims=False)
        for e in range(1, self.size):
            sent = lax.dynamic_index_in_dim(partial_sum, self.member ^ e, 1, keepdims=False)
            total = total + exchange(sent.astype(bf16), "seq", e).astype(f32)
        return total


def general_program(
    tokens,
    cotangent,
    lengths,
    first_gain,
    first_shift,
    qkv_weight,
    qv_bias,
    out_weight,
    out_bias,
    second_gain,
    second_shift,
    up_weight,
    up_bias,
    down_weight,
    down_bias,
):
    micro_count, block_rows, width = tokens.shape
    team = Team(micro_count)
    size, member, which = team.size, team.member, team.which
    shards = team.shards
    fsdp_shards = lax.axis_size("fsdp")
    seq_len = block_rows * shards
    head_size = width // H
    own_heads = H // size
    own_width = own_heads * head_size
    hidden = up_weight.shape[1]
    own_hidden = hidden // size
    fsdp_bits = [("fsdp", bit) for bit in powers(fsdp_shards)]
    line_bits = fsdp_bits[1:] + fsdp_bits[:1]
    pair_bits, team_bits = team.pair_bits, team.team_bits
    rows_first = lambda bits: sorted(bits, key=place)
    split = lambda bits: (2,) * len(bits)

    packed = jnp.concatenate(
        [
            first_gain,
            first_shift,
            second_gain,
            second_shift,
            out_bias,
            down_bias,
            qv_bias[0],
            qv_bias[1],
            up_bias,
        ]
    )
    packed = gather_bits(packed, line_bits).reshape(fsdp_shards, -1).astype(f32)
    part = width // fsdp_shards
    vectors = [packed[:, i * part : (i + 1) * part].reshape(width) for i in range(8)]
    gain_one, shift_one, gain_two, shift_two, bias_out, bias_down, bias_q, bias_v = vectors
    bias_up = packed[:, 8 * part :].reshape(hidden // (size * (hidden // (fsdp_shards * shards))), size, -1)
    bias_up = lax.dynamic_index_in_dim(bias_up, member, 1, keepdims=False).reshape(own_hidden)

    def part_rows(weight, bits, parts_of):
        rows = weight.shape[0] // parts_of
        index = jnp.int32(0)
        for bit in rows_first(bits):
            index = index * 2 + is_set(*bit)
        return lax.dynamic_slice_in_dim(weight, index * rows, rows, 0)

    qkv_own = lax.dynamic_slice_in_dim(qkv_weight, member * 3 * own_width, 3 * own_width, 1)
    qkv_own = jnp.swapaxes(qkv_own.reshape(-1, own_heads, 3, head_size), 1, 2).reshape(-1, 3 * own_width)
    whole_qkv = gather_bits(
        part_rows(qkv_own, pair_bits, micro_count), line_bits + pair_bits
    ).reshape(width, 3 * own_width)
    whole_out = gather_bits(
        part_rows(out_weight, pair_bits + team_bits, shards), line_bits + pair_bits + team_bits
    ).reshape(width, width)
    unit = hidden // (fsdp_shards * shards)
    up_own = lax.dynamic_index_in_dim(
        up_weight.reshape(width // fsdp_shards, hidden // (size * unit), size, unit),
        member,
        2,
        keepdims=False,
    ).reshape(width // fsdp_shards, own_hidden)
    whole_up = gather_bits(up_own, line_bits).reshape(width, own_hidden)
    down_own = lax.dynamic_index_in_dim(
        down_weight.reshape(micro_count, size, unit, width), member, 1, keepdims=False
    ).reshape(micro_count * unit, width)
    whole_down = gather_bits(
        part_rows(down_own, pair_bits, micro_count), line_bits + pair_bits
    ).reshape(own_hidden, width)

    length = lax.dynamic_index_in_dim(lengths, which, 0, keepdims=False)
    own_tokens = team.to_sequences(tokens)
    all_tokens = team.share(own_tokens).reshape(seq_len, width).astype(f32)
    own_rows = micro_count * block_rows
    own_tokens = own_tokens.reshape(own_rows, width).astype(f32)
    own_positions = (
        (jnp.arange(micro_count)[:, None] * size + member) * block_rows
        + jnp.arange(block_rows)[None, :]
    ).reshape(own_rows)
    valid_mask = (own_positions < length).astype(f32)[:, None]
    slopes = jnp.exp2(-((member * own_heads + jnp.arange(own_heads)).astype(f32) + 1.0) * 8.0 / H)
    score_scale = head_size ** (-0.5)

    by_member = (micro_count, size, block_rows)

    normed = layer_norm(all_tokens, gain_one, shift_one).astype(bf16)
    own_bias = lambda vector: lax.dynamic_slice_in_dim(vector, member * own_width, own_width, 0)
    bias_columns = jnp.concatenate([own_bias(bias_q), jnp.zeros((own_width,), f32), own_bias(bias_v)])
    projected = (product(normed, whole_qkv) + bias_columns).astype(bf16)
    split_heads = lambda value: jnp.moveaxis(value.reshape(seq_len, -1, head_size), 1, 0)
    join_heads = lambda value: jnp.moveaxis(value, 0, 1).reshape(seq_len, -1)
    queries, key_rows, value_rows = [
        split_heads(projected[:, i * own_width : (i + 1) * own_width]) for i in range(3)
    ]
    mixed, log_totals = attend(queries, key_rows, value_rows, length, slopes, score_scale)
    mixed = join_heads(mixed)
    mixed_rows = team.swap(mixed.reshape(by_member + (own_width,)), 1, 2).reshape(own_rows, width)
    middle = own_tokens + (product(mixed_rows, whole_out) + bias_out)
    normed_two_own = layer_norm(middle, gain_two, shift_two).astype(bf16)
    normed_two = team.share(normed_two_own.reshape(micro_count, block_rows, width)).reshape(
        seq_len, width
    )
    hidden_pre = product(normed_two, whole_up) + bias_up
    activation = jax.nn.gelu(hidden_pre, approximate=True).astype(bf16)
    fed = team.reduce(product(activation, whole_down).reshape(by_member + (width,)))
    block_own = (valid_mask * (middle + fed.reshape(own_rows, width) + bias_down)).astype(bf16)
    block_out = team.to_sequences(block_own.reshape(micro_count, block_rows, width))

    own_grad = team.to_sequences(cotangent)
    own_grad = jnp.where(
        (valid_mask > 0).reshape(micro_count, block_rows, 1), own_grad, jnp.zeros_like(own_grad)
    )
    grad_low = team.share(own_grad).reshape(seq_len, width)
    grad_out = own_grad.reshape(own_rows, width).astype(f32)
    down_bias_grad = jnp.sum(grad_out, axis=0)
    down_grad = contract_rows(activation, grad_low)
    grad_act = against(grad_low, whole_down)
    gelu_pull = jax.vjp(partial(jax.nn.gelu, approximate=True), hidden_pre)[1]
    grad_pre = gelu_pull(grad_act)[0].astype(bf16)
    up_grad = contract_rows(normed_two, grad_pre)
    up_bias_grad = jnp.sum(grad_pre.astype(f32), axis=0)
    grad_normed_two = team.reduce(
        against(grad_pre, whole_up).reshape(by_member + (width,))
    ).reshape(own_rows, width)
    norm_pull = jax.vjp(layer_norm, middle, gain_two, shift_two)[1]
    middle_part, second_gain_grad, second_shift_grad = norm_pull(grad_normed_two)
    grad_middle = grad_out + middle_part
    grad_branch = grad_middle.astype(bf16)
    out_bias_grad = jnp.sum(grad_branch.astype(f32), axis=0)
    out_grad = contract_rows(mixed_rows, grad_branch)
    grad_mixed_own = against(grad_branch, whole_out).astype(bf16)
    grad_mixed = team.swap(
        grad_mixed_own.reshape(micro_count, block_rows, size, own_width), 2, 1
    ).reshape(seq_len, own_width)
    backs = attend_back(
        queries,
        key_rows,
        value_rows,
        split_heads(grad_mixed),
        log_totals,
        length,
        slopes,
        score_scale,
    )
    grad_qkv = jnp.concatenate([join_heads(back) for back in backs], axis=1)
    qkv_grad = contract_rows(normed, grad_qkv)
    column_sums = jnp.sum(grad_qkv.astype(f32), axis=0).reshape(3, own_width)
    grad_normed = team.reduce(
        against(grad_qkv, whole_qkv).reshape(by_member + (width,))
    ).reshape(own_rows, width)
    first_pull = jax.vjp(layer_norm, own_tokens, gain_one, shift_one)[1]
    token_part, first_gain_grad, first_shift_grad = first_pull(grad_normed)
    row_grad = (grad_middle + token_part).astype(bf16)
    tokens_grad = team.to_sequences(row_grad.reshape(micro_count, block_rows, width))

    row_bits = rows_first(fsdp_bits + pair_bits)
    pair_first = pair_bits + fsdp_bits[:1] + fsdp_bits[:0:-1]
    pair_second = fsdp_bits[:1] + pair_bits + fsdp_bits[:0:-1]
    down_sum = scatter_bits(
        down_grad.reshape(split(row_bits) + (unit, width)), row_bits, pair_first
    )

    def by_columns(grad, order):
        total = scatter_bits(
            grad.reshape(split(row_bits) + (size, -1) + grad.shape[1:]), row_bits, order
        )
        return team.swap(total, 0, 1)

    up_sum = by_columns(up_grad, pair_second)
    up_sum = jnp.swapaxes(up_sum.reshape(-1, size, hidden // (size * unit), unit), 1, 2)
    up_sum = up_sum.reshape(-1, hidden)
    qkv_sum = by_columns(qkv_grad, pair_first).reshape(-1, size, 3, own_heads, head_size)
    qkv_sum = jnp.swapaxes(qkv_sum, 2, 3).reshape(-1, 3 * width)
    all_bits = rows_first(fsdp_bits + pair_bits + team_bits)
    out_sum = scatter_bits(
        out_grad.reshape(split(all_bits) + (-1, width)), all_bits, team_bits[::-1] + pair_first
    )

    devices = fsdp_shards * shards

    def spread(own, count):
        at_member = jnp.arange(size).reshape(1, size, 1) == member
        return jnp.where(at_member, own.reshape(count, 1, -1), 0.0)

    up_vector = spread(up_bias_grad, hidden // (size * unit)).reshape(devices, unit)
    by_team = lambda own: spread(own.reshape(1, own_width), 1).reshape(width)
    vectors = [
        first_gain_grad,
        first_shift_grad,
        second_gain_grad,
        second_shift_grad,
        out_bias_grad,
        down_bias_grad,
        by_team(column_sums[0]),
        by_team(column_sums[2]),
    ]
    buffer = jnp.concatenate([v.reshape(devices, -1) for v in vectors] + [up_vector], axis=1)
    buffer = buffer.reshape(split(all_bits) + (-1,))
    held = list(all_bits)
    for bit in team_bits + pair_first:
        at, mine = held.index(bit), is_set(*bit)
        sent = lax.dynamic_index_in_dim(buffer, 1 - mine, at, keepdims=False)
        kept = lax.dynamic_index_in_dim(buffer, mine, at, keepdims=False)
        buffer = kept + exchange(sent, *bit)
        held.remove(bit)
    each = width // devices
    sums = [buffer[i * each : (i + 1) * each] for i in range(8)]
    return (
        block_out,
        tokens_grad,
        sums[0],
        sums[1],
        qkv_sum,
        jnp.stack([sums[6], sums[7]]),
        out_sum,
        sums[4],
        sums[2],
        sums[3],
        up_sum,
        buffer[8 * each :],
        down_sum,
        sums[5],
    )


WORK = pl.CostEstimate(flops=10000000000, bytes_accessed=20000000, transcendentals=0)


def whole_block(array):
    return pl.BlockSpec(array.shape, lambda *_: (0,) * array.ndim, pipeline_mode=pl.Buffered(1))


def lanes(ref, block):
    return ref[:, pl.ds(pl.multiple_of(block * 128, 128), 128)]


def member_of(order):
    return order[1] & 1


def pair_of(order):
    return order[1] >> 1


def owner(order, i):
    return order[0] ^ ((i & 3) * 2 + (i >> 2))


def mixed_block(order, i):
    return owner(order, i) ^ (member_of(order) * 4 + pair_of(order) * 2)


def natural(order, i):
    return i


def picked(ref, order, first, block_of=owner):
    return jnp.concatenate([lanes(ref, block_of(order, first + i)) for i in range(4)], axis=1)


def flat(ref, start):
    value = ref[start : start + 4, :128]
    return value.reshape(512, value.shape[-1])


class Weight:
    def __init__(self, *parts, orders=None):
        self.parts = parts
        self.orders = orders or [owner] * len(parts)

    def slabs(self):
        found = []
        for pair in self.parts:
            for array, _, columns, which in pair:
                if not any(array is a and (columns, which) == b for a, b in found):
                    found.append((array, (columns, which)))
        return found

    def inputs(self):
        result = []
        for array, (columns, which) in self.slabs():
            spec = pl.BlockSpec(
                array.shape[:2] + (columns,),
                lambda *_, which=which: (0, 0, which),
                pipeline_mode=pl.Buffered(1),
            )
            result.append((array, spec))
        return result

    def views(self, refs):
        slabs = self.slabs()

        def find(view):
            array, first, columns, which = view
            at = [array is a and (columns, which) == b for a, b in slabs].index(True)
            return refs[at], first

        return [(find(pair[0]), find(pair[1])) for pair in self.parts]


def grid_call(name, kernel, order, grid, inputs, outputs, scratch=(), limit=16):
    return pl.pallas_call(
        kernel,
        name=name,
        grid_spec=pltpu.PrefetchScalarGridSpec(
            num_scalar_prefetch=1,
            grid=grid,
            in_specs=[spec for _, spec in inputs],
            out_specs=[spec for _, spec in outputs],
            scratch_shapes=list(scratch),
        ),
        out_shape=[shape for shape, _ in outputs],
        compiler_params=pltpu.CompilerParams(vmem_limit_bytes=limit << 20),
        cost_estimate=WORK,
    )(order, *[a for a, _ in inputs])


def shape_of(shape, dtype):
    return jax.ShapeDtypeStruct(shape, dtype)


def normalized(values):
    row_mean = jnp.mean(values, axis=-1, keepdims=True)
    centered = values - row_mean
    rstd = lax.rsqrt(jnp.mean(centered * centered, axis=-1, keepdims=True) + epsilon)
    return centered * rstd, rstd


def first_norm(order, tokens, came, other_mine, other_came, vectors):
    _, block, width = tokens.shape

    def kernel(order, mine_ref, came_ref, other_mine_ref, other_came_ref, vec_ref, out_ref):
        def write(ref):
            xhat, _ = normalized(ref[...].astype(f32))
            out_ref[...] = (xhat * vec_ref[0:1] + vec_ref[1:2]).astype(bf16)

        at = pl.program_id(0)
        for i, ref in enumerate((mine_ref.at[0], came_ref, other_mine_ref, other_came_ref)):
            pl.when(at == i)(partial(write, ref))

    def place(i, o):
        return (((i % 2) ^ pair_of(o)) * 2 + ((i // 2) ^ member_of(o)), 0)

    return grid_call(
        "first_norm",
        kernel,
        order,
        (4,),
        [(tokens, pl.BlockSpec((1, block, width), lambda i, o: (pair_of(o), 0, 0)))]
        + [(a, whole_block(a)) for a in (came, other_mine, other_came, vectors)],
        [(shape_of((4 * block, width), bf16), pl.BlockSpec((block, width), place))],
    )[0]


def project(order, normed, bias, part, weight, block=256):
    rows, width = normed.shape
    columns = bias.shape[1]
    step = columns // len(weight.parts)

    def kernel(order, lhs_ref, bias_ref, *rest):
        out_ref = rest[-1]
        left = [picked(lhs_ref, order, 0), picked(lhs_ref, order, 4)]
        for at, views in enumerate(weight.views(rest[:-1])):
            total = sum(mm(l, flat(*view), PLAIN) for l, view in zip(left, views))
            here = slice(at * step, (at + 1) * step)
            out_ref[:, here] = (total + bias_ref[part : part + 1, here]).astype(bf16)

    return grid_call(
        "project",
        kernel,
        order,
        (rows // block,),
        [(normed, pl.BlockSpec((block, width), lambda i, o: (i, 0))), (bias, whole_block(bias))]
        + weight.inputs(),
        [(shape_of((rows, columns), bf16), pl.BlockSpec((block, columns), lambda i, o: (i, 0)))],
    )[0]


def out_and_norm(order, mixed, tokens, vectors, weight, block=256):
    rows, width = mixed.shape

    def kernel(order, lhs_ref, tok_ref, vec_ref, *rest):
        middle_ref, norm_ref = rest[-2:]
        left = [picked(lhs_ref, order, i, mixed_block) for i in (0, 4)]
        for at, views in enumerate(weight.views(rest[:-2])):
            total = sum(mm(l, flat(*view), PLAIN) for l, view in zip(left, views))
            start = pl.multiple_of((member_of(order) ^ at) * (width // 2), 128)
            middle_ref[:, pl.ds(start, width // 2)] = total
        middle = tok_ref[...].astype(f32) + (middle_ref[...] + vec_ref[4:5])
        middle_ref[...] = middle
        xhat, _ = normalized(middle)
        norm_ref[...] = (xhat * vec_ref[2:3] + vec_ref[3:4]).astype(bf16)

    row = pl.BlockSpec((block, width), lambda i, o: (i, 0))
    return grid_call(
        "out_and_norm",
        kernel,
        order,
        (rows // block,),
        [(mixed, row), (tokens, row)]
        + [(vectors, whole_block(vectors))]
        + weight.inputs(),
        [(shape_of((rows, width), f32), row), (shape_of((rows, width), bf16), row)],
    )


def both(block, width):
    return (
        pl.BlockSpec((block, width), lambda i, o: (jnp.minimum(i, 1), 0)),
        pl.BlockSpec((block, width), lambda i, o: (jnp.maximum(i - 2, 0), 0)),
    )


def either(own_ref, other_ref, run):
    at = pl.program_id(0)
    pl.when(at < 2)(lambda: run(own_ref, True))
    pl.when(at >= 2)(lambda: run(other_ref, False))


ROOT = math.sqrt(2.0 / math.pi)


def gelu_and_slope(z):
    inner = jnp.tanh(ROOT * (z + 0.044715 * (z * z * z)))
    half_up = 0.5 * (1.0 + inner)
    slope = half_up + 0.5 * z * (1.0 - inner * inner) * (ROOT * (1.0 + 3 * 0.044715 * (z * z)))
    return z * half_up, slope


def feed_up(order, own, other, bias, part, weight):
    rows, width = own.shape
    block = rows // 2
    columns = bias.shape[1]

    def kernel(order, own_ref, other_ref, bias_ref, *rest):
        act_ref, slope_ref = rest[-2:]

        def run(lhs_ref, _):
            left = [picked(lhs_ref, order, i, weight.orders[0]) for i in (0, 4)]
            step = columns // len(weight.parts)
            for at, views in enumerate(weight.views(rest[:-2])):
                total = sum(mm(l, flat(*view), PLAIN) for l, view in zip(left, views))
                here = slice(at * step, (at + 1) * step)
                act, slope = gelu_and_slope(total + bias_ref[part : part + 1, here])
                act_ref[:, here] = act.astype(bf16)
                slope_ref[:, here] = slope.astype(bf16)

        either(own_ref, other_ref, run)

    row = pl.BlockSpec((block, columns), lambda i, o: (i, 0))
    return grid_call(
        "feed_up",
        kernel,
        order,
        (4,),
        list(zip((own, other), both(block, width)))
        + [(bias, whole_block(bias))]
        + weight.inputs(),
        [(shape_of((2 * rows, columns), bf16), row)] * 2,
    )


def own_and_sent(rows, width):
    block = rows // 2
    return list(
        zip(
            (shape_of((rows, width), f32), shape_of((rows, width), bf16)),
            both(block, width),
        )
    )


def feed_down(order, acts, weight):
    rows, columns = acts[0].shape
    width = 1024
    block = rows // 4
    count = len(acts)

    def kernel(order, *rest):
        own_ref, sent_ref = rest[-2:]
        total = 0.0
        for part, views, block_of in zip(rest[:count], weight.views(rest[count:-2]), weight.orders):
            for half, view in enumerate(views):
                total = total + mm(picked(part, order, 4 * half, block_of), flat(*view), PLAIN)

        def save(ref, _):
            ref[...] = total.astype(ref.dtype)

        either(own_ref, sent_ref, save)

    return grid_call(
        "feed_down",
        kernel,
        order,
        (4,),
        [(act, pl.BlockSpec((block, columns), lambda i, o: (i, 0))) for act in acts]
        + weight.inputs(),
        own_and_sent(rows // 2, width),
    )


def feed_down_back(order, own, other, slope, weight):
    rows, width = own.shape
    columns = slope.shape[1]
    block = rows // 2
    step = columns // len(weight.parts)

    def kernel(order, own_ref, other_ref, slope_ref, *rest):
        out_ref, sum_ref = rest[-2:]

        @pl.when(pl.program_id(0) == 0)
        def _():
            sum_ref[...] = jnp.zeros_like(sum_ref)

        def run(lhs_ref, _):
            left = lhs_ref[...]
            for at, views in enumerate(weight.views(rest[:-2])):
                for half, view in enumerate(views):
                    total = mm(left, flat(*view), ACROSS)
                    for k in range(4):
                        start = at * step + weight.orders[at](order, 4 * half + k) * 128
                        here = pl.ds(pl.multiple_of(start, 128), 128)
                        value = total[:, 128 * k : 128 * (k + 1)] * slope_ref[:, here].astype(f32)
                        low = value.astype(bf16)
                        out_ref[:, here] = low
                        sum_ref[:, here] += jnp.sum(
                            low.astype(f32).reshape(block // 8, 8, 128), axis=0
                        )

        either(own_ref, other_ref, run)

    row = pl.BlockSpec((block, columns), lambda i, o: (i, 0))
    return grid_call(
        "feed_down_back",
        kernel,
        order,
        (4,),
        list(zip((own, other), both(block, width)))
        + [(slope, row)]
        + weight.inputs(),
        [
            (shape_of((2 * rows, columns), bf16), row),
            (shape_of((8, columns), f32), pl.BlockSpec((8, columns), lambda i, o: (0, 0))),
        ],
    )


def feed_up_back(order, grads, weight):
    rows, columns = grads[0].shape
    width = 1024
    block = rows // 4
    count = len(grads)

    def kernel(order, *rest):
        own_ref, sent_ref, tmp = rest[-3:]
        each = len(weight.parts) // count
        step = columns // each
        for at, (pair, block_of) in enumerate(zip(weight.views(rest[count:-3]), weight.orders)):
            grad = rest[at // each][:, (at % each) * step : (at % each + 1) * step]
            for half in range(2):
                total = mm(grad, flat(*pair[half]), ACROSS)
                for k in range(4):
                    here = pl.ds(pl.multiple_of(block_of(order, 4 * half + k) * 128, 128), 128)
                    value = total[:, 128 * k : 128 * (k + 1)]
                    tmp[:, here] = value if at == 0 else tmp[:, here] + value

        def save(ref, _):
            ref[...] = tmp[...].astype(ref.dtype)

        either(own_ref, sent_ref, save)

    return grid_call(
        "feed_up_back",
        kernel,
        order,
        (4,),
        [(grad, pl.BlockSpec((block, columns), lambda i, o: (i, 0))) for grad in grads]
        + weight.inputs(),
        own_and_sent(rows // 2, width),
        scratch=[pltpu.VMEM((block, width), f32)],
    )


def rows_of_eight(value):
    return jnp.sum(value.reshape(value.shape[0] // 8, 8, value.shape[1]), axis=0)


def norm_back(xhat, rstd, grad_norm, gain):
    scaled = grad_norm * gain
    return rstd * (
        scaled
        - jnp.mean(scaled, axis=-1, keepdims=True)
        - xhat * jnp.mean(scaled * xhat, axis=-1, keepdims=True)
    )


def middle_back(order, own, came, middle, grad_out, vectors, weight, block=256):
    rows, width = middle.shape
    half_width = width // 2

    def kernel(order, own_ref, came_ref, middle_ref, dy_ref, vec_ref, *rest):
        grad_ref, branch_ref, keep_ref, sent_ref, sum_ref, tmp, low_ref = rest[-7:]

        @pl.when(pl.program_id(0) == 0)
        def _():
            sum_ref[...] = jnp.zeros_like(sum_ref)

        grad_norm = own_ref[...] + came_ref[...].astype(f32)
        xhat, rstd = normalized(middle_ref[...])
        grad_out = dy_ref[...].astype(f32)
        grad_middle = grad_out + norm_back(xhat, rstd, grad_norm, vec_ref[2:3])
        grad_ref[...] = grad_middle
        low = grad_middle.astype(bf16)
        low_ref[...] = low
        sum_ref[0] += rows_of_eight(grad_norm * xhat)
        sum_ref[1] += rows_of_eight(grad_norm)
        sum_ref[2] += rows_of_eight(low.astype(f32))
        sum_ref[3] += rows_of_eight(grad_out)
        views = weight.views(rest[:-7])
        member = member_of(order)
        for i in range(4):
            from_ = i ^ (member * 2 + pair_of(order))
            branch_ref[:, 256 * i : 256 * i + 256] = low_ref[:, pl.ds(pl.multiple_of(from_ * 256, 128), 256)]
        for half in range(2):
            total = 0.0
            for at, pair in enumerate(views):
                start = pl.multiple_of((member ^ at) * half_width, 128)
                total = total + mm(low_ref[:, pl.ds(start, half_width)], flat(*pair[half]), ACROSS)
            for k in range(4):
                here = pl.ds(pl.multiple_of(mixed_block(order, 4 * half + k) * 128, 128), 128)
                tmp[:, here] = total[:, 128 * k : 128 * (k + 1)].astype(bf16)
        keep_ref[...] = tmp[:, :half_width]
        sent_ref[...] = tmp[:, half_width:]

    row = pl.BlockSpec((block, width), lambda i, o: (i, 0))
    part = pl.BlockSpec((block, half_width), lambda i, o: (i, 0))
    return grid_call(
        "middle_back",
        kernel,
        order,
        (rows // block,),
        [(own, row), (came, row), (middle, row), (grad_out, row), (vectors, whole_block(vectors))]
        + weight.inputs(),
        [
            (shape_of((rows, width), f32), row),
            (shape_of((rows, width), bf16), row),
            (shape_of((rows, half_width), bf16), part),
            (shape_of((rows, half_width), bf16), part),
            (shape_of((4, 8, width), f32), pl.BlockSpec((4, 8, width), lambda i, o: (0, 0, 0))),
        ],
        scratch=[pltpu.VMEM((block, width), bf16)] * 2,
    )


def project_back(order, grads, weight):
    rows = grads[0][0].shape[0]
    block = rows // 4
    width = 1024
    given = [g for half in grads for g in half]

    def kernel(order, *rest):
        parts = rest[:6]
        own_ref, sent_ref = rest[-2:]

        def save(ref, _):
            views = weight.views(rest[6:-2])
            lefts = [
                jnp.concatenate([r[...] for r in parts[3 * i : 3 * i + 3]], axis=1) for i in range(2)
            ]
            for half in range(2):
                total = 0.0
                for left, pair in zip(lefts, views):
                    total = total + mm(left, flat(*pair[half]), ACROSS)
                for k in range(4):
                    here = pl.ds(pl.multiple_of(owner(order, 4 * half + k) * 128, 128), 128)
                    ref[:, here] = total[:, 128 * k : 128 * (k + 1)].astype(ref.dtype)

        either(own_ref, sent_ref, save)

    row = pl.BlockSpec(
        (block, given[0].shape[1]), lambda i, o: (((i % 2) ^ pair_of(o)) * 2 + ((i // 2) ^ member_of(o)), 0)
    )
    return grid_call(
        "project_back",
        kernel,
        order,
        (4,),
        [(g, row) for g in given] + weight.inputs(),
        own_and_sent(rows // 2, width),
    )


def first_back(order, own, came, tokens, grad_middle, vectors, block=256):
    rows, width = own.shape

    def kernel(order, own_ref, came_ref, tok_ref, mid_ref, vec_ref, out_ref, sum_ref):
        @pl.when(pl.program_id(0) == 0)
        def _():
            sum_ref[...] = jnp.zeros_like(sum_ref)

        grad_norm = own_ref[...] + came_ref[...].astype(f32)
        xhat, rstd = normalized(tok_ref[...].astype(f32))
        total = mid_ref[...] + norm_back(xhat, rstd, grad_norm, vec_ref[0:1])
        out_ref[...] = total.astype(bf16)
        sum_ref[0] += rows_of_eight(grad_norm * xhat)
        sum_ref[1] += rows_of_eight(grad_norm)

    row = pl.BlockSpec((block, width), lambda i, o: (i, 0))
    return grid_call(
        "first_back",
        kernel,
        order,
        (rows // block,),
        [(own, row), (came, row), (tokens, row), (grad_middle, row), (vectors, whole_block(vectors))],
        [
            (shape_of((rows, width), bf16), row),
            (shape_of((2, 8, width), f32), pl.BlockSpec((2, 8, width), lambda i, o: (0, 0, 0))),
        ],
    )


def weight_grad(order, first, count, left, rights, block_of=owner, extra=None):
    wide = sum(columns for _, columns, _ in rights)
    extra = extra or ()
    more = extra[0].shape[2] if extra else 0
    together = 2

    def kernel(order, left_ref, *rest):
        right_refs, out_ref = rest[: len(rights)], rest[-1]
        at = first + together * pl.program_id(0)
        lefts = [lanes(left_ref, block_of(order, at + k)) for k in range(together)]
        picked_left = jnp.concatenate(lefts, axis=1)
        start = 0
        for ref in right_refs:
            total = mm(picked_left, ref[...], DOWN)
            width = total.shape[1]
            out_ref[:, :, start : start + width] = total.reshape(together, 128, width).astype(bf16)
            start += width
        if extra:
            kept, came = rest[len(rights) : -1]
            out_ref[:, :, start:] = (kept[...].astype(f32) + came[...].astype(f32)).astype(bf16)

    def right_spec(array, columns, which):
        return pl.BlockSpec(
            (array.shape[0], columns), lambda *_: (0, which), pipeline_mode=pl.Buffered(1)
        )

    def extra_spec(array, which):
        return pl.BlockSpec(
            (together, 128, more // 2), lambda i, o: (first // together + i, 0, which)
        )

    return grid_call(
        "weight_grad",
        kernel,
        order,
        (count // together,),
        [(left, whole_block(left))]
        + [(right[0], right_spec(*right)) for right in rights]
        + [(a, extra_spec(a, extra[2])) for a in extra[:2]],
        [
            (
                shape_of((count, 128, wide + more // 2), bf16),
                pl.BlockSpec((together, 128, wide + more // 2), lambda i, o: (i, 0, 0)),
            )
        ],
    )[0]


def head_of(order, part):
    return member_of(order) * 8 + (pair_of(order) ^ part) * 4 + 2 * pl.program_id(0)


def team_attend_kernel(part, order, q_ref, k_ref, v_ref, o_ref, total_ref, vt, su):
    at = pl.program_id(1)
    block = q_ref.shape[0]

    @pl.when(at == 0)
    def _():
        vt[...] = v_ref[...].T
        set_bias(order[2], head_of(order, part), su)

    def branch(b):
        nk = (b + 1) * block
        q = q_ref[...]
        outs, totals = [], []
        for h in range(2):
            st = scores(k_ref, q, h, su, nk, block)
            m = jnp.max(st, axis=0, keepdims=True)
            p = jnp.exp(st - m)
            l = jnp.sum(p, axis=0, keepdims=True)
            ot = mm(vt[64 * h : 64 * h + 64, :nk], p.astype(bf16), PLAIN)
            outs.append(ot / l)
            totals.append(m + jnp.log(l))
        o_ref[...] = jnp.concatenate(outs, axis=0).T.astype(bf16)
        total_ref[0] = jnp.concatenate(totals + [jnp.zeros((6, block), f32)], axis=0)

    for b in range(k_ref.shape[0] // block):
        pl.when(at == b)(partial(branch, b))


def kept_place(i, o):
    return ((i % 2) ^ member_of(o)) * 2 + ((i // 2) ^ pair_of(o))


def team_attend(order, qkv, part, block):
    rows = qkv.shape[0]
    whole = lambda kind: pl.BlockSpec((rows, 128), lambda p, i, o: (0, 2 * kind + p))
    return pl.pallas_call(
        partial(team_attend_kernel, part),
        name="team_attend",
        grid_spec=pltpu.PrefetchScalarGridSpec(
            num_scalar_prefetch=1,
            grid=(2, rows // block),
            in_specs=[pl.BlockSpec((block, 128), lambda p, i, o: (i, p)), whole(1), whole(2)],
            out_specs=[
                pl.BlockSpec((block, 128), lambda p, i, o: (kept_place(i, o), p)),
                pl.BlockSpec((1, 8, block), lambda p, i, o: (p, 0, i)),
            ],
            scratch_shapes=[pltpu.VMEM((128, rows), bf16), pltpu.VMEM((2, rows, 128), f32)],
        ),
        out_shape=[shape_of((rows, 256), bf16), shape_of((2, 8, rows), f32)],
        compiler_params=pltpu.CompilerParams(vmem_limit_bytes=16 << 20),
        cost_estimate=WORK,
    )(order, qkv, qkv, qkv)


def team_back_kernel(
    part, order, q_ref, k_ref, v_ref, g_ref, total_ref, dq_ref, dk_ref, dv_ref, sum_ref,
    kt, su, dk, dv
):
    at = pl.program_id(1)
    block = q_ref.shape[0]
    blocks = k_ref.shape[0] // block

    @pl.when(at == 0)
    def _():
        kt[...] = k_ref[...].T
        set_bias(order[2], head_of(order, part), su)
        dk[...] = jnp.zeros_like(dk)
        dv[...] = jnp.zeros_like(dv)
        sum_ref[...] = jnp.zeros_like(sum_ref)

    def branch(b):
        nk = (b + 1) * block
        q, g = q_ref[...], g_ref[...]
        outs, dks, dvs = [], [], []
        for h in range(2):
            st = scores(k_ref, q, h, su, nk, block)
            p = jnp.exp(st - total_ref[0, h : h + 1])
            gm = half(g, h)
            dp = mm(v_ref[:nk], gm, ACROSS)
            inner = jnp.sum(p * dp, axis=0, keepdims=True)
            ds = (p * (dp - inner)).astype(bf16)
            outs.append(mm(kt[64 * h : 64 * h + 64, :nk], ds, PLAIN))
            dks.append(mm(ds, half(q, h), PLAIN))
            dvs.append(mm(p.astype(bf16), gm, PLAIN))
        low = (jnp.concatenate(outs, axis=0).T * 0.125).astype(bf16)
        dq_ref[...] = low
        sum_ref[0, 0] += rows_of_eight(low.astype(f32))
        dk[:nk] += dks[0] + dks[1]
        dv[:nk] += dvs[0] + dvs[1]

    for b in range(blocks):
        pl.when(at == b)(partial(branch, b))

    @pl.when(at == blocks - 1)
    def _():
        dk_ref[...] = (dk[...] * 0.125).astype(bf16)
        low = dv[...].astype(bf16)
        dv_ref[...] = low
        sum_ref[0, 1] = rows_of_eight(low.astype(f32))


def team_back(order, qkv, grad, totals, part, block):
    rows = qkv.shape[0]
    whole = lambda kind: pl.BlockSpec((rows, 128), lambda p, i, o: (0, 2 * kind + p))
    by_rows = pl.BlockSpec((block, 128), lambda p, i, o: (i, p))
    by_head = pl.BlockSpec((rows, 128), lambda p, i, o: (0, p))
    return pl.pallas_call(
        partial(team_back_kernel, part),
        name="team_back",
        grid_spec=pltpu.PrefetchScalarGridSpec(
            num_scalar_prefetch=1,
            grid=(2, rows // block),
            in_specs=[
                by_rows,
                whole(1),
                whole(2),
                pl.BlockSpec((block, 128), lambda p, i, o: (kept_place(i, o), 2 * part + p)),
                pl.BlockSpec((1, 8, block), lambda p, i, o: (p, 0, i)),
            ],
            out_specs=[
                by_rows,
                by_head,
                by_head,
                pl.BlockSpec((1, 2, 8, 128), lambda p, i, o: (p, 0, 0, 0)),
            ],
            scratch_shapes=[
                pltpu.VMEM((128, rows), bf16),
                pltpu.VMEM((2, rows, 128), f32),
                pltpu.VMEM((rows, 128), f32),
                pltpu.VMEM((rows, 128), f32),
            ],
        ),
        out_shape=[shape_of((rows, 256), bf16)] * 3 + [shape_of((2, 2, 8, 128), f32)],
        compiler_params=pltpu.CompilerParams(vmem_limit_bytes=24 << 20),
        cost_estimate=WORK,
    )(order, qkv, qkv, qkv, grad, totals)


def joined(first, second):
    count, rows, width = first.shape

    def kernel(first_ref, second_ref, out_ref):
        out_ref[:count] = first_ref[...]
        out_ref[count:] = second_ref[...]

    return pl.pallas_call(
        kernel,
        name="joined",
        out_shape=shape_of((2 * count, rows, width), first.dtype),
        compiler_params=pltpu.CompilerParams(vmem_limit_bytes=12 << 20),
        cost_estimate=WORK,
    )(first, second)


def qkv_unit(order, qkv_weight, packed):
    def kernel(order, qkv_ref, packed_ref, unit_ref):
        unit_ref[0, :128] = jnp.concatenate(
            [
                qkv_ref[:, n * 192 + kind * 64 : n * 192 + kind * 64 + 64]
                for kind in range(3)
                for n in range(4)
            ],
            axis=1,
        )
        unit_ref[0, 128:] = jnp.concatenate([packed_ref[...], jnp.zeros((16, 640), bf16)], axis=1)

    share = lambda i, o: (0, member_of(o) * 2 + pair_of(o))
    return grid_call(
        "qkv_unit",
        kernel,
        order,
        (1,),
        [(qkv_weight, pl.BlockSpec((128, 768), share)), (packed, whole_block(packed))],
        [(shape_of((1, 144, 768), bf16), pl.BlockSpec((1, 144, 768), lambda i, o: (0, 0, 0)))],
    )[0]


def other_units(order, out_weight, up_weight, down_weight):
    def kernel(order, out_ref, up_ref, down_ref, out_unit, own_unit, other_unit, down_unit):
        c, x = member_of(order), pair_of(order)
        out_unit[0] = out_ref[...]
        for i in range(8):
            own_unit[0, :, 128 * i : 128 * i + 128] = lanes(up_ref, i * 4 + x * 2 + c)
            other_unit[0, :, 128 * i : 128 * i + 128] = lanes(up_ref, i * 4 + (1 - x) * 2 + c)
        down_unit[0] = down_ref[...]

    shapes = [(1, 128, 512), (1, 128, 1024), (1, 128, 1024), (1, 128, 1024)]
    return grid_call(
        "other_units",
        kernel,
        order,
        (1,),
        [
            (out_weight, pl.BlockSpec((128, 512), lambda i, o: (0, member_of(o)))),
            (up_weight, whole_block(up_weight)),
            (down_weight, pl.BlockSpec((128, 1024), lambda i, o: (o[1], 0))),
        ],
        [(shape_of(s, bf16), pl.BlockSpec(s, lambda i, o: (0, 0, 0))) for s in shapes],
    )


def unpacked(order, mine, came):
    def kernel(order, mine_ref, came_ref, vec_ref, qkv_ref, up_ref, tmp):
        c, x = member_of(order), pair_of(order)
        for i in range(8):
            values = (mine_ref if i < 4 else came_ref)[i % 4].astype(f32)
            start = owner(order, i) * 128
            vec_ref[:, pl.ds(pl.multiple_of(start, 128), 128)] = values
            tmp[i] = values
            for part in range(2):
                row = tmp[i, pl.ds(8 + (x ^ part) * 2 + c, 1)]
                up_ref[part : part + 1, pl.ds(pl.multiple_of(start, 128), 128)] = row
        for part in range(2):
            here = pl.ds(pl.multiple_of(c * 512 + (x ^ part) * 256, 128), 256)
            qkv_ref[part : part + 1] = jnp.concatenate(
                [vec_ref[6:7, here], jnp.zeros((1, 256), f32), vec_ref[7:8, here]], axis=1
            )

    spec = pl.BlockSpec((4, 16, 128), lambda i, o: (0, 8, 0))
    shapes = [(16, 1024), (2, 768), (2, 1024)]
    return grid_call(
        "unpacked",
        kernel,
        order,
        (1,),
        [(mine, spec), (came, spec)],
        [(shape_of(s, f32), pl.BlockSpec(s, lambda i, o: (0, 0))) for s in shapes],
        scratch=[pltpu.VMEM((8, 16, 128), f32)],
    )


def one_of(pair, index):
    return lax.dynamic_index_in_dim(pair, index, 0, keepdims=False)


def flipped(pair, index):
    return jnp.where(index == 0, pair, pair[::-1])


def after(value, *earlier):
    return lax.optimization_barrier((value,) + earlier)[0]


def team_program(
    tokens,
    cotangent,
    lengths,
    first_gain,
    first_shift,
    qkv_weight,
    qv_bias,
    out_weight,
    out_bias,
    second_gain,
    second_shift,
    up_weight,
    up_bias,
    down_weight,
    down_bias,
):
    _, block, width = tokens.shape
    own_rows = 2 * block
    f, s = lax.axis_index("fsdp"), lax.axis_index("seq")
    x, c = s // 2, s % 2
    over_x = lambda v: exchange(v, "seq", 2)
    over_y = lambda v: exchange(v, "fsdp", 1)
    over_z = lambda v, k: exchange(v, "fsdp", 2 * k)

    length = one_of(lengths, x)

    def over_core(value):
        return lax.cond(length > 0, lambda v: exchange(v, "seq", 1), lambda v: v, value)

    order = jnp.stack([f, s, length]).astype(jnp.int32)

    order = [jnp.stack([f, s, length]).astype(jnp.int32)]

    def wait_for(*values):
        order[0] = after(order[0], *values)

    def run(kernel, *operands, **options):
        result = kernel(order[0], *operands, **options)
        wait_for(result[0] if isinstance(result, (list, tuple)) else result)
        return result

    def join(first, second):
        result = joined(after(first, order[0]), second)
        wait_for(result)
        return result

    full = lambda a, b: ((a, 0, a.shape[2], 0), (b, 0, b.shape[2], 0))

    packed = [first_gain, first_shift, second_gain, second_shift, out_bias, down_bias, qv_bias, up_bias]
    packed = jnp.concatenate([v.reshape(-1, 128) for v in packed] + [jnp.zeros((4, 128), bf16)])
    unit_qkv = run(qkv_unit, qkv_weight, packed)
    tokens_came = over_x(one_of(tokens, 1 - x))
    unit_out, unit_up, unit_up_other, unit_down = run(
        other_units, out_weight, up_weight, down_weight
    )
    own_mine = one_of(tokens, x)
    other_mine, other_came = over_core(own_mine), over_core(tokens_came)
    grad_came = over_x(one_of(after(cotangent, tokens_came), 1 - x))
    z_qkv = join(unit_qkv, over_z(unit_qkv, 1))
    z_out = over_z(after(unit_out, z_qkv), 1)
    own_tokens = jnp.concatenate([own_mine, tokens_came])
    wait_for(other_mine, other_came)
    z_qkv = join(z_qkv, over_z(z_qkv, 2))
    y_qkv, xz_qkv = over_y(z_qkv), over_x(z_qkv)
    z_out = join(unit_out, z_out)
    z_out_came = over_z(z_out, 2)
    z_up = over_z(after(unit_up, z_out), 1)

    blocks_at = (jnp.arange(2) ^ x) * 2 + c
    valid = ((blocks_at[:, None] * block + jnp.arange(block)) < length).reshape(own_rows, 1)
    grad_own = jnp.concatenate([one_of(cotangent, x), grad_came])
    grad_own = jnp.where(valid, grad_own, jnp.zeros_like(grad_own))
    grad_other = over_core(grad_own)
    grad_all = jnp.concatenate([grad_own, grad_other])
    wait_for(grad_all)
    z_up = join(unit_up, z_up)
    z_up_came = over_z(z_up, 2)
    z_out = join(z_out, z_out_came)
    y_out = over_y(z_out)
    z_down = over_z(after(unit_down, z_up), 1)
    xy_qkv = over_x(y_qkv)
    qkv_own, qkv_other = full(z_qkv, y_qkv), full(xz_qkv, xy_qkv)
    vectors, bias_qkv, bias_up = run(unpacked, z_qkv, y_qkv)
    normed = run(first_norm, tokens, tokens_came, other_mine, other_came, vectors)
    projected = [None, None]
    mixed, totals = [None, None], [None, None]
    projected[0] = run(project, normed, bias_qkv, 0, Weight(qkv_own))
    mixed[0], totals[0] = run(team_attend, projected[0], 0, block)
    z_up = join(z_up, z_up_came)
    y_up = over_y(z_up)
    z_down = join(unit_down, z_down)
    z_down_came = over_z(z_down, 2)
    z_up_other = over_z(after(unit_up_other, z_down), 1)
    out_other = over_core(jnp.concatenate([z_out, y_out]))
    projected[1] = run(project, normed, bias_qkv, 1, Weight(qkv_other))
    wait_for(out_other)
    mixed[1], totals[1] = run(team_attend, projected[1], 1, block)
    out = Weight(full(z_out, y_out), ((out_other, 0, 512, 0), (out_other, 4, 512, 0)))
    sent = jnp.concatenate([m[own_rows:] for m in mixed], axis=1)
    mixed_rows = jnp.concatenate([m[:own_rows] for m in mixed] + [over_core(sent)], axis=1)
    middle, norm_own = run(out_and_norm, mixed_rows, own_tokens, vectors, out)
    norm_other = over_core(norm_own)
    wait_for(norm_other)
    z_down = join(z_down, z_down_came)
    y_down, xz_down = over_y(z_down), over_x(z_down)
    z_up_other = join(unit_up_other, z_up_other)
    z_up_other_came = over_z(z_up_other, 2)
    norm_all = jnp.concatenate([norm_own, norm_other])

    act, slope, grad_pre, pre_sums = ([None, None] for _ in range(4))
    up_sent, up_kept, up_came = ([None, None] for _ in range(3))

    def up_grad(part, first):
        return run(weight_grad, first, 4, norm_all, [(grad_pre[part], 1024, 0)])

    def down_grad(part, first, count):
        return run(weight_grad, first, count, act[part], [(grad_all, 1024, 0)])

    act[0], slope[0] = run(feed_up, norm_own, norm_other, bias_up, 0, Weight(full(z_up, y_up)))
    down_kept = down_grad(0, 0, 8)
    z_up_other = join(z_up_other, z_up_other_came)
    y_up_other = over_y(z_up_other)
    up = [full(z_up, y_up), full(z_up_other, y_up_other)]
    xy_down = over_x(y_down)
    down = [full(z_down, y_down), full(xz_down, xy_down)]
    grad_pre[0], pre_sums[0] = run(
        feed_down_back, grad_own, grad_other, slope[0], Weight(down[0])
    )
    up_sent[0] = up_grad(0, 4)
    up_came[0] = over_y(up_sent[0])
    up_kept[0] = up_grad(0, 0)
    act[1], slope[1] = run(feed_up, norm_own, norm_other, bias_up, 1, Weight(up[1]))
    down_sent = [None, None]
    for i in (1, 0):
        down_sent[i] = down_grad(1, 4 * i, 4)
    down_came = [over_x(sent) for sent in down_sent]
    wait_for(up_came[0])
    grad_pre[1], pre_sums[1] = run(
        feed_down_back, grad_own, grad_other, slope[1], Weight(down[1])
    )
    up_sent[1] = up_grad(1, 4)
    up_came[1] = over_y(up_sent[1])
    back_own, back_sent = run(
        feed_up_back,
        grad_pre,
        Weight(*up),
    )
    back_came = over_core(back_sent)
    up_kept[1] = up_grad(1, 0)
    grad_middle, branch, mixed_kept, mixed_sent, middle_sums = run(
        middle_back, back_own, back_came, middle, grad_own, vectors, out
    )
    grad_mixed = jnp.concatenate([mixed_kept, over_core(mixed_sent)])
    out_grad = lambda which: run(
        weight_grad, 0, 8, mixed_rows, [(branch, 512, which)], block_of=mixed_block
    )
    out_sent = out_grad(1)
    out_came = over_core(out_sent)
    out_kept = out_grad(0)

    def added(kept, came):
        return kept.astype(f32) + came.astype(f32)

    def low_sum(kept, came):
        return added(kept, came).astype(bf16)

    def z_pieces(total):
        return [total[k].astype(bf16) for k in (1, 2, 3)]

    def sum_z(total, pieces):
        result = total[0]
        for k, piece in enumerate(pieces):
            result = result + over_z(piece, k + 1).astype(f32)
        return result

    def qkv_grad(grads, first, part):
        rights = [(grad, 256, 0) for grad in grads]
        return run(weight_grad, first, 4, normed, rights, extra=(out_kept, out_came, part))

    def z_far(total):
        return total[2:].astype(bf16)

    def z_near(total, far_came):
        total = added(total[:2], far_came)
        return total[0], total[1].astype(bf16)

    up_x = low_sum(up_kept[1], up_came[1])
    up_x_came = over_x(up_x)
    down_y = low_sum(down_kept[4:], down_came[1])
    down_y_came = over_y(down_y)
    wait_for(up_x, down_y)
    *heads_other, sums_other = run(team_back, projected[1], grad_mixed, totals[1], 1, block)
    other_y_came = over_y(qkv_grad(heads_other, 4, 1))
    down_total = added(low_sum(after(down_kept[:4], order[0]), down_came[0]), down_y_came)
    down_far = z_far(down_total)
    down_far_came = over_z(down_far, 2)
    wait_for(down_far)
    other_kept = qkv_grad(heads_other, 0, 1)
    up_total = added(low_sum(after(up_kept[0], order[0]), up_came[0]), up_x_came)
    up_far = z_far(up_total)
    up_far_came = over_z(up_far, 2)
    wait_for(up_far)
    *heads_own, sums_own = run(team_back, projected[0], grad_mixed, totals[0], 0, block)
    other_x = low_sum(other_kept, other_y_came)
    other_x_came = over_x(other_x)
    wait_for(other_x)
    own_y_came = over_y(qkv_grad(heads_own, 4, 0))
    down_sum, down_near = z_near(down_total, down_far_came)
    down_near_came = over_z(down_near, 1)
    wait_for(down_near)
    first_own, first_sent = run(
        project_back, [heads_own, heads_other], Weight(qkv_own, qkv_other)
    )
    first_came = over_core(first_sent)
    up_sum, up_near = z_near(up_total, up_far_came)
    up_near_came = over_z(up_near, 1)
    wait_for(up_near, down_near_came)
    own_kept = qkv_grad(heads_own, 0, 0)
    row_grad, first_sums = run(first_back, first_own, first_came, own_tokens, grad_middle, vectors)
    qkv_total = added(own_kept, own_y_came) + other_x_came.astype(f32)
    qkv_pieces = z_pieces(qkv_total)
    wait_for(*qkv_pieces)
    fed_own, fed_sent = run(feed_down, act, Weight(*down))
    block_own = jnp.where(
        valid, middle + (fed_own + over_core(fed_sent).astype(f32)) + vectors[5:6], 0.0
    ).astype(bf16)

    def to_devices(rows):
        return flipped(jnp.stack([rows[:block], over_x(rows[block:])]), x)

    tokens_grad = to_devices(row_grad)
    block_out = to_devices(block_own)

    def over_pair(total):
        pieces = total.reshape(2, 64, -1)
        rows = flipped(jnp.stack([one_of(pieces, x), over_x(one_of(pieces, 1 - x))]), x)
        return jnp.swapaxes(rows, 0, 1)

    def over_team(total):
        pieces = total.reshape((2, 32) + total.shape[1:])
        rows = flipped(jnp.stack([one_of(pieces, c), over_core(one_of(pieces, 1 - c))]), c)
        return jnp.swapaxes(rows, 0, 1)

    down_sum = added(down_sum, down_near_came)
    up_sum = over_team(over_pair(added(up_sum, up_near_came)))
    up_sum = up_sum.reshape(32, 2, 2, 8, 128).transpose(0, 3, 2, 1, 4).reshape(32, 4096)
    qkv_sum = over_team(over_pair(sum_z(qkv_total, qkv_pieces)))
    out_sum = qkv_sum[..., 768:].reshape(32, width)
    qkv_sum = qkv_sum[..., :768].reshape(32, 2, 2, 3, 4, 64)
    qkv_sum = jnp.transpose(qkv_sum, (0, 1, 2, 4, 3, 5)).reshape(32, 3 * width)

    at_member = jnp.arange(2) == c
    up_vector = flipped(jnp.sum(jnp.stack(pre_sums), axis=1).reshape(2, 8, 128), x)
    up_vector = jnp.where(
        at_member[None, None, :, None], jnp.swapaxes(up_vector, 0, 1)[:, :, None], 0.0
    ).reshape(32, 128)
    middle_sums = jnp.sum(middle_sums, axis=1).reshape(4, 32, 32)
    first_sums = jnp.sum(first_sums, axis=1).reshape(2, 32, 32)
    head_sums = flipped(jnp.sum(jnp.stack([sums_own, sums_other]), axis=3), x)

    def head_vector(kind):
        return jnp.where(at_member[:, None], head_sums[:, :, kind].reshape(1, 512), 0.0).reshape(32, 32)

    totals = jnp.concatenate(
        [middle_sums[i] for i in range(4)]
        + [up_vector, head_vector(0), head_vector(1), first_sums[0], first_sums[1]],
        axis=1,
    )
    totals = after(totals, *qkv_pieces)

    def summed(value):
        for axis, bit in (("seq", 1), ("seq", 2), ("fsdp", 1), ("fsdp", 2), ("fsdp", 4)):
            value = value + exchange(value, axis, bit)
        return value

    totals = lax.cond(length > 0, summed, lambda v: v, totals)
    totals = one_of(totals, f * 4 + s)
    piece = lambda i: totals[i * 32 : (i + 1) * 32]
    return (
        block_out,
        tokens_grad,
        piece(10),
        piece(11),
        qkv_sum,
        jnp.stack([piece(8), piece(9)]),
        out_sum,
        piece(2),
        piece(0),
        piece(1),
        up_sum,
        totals[128:256],
        down_sum,
        piece(3),
    )


def local(tokens, *others):
    width = tokens.shape[2]
    shards = (lax.axis_size("fsdp"), lax.axis_size("seq"))
    hidden = others[10].shape[1]
    if tokens.shape[0] == 2 and tokens.shape[1] % 256 == 0 and shards == (8, 4) and tokens.shape[1] * 4 <= 1024 and (width, hidden) == (1024, 4096):
        return team_program(tokens, *others)
    return general_program(tokens, *others)


def solution(mesh):
    return jax.shard_map(
        local,
        mesh=mesh,
        in_specs=(
            P("fsdp", "seq", None),
            P("fsdp", "seq", None),
            P("fsdp"),
            P("fsdp"),
            P("fsdp"),
            P("fsdp", None),
            P(None, "fsdp"),
            P("fsdp", None),
            P("fsdp"),
            P("fsdp"),
            P("fsdp"),
            P("fsdp", None),
            P("fsdp"),
            P("fsdp", None),
            P("fsdp"),
        ),
        out_specs=(
            P("fsdp", "seq", None),
            P("fsdp", "seq", None),
            P(("fsdp", "seq")),
            P(("fsdp", "seq")),
            P(("fsdp", "seq"), None),
            P(None, ("fsdp", "seq")),
            P(("fsdp", "seq"), None),
            P(("fsdp", "seq")),
            P(("fsdp", "seq")),
            P(("fsdp", "seq")),
            P(("fsdp", "seq"), None),
            P(("fsdp", "seq")),
            P(("fsdp", "seq"), None),
            P(("fsdp", "seq")),
        ),
        check_vma=False,
    )
```

```python
from functools import partial
import math

import jax
import jax.numpy as jnp
from jax import lax
from jax.experimental import pallas as pl
from jax.experimental.pallas import tpu as pltpu
from jax.sharding import PartitionSpec as P

H = 16


epsilon = 1e-05
f32 = jnp.float32
bf16 = jnp.bfloat16


def layer_norm(values, norm_gain, norm_shift):
    row_mean = jnp.mean(values, axis=-1, keepdims=True)
    centered = values - row_mean
    variance = jnp.mean(centered * centered, axis=-1, keepdims=True)
    return centered * lax.rsqrt(variance + epsilon) * norm_gain + norm_shift


def product(left_side, right_side):
    return jnp.dot(left_side, right_side, preferred_element_type=f32)


def contract_rows(left_side, right_side):
    return lax.dot_general(
        left_side, right_side, (((0,), (0,)), ((), ())), preferred_element_type=f32
    )


def against(left_side, right_side):
    return lax.dot_general(
        left_side, right_side, (((1,), (1,)), ((), ())), preferred_element_type=f32
    )


def head_scores(query_block, key_rows, start_row, slopes, length, score_scale):
    block_size = query_block.shape[1]
    seq_len = key_rows.shape[1]
    row_index = start_row + jnp.arange(block_size)
    columns = jnp.arange(seq_len)
    products = jnp.einsum("hqd,hkd->hqk", query_block, key_rows, preferred_element_type=f32)
    distance = (columns[None, :] - row_index[:, None]).astype(f32)
    allowed = (columns[None, :] <= row_index[:, None]) & (columns[None, :] < length)
    return jnp.where(
        allowed[None], products * score_scale + slopes[:, None, None] * distance, -jnp.inf
    )


def attend(queries, key_rows, value_rows, length, slopes, score_scale):
    head_count, seq_len, head_size = queries.shape
    block_size = math.gcd(512, seq_len)

    def one_block(start_row):
        query_block = lax.dynamic_slice_in_dim(queries, start_row, block_size, 1)
        scores = head_scores(query_block, key_rows, start_row, slopes, length, score_scale)
        largest = jnp.max(scores, axis=-1, keepdims=True)
        log_total = largest + jnp.log(jnp.sum(jnp.exp(scores - largest), axis=-1, keepdims=True))
        attention_probs = jnp.exp(scores - log_total).astype(bf16)
        mixed_rows = jnp.einsum(
            "hqk,hkd->hqd", attention_probs, value_rows, preferred_element_type=f32
        )
        return (mixed_rows.astype(bf16), log_total[..., 0])

    starts = jnp.arange(seq_len // block_size, dtype=jnp.int32) * block_size
    mixed_rows, log_totals = lax.map(one_block, starts)
    return (
        jnp.moveaxis(mixed_rows, 0, 1).reshape(head_count, seq_len, head_size),
        jnp.moveaxis(log_totals, 0, 1).reshape(head_count, seq_len),
    )


def attend_back(queries, key_rows, value_rows, grad_mixed, log_totals, length, slopes, score_scale):
    head_count, seq_len, head_size = queries.shape
    block_size = math.gcd(512, seq_len)

    def one_block(carried, start_row):
        key_sum, value_sum = carried
        query_block = lax.dynamic_slice_in_dim(queries, start_row, block_size, 1)
        grad_block = lax.dynamic_slice_in_dim(grad_mixed, start_row, block_size, 1)
        total_block = lax.dynamic_slice_in_dim(log_totals, start_row, block_size, 1)
        scores = head_scores(query_block, key_rows, start_row, slopes, length, score_scale)
        attention_probs = jnp.exp(scores - total_block[..., None])
        grad_probs = jnp.einsum(
            "hqd,hkd->hqk", grad_block, value_rows, preferred_element_type=f32
        )
        row_inner = jnp.sum(attention_probs * grad_probs, axis=-1, keepdims=True)
        grad_scores = (attention_probs * (grad_probs - row_inner)).astype(bf16)
        query_grad = (
            jnp.einsum("hqk,hkd->hqd", grad_scores, key_rows, preferred_element_type=f32)
            * score_scale
        ).astype(bf16)
        key_sum = (
            key_sum
            + jnp.einsum("hqk,hqd->hkd", grad_scores, query_block, preferred_element_type=f32)
            * score_scale
        )
        value_sum = value_sum + jnp.einsum(
            "hqk,hqd->hkd",
            attention_probs.astype(bf16),
            grad_block,
            preferred_element_type=f32,
        )
        return ((key_sum, value_sum), query_grad)

    starts = jnp.arange(seq_len // block_size, dtype=jnp.int32) * block_size
    empty = jnp.zeros(queries.shape, f32)
    (key_sum, value_sum), query_grads = lax.scan(one_block, (empty, empty), starts)
    query_grad = jnp.moveaxis(query_grads, 0, 1).reshape(head_count, seq_len, head_size)
    return (query_grad, key_sum.astype(bf16), value_sum.astype(bf16))


ACROSS = ((1,), (1,))
PLAIN = ((1,), (0,))
DOWN = ((0,), (0,))

def mm(left_side, right_side, dims):
    return lax.dot_general(left_side, right_side, (dims, ((), ())), preferred_element_type=f32)


def set_bias(length, head, su):
    rows = su.shape[1]
    u = lax.broadcasted_iota(jnp.int32, (rows, 128), 0)
    for h in range(2):
        power = jnp.full((rows, 128), head + (h + 1), jnp.int32).astype(f32)
        slope = jnp.exp2(power * (-8.0 / H))
        su[h] = jnp.where(u < length, u.astype(f32) * slope, -jnp.inf)


def half(value, h):
    lane = lax.broadcasted_iota(jnp.int32, value.shape, 1)
    return jnp.where((lane // 64) == h, value, jnp.zeros_like(value))


def scores(k_ref, q, h, su, nk, block):
    st = mm(k_ref[:nk], half(q, h) * jnp.asarray(0.125, bf16), ACROSS)
    st = st + jnp.concatenate([su[h, :nk]] * (block // 128), axis=1)
    keep = lax.broadcasted_iota(jnp.int32, (block, block), 0) <= lax.broadcasted_iota(
        jnp.int32, (block, block), 1
    )
    tail = jnp.where(keep, st[nk - block :], -jnp.inf)
    return tail if nk == block else jnp.concatenate([st[: nk - block], tail], axis=0)


def exchange(value, axis, bit):
    return lax.ppermute(value, axis, [(i, i ^ bit) for i in range(lax.axis_size(axis))])


def is_set(axis, bit):
    return (lax.axis_index(axis) // bit) % 2


def place(bit):
    return (0 if bit[0] == "fsdp" else 1, -bit[1])


def powers(size):
    return [1 << i for i in range(size.bit_length() - 1)]


def gather_bits(unit, order):
    held, buffer = [], unit
    for bit in order:
        received = exchange(buffer, *bit)
        second = is_set(*bit) == 1
        at = sum(1 for other in held if place(other) < place(bit))
        buffer = jnp.stack(
            [jnp.where(second, received, buffer), jnp.where(second, buffer, received)], axis=at
        )
        held.append(bit)
    return buffer


def scatter_bits(partial_sum, held, order):
    held, buffer = list(held), partial_sum
    for bit in order:
        at, mine = held.index(bit), is_set(*bit)
        sent = lax.dynamic_index_in_dim(buffer, 1 - mine, at, keepdims=False).astype(bf16)
        kept = lax.dynamic_index_in_dim(buffer, mine, at, keepdims=False).astype(f32)
        buffer = kept + exchange(sent, *bit).astype(f32)
        held.remove(bit)
    return buffer


def in_order(pieces, own):
    pieces = list(pieces)
    for bit in powers(len(pieces)):
        second = (own // bit) % 2 == 1
        pieces = [
            jnp.where(second, pieces[i ^ bit], pieces[i]) for i in range(len(pieces))
        ]
    return pieces


class Team:
    def __init__(self, micro_count):
        self.shards = lax.axis_size("seq")
        self.size = self.shards // micro_count
        self.micro_count = micro_count
        self.member = lax.axis_index("seq") % self.size
        self.which = lax.axis_index("seq") // self.size
        self.team_bits = [("seq", bit) for bit in powers(self.size)]
        self.pair_bits = [("seq", self.size * bit) for bit in powers(micro_count)]

    def to_sequences(self, pieces):
        arrived = []
        for offset in range(self.micro_count):
            sent = lax.dynamic_index_in_dim(pieces, self.which ^ offset, 0, keepdims=False)
            arrived.append(sent if offset == 0 else exchange(sent, "seq", offset * self.size))
        return jnp.stack(in_order(arrived, self.which))

    def share(self, own):
        arrived = [own if e == 0 else exchange(own, "seq", e) for e in range(self.size)]
        return jnp.stack(in_order(arrived, self.member), axis=1)

    def swap(self, pieces, axis, onto):
        arrived = []
        for e in range(self.size):
            sent = lax.dynamic_index_in_dim(pieces, self.member ^ e, axis, keepdims=False)
            arrived.append(sent if e == 0 else exchange(sent, "seq", e))
        return jnp.stack(in_order(arrived, self.member), axis=onto)

    def reduce(self, partial_sum):
        total = lax.dynamic_index_in_dim(partial_sum, self.member, 1, keepdims=False)
        for e in range(1, self.size):
            sent = lax.dynamic_index_in_dim(partial_sum, self.member ^ e, 1, keepdims=False)
            total = total + exchange(sent.astype(bf16), "seq", e).astype(f32)
        return total


def general_program(
    tokens,
    cotangent,
    lengths,
    first_gain,
    first_shift,
    qkv_weight,
    qv_bias,
    out_weight,
    out_bias,
    second_gain,
    second_shift,
    up_weight,
    up_bias,
    down_weight,
    down_bias,
):
    micro_count, block_rows, width = tokens.shape
    team = Team(micro_count)
    size, member, which = team.size, team.member, team.which
    shards = team.shards
    fsdp_shards = lax.axis_size("fsdp")
    seq_len = block_rows * shards
    head_size = width // H
    own_heads = H // size
    own_width = own_heads * head_size
    hidden = up_weight.shape[1]
    own_hidden = hidden // size
    fsdp_bits = [("fsdp", bit) for bit in powers(fsdp_shards)]
    line_bits = fsdp_bits[1:] + fsdp_bits[:1]
    pair_bits, team_bits = team.pair_bits, team.team_bits
    rows_first = lambda bits: sorted(bits, key=place)
    split = lambda bits: (2,) * len(bits)

    packed = jnp.concatenate(
        [
            first_gain,
            first_shift,
            second_gain,
            second_shift,
            out_bias,
            down_bias,
            qv_bias[0],
            qv_bias[1],
            up_bias,
        ]
    )
    packed = gather_bits(packed, line_bits).reshape(fsdp_shards, -1).astype(f32)
    part = width // fsdp_shards
    vectors = [packed[:, i * part : (i + 1) * part].reshape(width) for i in range(8)]
    gain_one, shift_one, gain_two, shift_two, bias_out, bias_down, bias_q, bias_v = vectors
    bias_up = packed[:, 8 * part :].reshape(hidden // (size * (hidden // (fsdp_shards * shards))), size, -1)
    bias_up = lax.dynamic_index_in_dim(bias_up, member, 1, keepdims=False).reshape(own_hidden)

    def part_rows(weight, bits, parts_of):
        rows = weight.shape[0] // parts_of
        index = jnp.int32(0)
        for bit in rows_first(bits):
            index = index * 2 + is_set(*bit)
        return lax.dynamic_slice_in_dim(weight, index * rows, rows, 0)

    qkv_own = lax.dynamic_slice_in_dim(qkv_weight, member * 3 * own_width, 3 * own_width, 1)
    qkv_own = jnp.swapaxes(qkv_own.reshape(-1, own_heads, 3, head_size), 1, 2).reshape(-1, 3 * own_width)
    whole_qkv = gather_bits(
        part_rows(qkv_own, pair_bits, micro_count), line_bits + pair_bits
    ).reshape(width, 3 * own_width)
    whole_out = gather_bits(
        part_rows(out_weight, pair_bits + team_bits, shards), line_bits + pair_bits + team_bits
    ).reshape(width, width)
    unit = hidden // (fsdp_shards * shards)
    up_own = lax.dynamic_index_in_dim(
        up_weight.reshape(width // fsdp_shards, hidden // (size * unit), size, unit),
        member,
        2,
        keepdims=False,
    ).reshape(width // fsdp_shards, own_hidden)
    whole_up = gather_bits(up_own, line_bits).reshape(width, own_hidden)
    down_own = lax.dynamic_index_in_dim(
        down_weight.reshape(micro_count, size, unit, width), member, 1, keepdims=False
    ).reshape(micro_count * unit, width)
    whole_down = gather_bits(
        part_rows(down_own, pair_bits, micro_count), line_bits + pair_bits
    ).reshape(own_hidden, width)

    length = lax.dynamic_index_in_dim(lengths, which, 0, keepdims=False)
    own_tokens = team.to_sequences(tokens)
    all_tokens = team.share(own_tokens).reshape(seq_len, width).astype(f32)
    own_rows = micro_count * block_rows
    own_tokens = own_tokens.reshape(own_rows, width).astype(f32)
    own_positions = (
        (jnp.arange(micro_count)[:, None] * size + member) * block_rows
        + jnp.arange(block_rows)[None, :]
    ).reshape(own_rows)
    valid_mask = (own_positions < length).astype(f32)[:, None]
    slopes = jnp.exp2(-((member * own_heads + jnp.arange(own_heads)).astype(f32) + 1.0) * 8.0 / H)
    score_scale = head_size ** (-0.5)

    by_member = (micro_count, size, block_rows)

    normed = layer_norm(all_tokens, gain_one, shift_one).astype(bf16)
    own_bias = lambda vector: lax.dynamic_slice_in_dim(vector, member * own_width, own_width, 0)
    bias_columns = jnp.concatenate([own_bias(bias_q), jnp.zeros((own_width,), f32), own_bias(bias_v)])
    projected = (product(normed, whole_qkv) + bias_columns).astype(bf16)
    split_heads = lambda value: jnp.moveaxis(value.reshape(seq_len, -1, head_size), 1, 0)
    join_heads = lambda value: jnp.moveaxis(value, 0, 1).reshape(seq_len, -1)
    queries, key_rows, value_rows = [
        split_heads(projected[:, i * own_width : (i + 1) * own_width]) for i in range(3)
    ]
    mixed, log_totals = attend(queries, key_rows, value_rows, length, slopes, score_scale)
    mixed = join_heads(mixed)
    mixed_rows = team.swap(mixed.reshape(by_member + (own_width,)), 1, 2).reshape(own_rows, width)
    middle = own_tokens + (product(mixed_rows, whole_out) + bias_out)
    normed_two_own = layer_norm(middle, gain_two, shift_two).astype(bf16)
    normed_two = team.share(normed_two_own.reshape(micro_count, block_rows, width)).reshape(
        seq_len, width
    )
    hidden_pre = product(normed_two, whole_up) + bias_up
    activation = jax.nn.gelu(hidden_pre, approximate=True).astype(bf16)
    fed = team.reduce(product(activation, whole_down).reshape(by_member + (width,)))
    block_own = (valid_mask * (middle + fed.reshape(own_rows, width) + bias_down)).astype(bf16)
    block_out = team.to_sequences(block_own.reshape(micro_count, block_rows, width))

    own_grad = team.to_sequences(cotangent)
    own_grad = jnp.where(
        (valid_mask > 0).reshape(micro_count, block_rows, 1), own_grad, jnp.zeros_like(own_grad)
    )
    grad_low = team.share(own_grad).reshape(seq_len, width)
    grad_out = own_grad.reshape(own_rows, width).astype(f32)
    down_bias_grad = jnp.sum(grad_out, axis=0)
    down_grad = contract_rows(activation, grad_low)
    grad_act = against(grad_low, whole_down)
    gelu_pull = jax.vjp(partial(jax.nn.gelu, approximate=True), hidden_pre)[1]
    grad_pre = gelu_pull(grad_act)[0].astype(bf16)
    up_grad = contract_rows(normed_two, grad_pre)
    up_bias_grad = jnp.sum(grad_pre.astype(f32), axis=0)
    grad_normed_two = team.reduce(
        against(grad_pre, whole_up).reshape(by_member + (width,))
    ).reshape(own_rows, width)
    norm_pull = jax.vjp(layer_norm, middle, gain_two, shift_two)[1]
    middle_part, second_gain_grad, second_shift_grad = norm_pull(grad_normed_two)
    grad_middle = grad_out + middle_part
    grad_branch = grad_middle.astype(bf16)
    out_bias_grad = jnp.sum(grad_branch.astype(f32), axis=0)
    out_grad = contract_rows(mixed_rows, grad_branch)
    grad_mixed_own = against(grad_branch, whole_out).astype(bf16)
    grad_mixed = team.swap(
        grad_mixed_own.reshape(micro_count, block_rows, size, own_width), 2, 1
    ).reshape(seq_len, own_width)
    backs = attend_back(
        queries,
        key_rows,
        value_rows,
        split_heads(grad_mixed),
        log_totals,
        length,
        slopes,
        score_scale,
    )
    grad_qkv = jnp.concatenate([join_heads(back) for back in backs], axis=1)
    qkv_grad = contract_rows(normed, grad_qkv)
    column_sums = jnp.sum(grad_qkv.astype(f32), axis=0).reshape(3, own_width)
    grad_normed = team.reduce(
        against(grad_qkv, whole_qkv).reshape(by_member + (width,))
    ).reshape(own_rows, width)
    first_pull = jax.vjp(layer_norm, own_tokens, gain_one, shift_one)[1]
    token_part, first_gain_grad, first_shift_grad = first_pull(grad_normed)
    row_grad = (grad_middle + token_part).astype(bf16)
    tokens_grad = team.to_sequences(row_grad.reshape(micro_count, block_rows, width))

    row_bits = rows_first(fsdp_bits + pair_bits)
    pair_first = pair_bits + fsdp_bits[:1] + fsdp_bits[:0:-1]
    pair_second = fsdp_bits[:1] + pair_bits + fsdp_bits[:0:-1]
    down_sum = scatter_bits(
        down_grad.reshape(split(row_bits) + (unit, width)), row_bits, pair_first
    )

    def by_columns(grad, order):
        total = scatter_bits(
            grad.reshape(split(row_bits) + (size, -1) + grad.shape[1:]), row_bits, order
        )
        return team.swap(total, 0, 1)

    up_sum = by_columns(up_grad, pair_second)
    up_sum = jnp.swapaxes(up_sum.reshape(-1, size, hidden // (size * unit), unit), 1, 2)
    up_sum = up_sum.reshape(-1, hidden)
    qkv_sum = by_columns(qkv_grad, pair_first).reshape(-1, size, 3, own_heads, head_size)
    qkv_sum = jnp.swapaxes(qkv_sum, 2, 3).reshape(-1, 3 * width)
    all_bits = rows_first(fsdp_bits + pair_bits + team_bits)
    out_sum = scatter_bits(
        out_grad.reshape(split(all_bits) + (-1, width)), all_bits, team_bits[::-1] + pair_first
    )

    devices = fsdp_shards * shards

    def spread(own, count):
        at_member = jnp.arange(size).reshape(1, size, 1) == member
        return jnp.where(at_member, own.reshape(count, 1, -1), 0.0)

    up_vector = spread(up_bias_grad, hidden // (size * unit)).reshape(devices, unit)
    by_team = lambda own: spread(own.reshape(1, own_width), 1).reshape(width)
    vectors = [
        first_gain_grad,
        first_shift_grad,
        second_gain_grad,
        second_shift_grad,
        out_bias_grad,
        down_bias_grad,
        by_team(column_sums[0]),
        by_team(column_sums[2]),
    ]
    buffer = jnp.concatenate([v.reshape(devices, -1) for v in vectors] + [up_vector], axis=1)
    buffer = buffer.reshape(split(all_bits) + (-1,))
    held = list(all_bits)
    for bit in team_bits + pair_first:
        at, mine = held.index(bit), is_set(*bit)
        sent = lax.dynamic_index_in_dim(buffer, 1 - mine, at, keepdims=False)
        kept = lax.dynamic_index_in_dim(buffer, mine, at, keepdims=False)
        buffer = kept + exchange(sent, *bit)
        held.remove(bit)
    each = width // devices
    sums = [buffer[i * each : (i + 1) * each] for i in range(8)]
    return (
        block_out,
        tokens_grad,
        sums[0],
        sums[1],
        qkv_sum,
        jnp.stack([sums[6], sums[7]]),
        out_sum,
        sums[4],
        sums[2],
        sums[3],
        up_sum,
        buffer[8 * each :],
        down_sum,
        sums[5],
    )


WORK = pl.CostEstimate(flops=10000000000, bytes_accessed=20000000, transcendentals=0)


def whole_block(array):
    return pl.BlockSpec(array.shape, lambda *_: (0,) * array.ndim, pipeline_mode=pl.Buffered(1))


def lanes(ref, block):
    return ref[:, pl.ds(pl.multiple_of(block * 128, 128), 128)]


def member_of(order):
    return order[1] & 1


def pair_of(order):
    return order[1] >> 1


def owner(order, i):
    return order[0] ^ ((i & 3) * 2 + (i >> 2))


def mixed_block(order, i):
    return owner(order, i) ^ (member_of(order) * 4 + pair_of(order) * 2)


def natural(order, i):
    return i


def picked(ref, order, first, block_of=owner):
    return jnp.concatenate([lanes(ref, block_of(order, first + i)) for i in range(4)], axis=1)


def flat(ref, start):
    value = ref[start : start + 4, :128]
    return value.reshape(512, value.shape[-1])


class Weight:
    def __init__(self, *parts, orders=None):
        self.parts = parts
        self.orders = orders or [owner] * len(parts)

    def slabs(self):
        found = []
        for pair in self.parts:
            for array, _, columns, which in pair:
                if not any(array is a and (columns, which) == b for a, b in found):
                    found.append((array, (columns, which)))
        return found

    def inputs(self):
        result = []
        for array, (columns, which) in self.slabs():
            spec = pl.BlockSpec(
                array.shape[:2] + (columns,),
                lambda *_, which=which: (0, 0, which),
                pipeline_mode=pl.Buffered(1),
            )
            result.append((array, spec))
        return result

    def views(self, refs):
        slabs = self.slabs()

        def find(view):
            array, first, columns, which = view
            at = [array is a and (columns, which) == b for a, b in slabs].index(True)
            return refs[at], first

        return [(find(pair[0]), find(pair[1])) for pair in self.parts]


def grid_call(name, kernel, order, grid, inputs, outputs, scratch=(), limit=16):
    return pl.pallas_call(
        kernel,
        name=name,
        grid_spec=pltpu.PrefetchScalarGridSpec(
            num_scalar_prefetch=1,
            grid=grid,
            in_specs=[spec for _, spec in inputs],
            out_specs=[spec for _, spec in outputs],
            scratch_shapes=list(scratch),
        ),
        out_shape=[shape for shape, _ in outputs],
        compiler_params=pltpu.CompilerParams(vmem_limit_bytes=limit << 20),
        cost_estimate=WORK,
    )(order, *[a for a, _ in inputs])


def shape_of(shape, dtype):
    return jax.ShapeDtypeStruct(shape, dtype)


def normalized(values):
    row_mean = jnp.mean(values, axis=-1, keepdims=True)
    centered = values - row_mean
    rstd = lax.rsqrt(jnp.mean(centered * centered, axis=-1, keepdims=True) + epsilon)
    return centered * rstd, rstd


def first_norm(order, tokens, came, other_mine, other_came, vectors):
    _, block, width = tokens.shape

    def kernel(order, mine_ref, came_ref, other_mine_ref, other_came_ref, vec_ref, out_ref):
        def write(ref):
            xhat, _ = normalized(ref[...].astype(f32))
            out_ref[...] = (xhat * vec_ref[0:1] + vec_ref[1:2]).astype(bf16)

        at = pl.program_id(0)
        for i, ref in enumerate((mine_ref.at[0], came_ref, other_mine_ref, other_came_ref)):
            pl.when(at == i)(partial(write, ref))

    def place(i, o):
        return (((i % 2) ^ pair_of(o)) * 2 + ((i // 2) ^ member_of(o)), 0)

    return grid_call(
        "first_norm",
        kernel,
        order,
        (4,),
        [(tokens, pl.BlockSpec((1, block, width), lambda i, o: (pair_of(o), 0, 0)))]
        + [(a, whole_block(a)) for a in (came, other_mine, other_came, vectors)],
        [(shape_of((4 * block, width), bf16), pl.BlockSpec((block, width), place))],
    )[0]


def project(order, normed, bias, part, weight, block=256):
    rows, width = normed.shape
    columns = bias.shape[1]
    step = columns // len(weight.parts)

    def kernel(order, lhs_ref, bias_ref, *rest):
        out_ref = rest[-1]
        left = [picked(lhs_ref, order, 0), picked(lhs_ref, order, 4)]
        for at, views in enumerate(weight.views(rest[:-1])):
            total = sum(mm(l, flat(*view), PLAIN) for l, view in zip(left, views))
            here = slice(at * step, (at + 1) * step)
            out_ref[:, here] = (total + bias_ref[part : part + 1, here]).astype(bf16)

    return grid_call(
        "project",
        kernel,
        order,
        (rows // block,),
        [(normed, pl.BlockSpec((block, width), lambda i, o: (i, 0))), (bias, whole_block(bias))]
        + weight.inputs(),
        [(shape_of((rows, columns), bf16), pl.BlockSpec((block, columns), lambda i, o: (i, 0)))],
    )[0]


def out_and_norm(order, mixed, tokens, vectors, weight, block=256):
    rows, width = mixed.shape

    def kernel(order, lhs_ref, tok_ref, vec_ref, *rest):
        middle_ref, norm_ref = rest[-2:]
        left = [picked(lhs_ref, order, i, mixed_block) for i in (0, 4)]
        for at, views in enumerate(weight.views(rest[:-2])):
            total = sum(mm(l, flat(*view), PLAIN) for l, view in zip(left, views))
            start = pl.multiple_of((member_of(order) ^ at) * (width // 2), 128)
            middle_ref[:, pl.ds(start, width // 2)] = total
        middle = tok_ref[...].astype(f32) + (middle_ref[...] + vec_ref[4:5])
        middle_ref[...] = middle
        xhat, _ = normalized(middle)
        norm_ref[...] = (xhat * vec_ref[2:3] + vec_ref[3:4]).astype(bf16)

    row = pl.BlockSpec((block, width), lambda i, o: (i, 0))
    return grid_call(
        "out_and_norm",
        kernel,
        order,
        (rows // block,),
        [(mixed, row), (tokens, row)]
        + [(vectors, whole_block(vectors))]
        + weight.inputs(),
        [(shape_of((rows, width), f32), row), (shape_of((rows, width), bf16), row)],
    )


def both(block, width):
    return (
        pl.BlockSpec((block, width), lambda i, o: (jnp.minimum(i, 1), 0)),
        pl.BlockSpec((block, width), lambda i, o: (jnp.maximum(i - 2, 0), 0)),
    )


def either(own_ref, other_ref, run):
    at = pl.program_id(0)
    pl.when(at < 2)(lambda: run(own_ref, True))
    pl.when(at >= 2)(lambda: run(other_ref, False))


ROOT = math.sqrt(2.0 / math.pi)


def gelu_and_slope(z):
    inner = jnp.tanh(ROOT * (z + 0.044715 * (z * z * z)))
    half_up = 0.5 * (1.0 + inner)
    slope = half_up + 0.5 * z * (1.0 - inner * inner) * (ROOT * (1.0 + 3 * 0.044715 * (z * z)))
    return z * half_up, slope


def feed_up(order, own, other, bias, part, weight):
    rows, width = own.shape
    block = rows // 2
    columns = bias.shape[1]

    def kernel(order, own_ref, other_ref, bias_ref, *rest):
        act_ref, slope_ref = rest[-2:]

        def run(lhs_ref, _):
            left = [picked(lhs_ref, order, i, weight.orders[0]) for i in (0, 4)]
            step = columns // len(weight.parts)
            for at, views in enumerate(weight.views(rest[:-2])):
                total = sum(mm(l, flat(*view), PLAIN) for l, view in zip(left, views))
                here = slice(at * step, (at + 1) * step)
                act, slope = gelu_and_slope(total + bias_ref[part : part + 1, here])
                act_ref[:, here] = act.astype(bf16)
                slope_ref[:, here] = slope.astype(bf16)

        either(own_ref, other_ref, run)

    row = pl.BlockSpec((block, columns), lambda i, o: (i, 0))
    return grid_call(
        "feed_up",
        kernel,
        order,
        (4,),
        list(zip((own, other), both(block, width)))
        + [(bias, whole_block(bias))]
        + weight.inputs(),
        [(shape_of((2 * rows, columns), bf16), row)] * 2,
    )


def own_and_sent(rows, width):
    block = rows // 2
    return list(
        zip(
            (shape_of((rows, width), f32), shape_of((rows, width), bf16)),
            both(block, width),
        )
    )


def feed_down(order, acts, weight):
    rows, columns = acts[0].shape
    width = 1024
    block = rows // 4
    count = len(acts)

    def kernel(order, *rest):
        own_ref, sent_ref = rest[-2:]
        total = 0.0
        for part, views, block_of in zip(rest[:count], weight.views(rest[count:-2]), weight.orders):
            for half, view in enumerate(views):
                total = total + mm(picked(part, order, 4 * half, block_of), flat(*view), PLAIN)

        def save(ref, _):
            ref[...] = total.astype(ref.dtype)

        either(own_ref, sent_ref, save)

    return grid_call(
        "feed_down",
        kernel,
        order,
        (4,),
        [(act, pl.BlockSpec((block, columns), lambda i, o: (i, 0))) for act in acts]
        + weight.inputs(),
        own_and_sent(rows // 2, width),
    )


def feed_down_back(order, own, other, slope, weight):
    rows, width = own.shape
    columns = slope.shape[1]
    block = rows // 2
    step = columns // len(weight.parts)

    def kernel(order, own_ref, other_ref, slope_ref, *rest):
        out_ref, sum_ref = rest[-2:]

        @pl.when(pl.program_id(0) == 0)
        def _():
            sum_ref[...] = jnp.zeros_like(sum_ref)

        def run(lhs_ref, _):
            left = lhs_ref[...]
            for at, views in enumerate(weight.views(rest[:-2])):
                for half, view in enumerate(views):
                    total = mm(left, flat(*view), ACROSS)
                    for k in range(4):
                        start = at * step + weight.orders[at](order, 4 * half + k) * 128
                        here = pl.ds(pl.multiple_of(start, 128), 128)
                        value = total[:, 128 * k : 128 * (k + 1)] * slope_ref[:, here].astype(f32)
                        low = value.astype(bf16)
                        out_ref[:, here] = low
                        sum_ref[:, here] += jnp.sum(
                            low.astype(f32).reshape(block // 8, 8, 128), axis=0
                        )

        either(own_ref, other_ref, run)

    row = pl.BlockSpec((block, columns), lambda i, o: (i, 0))
    return grid_call(
        "feed_down_back",
        kernel,
        order,
        (4,),
        list(zip((own, other), both(block, width)))
        + [(slope, row)]
        + weight.inputs(),
        [
            (shape_of((2 * rows, columns), bf16), row),
            (shape_of((8, columns), f32), pl.BlockSpec((8, columns), lambda i, o: (0, 0))),
        ],
    )


def feed_up_back(order, grads, weight):
    rows, columns = grads[0].shape
    width = 1024
    block = rows // 4
    count = len(grads)

    def kernel(order, *rest):
        own_ref, sent_ref, tmp = rest[-3:]
        each = len(weight.parts) // count
        step = columns // each
        for at, (pair, block_of) in enumerate(zip(weight.views(rest[count:-3]), weight.orders)):
            grad = rest[at // each][:, (at % each) * step : (at % each + 1) * step]
            for half in range(2):
                total = mm(grad, flat(*pair[half]), ACROSS)
                for k in range(4):
                    here = pl.ds(pl.multiple_of(block_of(order, 4 * half + k) * 128, 128), 128)
                    value = total[:, 128 * k : 128 * (k + 1)]
                    tmp[:, here] = value if at == 0 else tmp[:, here] + value

        def save(ref, _):
            ref[...] = tmp[...].astype(ref.dtype)

        either(own_ref, sent_ref, save)

    return grid_call(
        "feed_up_back",
        kernel,
        order,
        (4,),
        [(grad, pl.BlockSpec((block, columns), lambda i, o: (i, 0))) for grad in grads]
        + weight.inputs(),
        own_and_sent(rows // 2, width),
        scratch=[pltpu.VMEM((block, width), f32)],
    )


def rows_of_eight(value):
    return jnp.sum(value.reshape(value.shape[0] // 8, 8, value.shape[1]), axis=0)


def norm_back(xhat, rstd, grad_norm, gain):
    scaled = grad_norm * gain
    return rstd * (
        scaled
        - jnp.mean(scaled, axis=-1, keepdims=True)
        - xhat * jnp.mean(scaled * xhat, axis=-1, keepdims=True)
    )


def middle_back(order, own, came, middle, grad_out, vectors, weight, block=256):
    rows, width = middle.shape
    half_width = width // 2

    def kernel(order, own_ref, came_ref, middle_ref, dy_ref, vec_ref, *rest):
        grad_ref, branch_ref, keep_ref, sent_ref, sum_ref, tmp, low_ref = rest[-7:]

        @pl.when(pl.program_id(0) == 0)
        def _():
            sum_ref[...] = jnp.zeros_like(sum_ref)

        grad_norm = own_ref[...] + came_ref[...].astype(f32)
        xhat, rstd = normalized(middle_ref[...])
        grad_out = dy_ref[...].astype(f32)
        grad_middle = grad_out + norm_back(xhat, rstd, grad_norm, vec_ref[2:3])
        grad_ref[...] = grad_middle
        low = grad_middle.astype(bf16)
        low_ref[...] = low
        sum_ref[0] += rows_of_eight(grad_norm * xhat)
        sum_ref[1] += rows_of_eight(grad_norm)
        sum_ref[2] += rows_of_eight(low.astype(f32))
        sum_ref[3] += rows_of_eight(grad_out)
        views = weight.views(rest[:-7])
        member = member_of(order)
        for i in range(4):
            from_ = i ^ (member * 2 + pair_of(order))
            branch_ref[:, 256 * i : 256 * i + 256] = low_ref[:, pl.ds(pl.multiple_of(from_ * 256, 128), 256)]
        for half in range(2):
            total = 0.0
            for at, pair in enumerate(views):
                start = pl.multiple_of((member ^ at) * half_width, 128)
                total = total + mm(low_ref[:, pl.ds(start, half_width)], flat(*pair[half]), ACROSS)
            for k in range(4):
                here = pl.ds(pl.multiple_of(mixed_block(order, 4 * half + k) * 128, 128), 128)
                tmp[:, here] = total[:, 128 * k : 128 * (k + 1)].astype(bf16)
        keep_ref[...] = tmp[:, :half_width]
        sent_ref[...] = tmp[:, half_width:]

    row = pl.BlockSpec((block, width), lambda i, o: (i, 0))
    part = pl.BlockSpec((block, half_width), lambda i, o: (i, 0))
    return grid_call(
        "middle_back",
        kernel,
        order,
        (rows // block,),
        [(own, row), (came, row), (middle, row), (grad_out, row), (vectors, whole_block(vectors))]
        + weight.inputs(),
        [
            (shape_of((rows, width), f32), row),
            (shape_of((rows, width), bf16), row),
            (shape_of((rows, half_width), bf16), part),
            (shape_of((rows, half_width), bf16), part),
            (shape_of((4, 8, width), f32), pl.BlockSpec((4, 8, width), lambda i, o: (0, 0, 0))),
        ],
        scratch=[pltpu.VMEM((block, width), bf16)] * 2,
    )


def project_back(order, grads, weight):
    rows = grads[0][0].shape[0]
    block = rows // 4
    width = 1024
    given = [g for half in grads for g in half]

    def kernel(order, *rest):
        parts = rest[:6]
        own_ref, sent_ref = rest[-2:]

        def save(ref, _):
            views = weight.views(rest[6:-2])
            lefts = [
                jnp.concatenate([r[...] for r in parts[3 * i : 3 * i + 3]], axis=1) for i in range(2)
            ]
            for half in range(2):
                total = 0.0
                for left, pair in zip(lefts, views):
                    total = total + mm(left, flat(*pair[half]), ACROSS)
                for k in range(4):
                    here = pl.ds(pl.multiple_of(owner(order, 4 * half + k) * 128, 128), 128)
                    ref[:, here] = total[:, 128 * k : 128 * (k + 1)].astype(ref.dtype)

        either(own_ref, sent_ref, save)

    row = pl.BlockSpec(
        (block, given[0].shape[1]), lambda i, o: (((i % 2) ^ pair_of(o)) * 2 + ((i // 2) ^ member_of(o)), 0)
    )
    return grid_call(
        "project_back",
        kernel,
        order,
        (4,),
        [(g, row) for g in given] + weight.inputs(),
        own_and_sent(rows // 2, width),
    )


def first_back(order, own, came, tokens, grad_middle, vectors, block=256):
    rows, width = own.shape

    def kernel(order, own_ref, came_ref, tok_ref, mid_ref, vec_ref, out_ref, sum_ref):
        @pl.when(pl.program_id(0) == 0)
        def _():
            sum_ref[...] = jnp.zeros_like(sum_ref)

        grad_norm = own_ref[...] + came_ref[...].astype(f32)
        xhat, rstd = normalized(tok_ref[...].astype(f32))
        total = mid_ref[...] + norm_back(xhat, rstd, grad_norm, vec_ref[0:1])
        out_ref[...] = total.astype(bf16)
        sum_ref[0] += rows_of_eight(grad_norm * xhat)
        sum_ref[1] += rows_of_eight(grad_norm)

    row = pl.BlockSpec((block, width), lambda i, o: (i, 0))
    return grid_call(
        "first_back",
        kernel,
        order,
        (rows // block,),
        [(own, row), (came, row), (tokens, row), (grad_middle, row), (vectors, whole_block(vectors))],
        [
            (shape_of((rows, width), bf16), row),
            (shape_of((2, 8, width), f32), pl.BlockSpec((2, 8, width), lambda i, o: (0, 0, 0))),
        ],
    )


def weight_grad(order, first, count, left, rights, block_of=owner, extra=None):
    wide = sum(columns for _, columns, _ in rights)
    extra = extra or ()
    more = extra[0].shape[2] if extra else 0
    together = 2

    def kernel(order, left_ref, *rest):
        right_refs, out_ref = rest[: len(rights)], rest[-1]
        at = first + together * pl.program_id(0)
        lefts = [lanes(left_ref, block_of(order, at + k)) for k in range(together)]
        picked_left = jnp.concatenate(lefts, axis=1)
        start = 0
        for ref in right_refs:
            total = mm(picked_left, ref[...], DOWN)
            width = total.shape[1]
            out_ref[:, :, start : start + width] = total.reshape(together, 128, width).astype(bf16)
            start += width
        if extra:
            kept, came = rest[len(rights) : -1]
            out_ref[:, :, start:] = (kept[...].astype(f32) + came[...].astype(f32)).astype(bf16)

    def right_spec(array, columns, which):
        return pl.BlockSpec(
            (array.shape[0], columns), lambda *_: (0, which), pipeline_mode=pl.Buffered(1)
        )

    def extra_spec(array, which):
        return pl.BlockSpec(
            (together, 128, more // 2), lambda i, o: (first // together + i, 0, which)
        )

    return grid_call(
        "weight_grad",
        kernel,
        order,
        (count // together,),
        [(left, whole_block(left))]
        + [(right[0], right_spec(*right)) for right in rights]
        + [(a, extra_spec(a, extra[2])) for a in extra[:2]],
        [
            (
                shape_of((count, 128, wide + more // 2), bf16),
                pl.BlockSpec((together, 128, wide + more // 2), lambda i, o: (i, 0, 0)),
            )
        ],
    )[0]


def head_of(order, part):
    return member_of(order) * 8 + (pair_of(order) ^ part) * 4 + 2 * pl.program_id(0)


def team_attend_kernel(part, order, q_ref, k_ref, v_ref, o_ref, total_ref, vt, su):
    at = pl.program_id(1)
    block = q_ref.shape[0]

    @pl.when(at == 0)
    def _():
        vt[...] = v_ref[...].T
        set_bias(order[2], head_of(order, part), su)

    def branch(b):
        nk = (b + 1) * block
        q = q_ref[...]
        outs, totals = [], []
        for h in range(2):
            st = scores(k_ref, q, h, su, nk, block)
            m = jnp.max(st, axis=0, keepdims=True)
            p = jnp.exp(st - m)
            l = jnp.sum(p, axis=0, keepdims=True)
            ot = mm(vt[64 * h : 64 * h + 64, :nk], p.astype(bf16), PLAIN)
            outs.append(ot / l)
            totals.append(m + jnp.log(l))
        o_ref[...] = jnp.concatenate(outs, axis=0).T.astype(bf16)
        total_ref[0] = jnp.concatenate(totals + [jnp.zeros((6, block), f32)], axis=0)

    for b in range(k_ref.shape[0] // block):
        pl.when(at == b)(partial(branch, b))


def kept_place(i, o):
    return ((i % 2) ^ member_of(o)) * 2 + ((i // 2) ^ pair_of(o))


def team_attend(order, qkv, part, block):
    rows = qkv.shape[0]
    whole = lambda kind: pl.BlockSpec((rows, 128), lambda p, i, o: (0, 2 * kind + p))
    return pl.pallas_call(
        partial(team_attend_kernel, part),
        name="team_attend",
        grid_spec=pltpu.PrefetchScalarGridSpec(
            num_scalar_prefetch=1,
            grid=(2, rows // block),
            in_specs=[pl.BlockSpec((block, 128), lambda p, i, o: (i, p)), whole(1), whole(2)],
            out_specs=[
                pl.BlockSpec((block, 128), lambda p, i, o: (kept_place(i, o), p)),
                pl.BlockSpec((1, 8, block), lambda p, i, o: (p, 0, i)),
            ],
            scratch_shapes=[pltpu.VMEM((128, rows), bf16), pltpu.VMEM((2, rows, 128), f32)],
        ),
        out_shape=[shape_of((rows, 256), bf16), shape_of((2, 8, rows), f32)],
        compiler_params=pltpu.CompilerParams(vmem_limit_bytes=16 << 20),
        cost_estimate=WORK,
    )(order, qkv, qkv, qkv)


def team_back_kernel(
    part, order, q_ref, k_ref, v_ref, g_ref, total_ref, dq_ref, dk_ref, dv_ref, sum_ref,
    kt, su, dk, dv
):
    at = pl.program_id(1)
    block = q_ref.shape[0]
    blocks = k_ref.shape[0] // block

    @pl.when(at == 0)
    def _():
        kt[...] = k_ref[...].T
        set_bias(order[2], head_of(order, part), su)
        dk[...] = jnp.zeros_like(dk)
        dv[...] = jnp.zeros_like(dv)
        sum_ref[...] = jnp.zeros_like(sum_ref)

    def branch(b):
        nk = (b + 1) * block
        q, g = q_ref[...], g_ref[...]
        outs, dks, dvs = [], [], []
        for h in range(2):
            st = scores(k_ref, q, h, su, nk, block)
            p = jnp.exp(st - total_ref[0, h : h + 1])
            gm = half(g, h)
            dp = mm(v_ref[:nk], gm, ACROSS)
            inner = jnp.sum(p * dp, axis=0, keepdims=True)
            ds = (p * (dp - inner)).astype(bf16)
            outs.append(mm(kt[64 * h : 64 * h + 64, :nk], ds, PLAIN))
            dks.append(mm(ds, half(q, h), PLAIN))
            dvs.append(mm(p.astype(bf16), gm, PLAIN))
        low = (jnp.concatenate(outs, axis=0).T * 0.125).astype(bf16)
        dq_ref[...] = low
        sum_ref[0, 0] += rows_of_eight(low.astype(f32))
        dk[:nk] += dks[0] + dks[1]
        dv[:nk] += dvs[0] + dvs[1]

    for b in range(blocks):
        pl.when(at == b)(partial(branch, b))

    @pl.when(at == blocks - 1)
    def _():
        dk_ref[...] = (dk[...] * 0.125).astype(bf16)
        low = dv[...].astype(bf16)
        dv_ref[...] = low
        sum_ref[0, 1] = rows_of_eight(low.astype(f32))


def team_back(order, qkv, grad, totals, part, block):
    rows = qkv.shape[0]
    whole = lambda kind: pl.BlockSpec((rows, 128), lambda p, i, o: (0, 2 * kind + p))
    by_rows = pl.BlockSpec((block, 128), lambda p, i, o: (i, p))
    by_head = pl.BlockSpec((rows, 128), lambda p, i, o: (0, p))
    return pl.pallas_call(
        partial(team_back_kernel, part),
        name="team_back",
        grid_spec=pltpu.PrefetchScalarGridSpec(
            num_scalar_prefetch=1,
            grid=(2, rows // block),
            in_specs=[
                by_rows,
                whole(1),
                whole(2),
                pl.BlockSpec((block, 128), lambda p, i, o: (kept_place(i, o), 2 * part + p)),
                pl.BlockSpec((1, 8, block), lambda p, i, o: (p, 0, i)),
            ],
            out_specs=[
                by_rows,
                by_head,
                by_head,
                pl.BlockSpec((1, 2, 8, 128), lambda p, i, o: (p, 0, 0, 0)),
            ],
            scratch_shapes=[
                pltpu.VMEM((128, rows), bf16),
                pltpu.VMEM((2, rows, 128), f32),
                pltpu.VMEM((rows, 128), f32),
                pltpu.VMEM((rows, 128), f32),
            ],
        ),
        out_shape=[shape_of((rows, 256), bf16)] * 3 + [shape_of((2, 2, 8, 128), f32)],
        compiler_params=pltpu.CompilerParams(vmem_limit_bytes=24 << 20),
        cost_estimate=WORK,
    )(order, qkv, qkv, qkv, grad, totals)


def joined(first, second):
    count, rows, width = first.shape

    def kernel(first_ref, second_ref, out_ref):
        out_ref[:count] = first_ref[...]
        out_ref[count:] = second_ref[...]

    return pl.pallas_call(
        kernel,
        name="joined",
        out_shape=shape_of((2 * count, rows, width), first.dtype),
        compiler_params=pltpu.CompilerParams(vmem_limit_bytes=12 << 20),
        cost_estimate=WORK,
    )(first, second)


def qkv_unit(order, qkv_weight, packed):
    def kernel(order, qkv_ref, packed_ref, unit_ref):
        unit_ref[0, :128] = jnp.concatenate(
            [
                qkv_ref[:, n * 192 + kind * 64 : n * 192 + kind * 64 + 64]
                for kind in range(3)
                for n in range(4)
            ],
            axis=1,
        )
        unit_ref[0, 128:] = jnp.concatenate([packed_ref[...], jnp.zeros((16, 640), bf16)], axis=1)

    share = lambda i, o: (0, member_of(o) * 2 + pair_of(o))
    return grid_call(
        "qkv_unit",
        kernel,
        order,
        (1,),
        [(qkv_weight, pl.BlockSpec((128, 768), share)), (packed, whole_block(packed))],
        [(shape_of((1, 144, 768), bf16), pl.BlockSpec((1, 144, 768), lambda i, o: (0, 0, 0)))],
    )[0]


def other_units(order, out_weight, up_weight, down_weight):
    def kernel(order, out_ref, up_ref, down_ref, out_unit, own_unit, other_unit, down_unit):
        c, x = member_of(order), pair_of(order)
        out_unit[0] = out_ref[...]
        for i in range(8):
            own_unit[0, :, 128 * i : 128 * i + 128] = lanes(up_ref, i * 4 + x * 2 + c)
            other_unit[0, :, 128 * i : 128 * i + 128] = lanes(up_ref, i * 4 + (1 - x) * 2 + c)
        down_unit[0] = down_ref[...]

    shapes = [(1, 128, 512), (1, 128, 1024), (1, 128, 1024), (1, 128, 1024)]
    return grid_call(
        "other_units",
        kernel,
        order,
        (1,),
        [
            (out_weight, pl.BlockSpec((128, 512), lambda i, o: (0, member_of(o)))),
            (up_weight, whole_block(up_weight)),
            (down_weight, pl.BlockSpec((128, 1024), lambda i, o: (o[1], 0))),
        ],
        [(shape_of(s, bf16), pl.BlockSpec(s, lambda i, o: (0, 0, 0))) for s in shapes],
    )


def unpacked(order, mine, came):
    def kernel(order, mine_ref, came_ref, vec_ref, qkv_ref, up_ref, tmp):
        c, x = member_of(order), pair_of(order)
        for i in range(8):
            values = (mine_ref if i < 4 else came_ref)[i % 4].astype(f32)
            start = owner(order, i) * 128
            vec_ref[:, pl.ds(pl.multiple_of(start, 128), 128)] = values
            tmp[i] = values
            for part in range(2):
                row = tmp[i, pl.ds(8 + (x ^ part) * 2 + c, 1)]
                up_ref[part : part + 1, pl.ds(pl.multiple_of(start, 128), 128)] = row
        for part in range(2):
            here = pl.ds(pl.multiple_of(c * 512 + (x ^ part) * 256, 128), 256)
            qkv_ref[part : part + 1] = jnp.concatenate(
                [vec_ref[6:7, here], jnp.zeros((1, 256), f32), vec_ref[7:8, here]], axis=1
            )

    spec = pl.BlockSpec((4, 16, 128), lambda i, o: (0, 8, 0))
    shapes = [(16, 1024), (2, 768), (2, 1024)]
    return grid_call(
        "unpacked",
        kernel,
        order,
        (1,),
        [(mine, spec), (came, spec)],
        [(shape_of(s, f32), pl.BlockSpec(s, lambda i, o: (0, 0))) for s in shapes],
        scratch=[pltpu.VMEM((8, 16, 128), f32)],
    )


def one_of(pair, index):
    return lax.dynamic_index_in_dim(pair, index, 0, keepdims=False)


def flipped(pair, index):
    return jnp.where(index == 0, pair, pair[::-1])


def after(value, *earlier):
    return lax.optimization_barrier((value,) + earlier)[0]


def team_program(
    tokens,
    cotangent,
    lengths,
    first_gain,
    first_shift,
    qkv_weight,
    qv_bias,
    out_weight,
    out_bias,
    second_gain,
    second_shift,
    up_weight,
    up_bias,
    down_weight,
    down_bias,
):
    _, block, width = tokens.shape
    own_rows = 2 * block
    f, s = lax.axis_index("fsdp"), lax.axis_index("seq")
    x, c = s // 2, s % 2
    over_x = lambda v: exchange(v, "seq", 2)
    over_y = lambda v: exchange(v, "fsdp", 1)
    over_z = lambda v, k: exchange(v, "fsdp", 2 * k)

    length = one_of(lengths, x)

    def over_core(value):
        return lax.cond(length > 0, lambda v: exchange(v, "seq", 1), lambda v: v, value)

    order = jnp.stack([f, s, length]).astype(jnp.int32)

    order = [jnp.stack([f, s, length]).astype(jnp.int32)]

    def wait_for(*values):
        order[0] = after(order[0], *values)

    def run(kernel, *operands, **options):
        result = kernel(order[0], *operands, **options)
        wait_for(result[0] if isinstance(result, (list, tuple)) else result)
        return result

    def join(first, second):
        result = joined(after(first, order[0]), second)
        wait_for(result)
        return result

    full = lambda a, b: ((a, 0, a.shape[2], 0), (b, 0, b.shape[2], 0))

    packed = [first_gain, first_shift, second_gain, second_shift, out_bias, down_bias, qv_bias, up_bias]
    packed = jnp.concatenate([v.reshape(-1, 128) for v in packed] + [jnp.zeros((4, 128), bf16)])
    unit_qkv = run(qkv_unit, qkv_weight, packed)
    tokens_came = over_x(one_of(tokens, 1 - x))
    unit_out, unit_up, unit_up_other, unit_down = run(
        other_units, out_weight, up_weight, down_weight
    )
    own_mine = one_of(tokens, x)
    other_mine, other_came = over_core(own_mine), over_core(tokens_came)
    grad_came = over_x(one_of(after(cotangent, tokens_came), 1 - x))
    z_qkv = join(unit_qkv, over_z(unit_qkv, 1))
    z_out = over_z(after(unit_out, z_qkv), 1)
    own_tokens = jnp.concatenate([own_mine, tokens_came])
    wait_for(other_mine, other_came)
    z_qkv = join(z_qkv, over_z(z_qkv, 2))
    y_qkv, xz_qkv = over_y(z_qkv), over_x(z_qkv)
    z_out = join(unit_out, z_out)
    z_out_came = over_z(z_out, 2)
    z_up = over_z(after(unit_up, z_out), 1)

    blocks_at = (jnp.arange(2) ^ x) * 2 + c
    valid = ((blocks_at[:, None] * block + jnp.arange(block)) < length).reshape(own_rows, 1)
    grad_own = jnp.concatenate([one_of(cotangent, x), grad_came])
    grad_own = jnp.where(valid, grad_own, jnp.zeros_like(grad_own))
    grad_other = over_core(grad_own)
    grad_all = jnp.concatenate([grad_own, grad_other])
    wait_for(grad_all)
    z_up = join(unit_up, z_up)
    z_up_came = over_z(z_up, 2)
    z_out = join(z_out, z_out_came)
    y_out = over_y(z_out)
    z_down = over_z(after(unit_down, z_up), 1)
    xy_qkv = over_x(y_qkv)
    qkv_own, qkv_other = full(z_qkv, y_qkv), full(xz_qkv, xy_qkv)
    vectors, bias_qkv, bias_up = run(unpacked, z_qkv, y_qkv)
    normed = run(first_norm, tokens, tokens_came, other_mine, other_came, vectors)
    projected = [None, None]
    mixed, totals = [None, None], [None, None]
    projected[0] = run(project, normed, bias_qkv, 0, Weight(qkv_own))
    mixed[0], totals[0] = run(team_attend, projected[0], 0, block)
    z_up = join(z_up, z_up_came)
    y_up = over_y(z_up)
    z_down = join(unit_down, z_down)
    z_down_came = over_z(z_down, 2)
    z_up_other = over_z(after(unit_up_other, z_down), 1)
    out_other = over_core(jnp.concatenate([z_out, y_out]))
    projected[1] = run(project, normed, bias_qkv, 1, Weight(qkv_other))
    wait_for(out_other)
    mixed[1], totals[1] = run(team_attend, projected[1], 1, block)
    z_down = join(z_down, z_down_came)
    y_down, xz_down = over_y(z_down), over_x(z_down)
    z_up_other = join(unit_up_other, z_up_other)
    z_up_other_came = over_z(z_up_other, 2)
    out = Weight(full(z_out, y_out), ((out_other, 0, 512, 0), (out_other, 4, 512, 0)))
    sent = jnp.concatenate([m[own_rows:] for m in mixed], axis=1)
    mixed_rows = jnp.concatenate([m[:own_rows] for m in mixed] + [over_core(sent)], axis=1)
    middle, norm_own = run(out_and_norm, mixed_rows, own_tokens, vectors, out)
    norm_other = over_core(norm_own)
    wait_for(norm_other)
    norm_all = jnp.concatenate([norm_own, norm_other])

    act, slope, grad_pre, pre_sums = ([None, None] for _ in range(4))
    up_sent, up_kept, up_came = ([None, None] for _ in range(3))

    def up_grad(part, first):
        return run(weight_grad, first, 4, norm_all, [(grad_pre[part], 1024, 0)])

    def down_grad(part, first, count):
        return run(weight_grad, first, count, act[part], [(grad_all, 1024, 0)])

    act[0], slope[0] = run(feed_up, norm_own, norm_other, bias_up, 0, Weight(full(z_up, y_up)))
    z_up_other = join(z_up_other, z_up_other_came)
    y_up_other = over_y(z_up_other)
    down_kept = down_grad(0, 0, 8)
    up = [full(z_up, y_up), full(z_up_other, y_up_other)]
    xy_down = over_x(y_down)
    down = [full(z_down, y_down), full(xz_down, xy_down)]
    grad_pre[0], pre_sums[0] = run(
        feed_down_back, grad_own, grad_other, slope[0], Weight(down[0])
    )
    up_sent[0] = up_grad(0, 4)
    up_came[0] = over_y(up_sent[0])
    up_kept[0] = up_grad(0, 0)
    act[1], slope[1] = run(feed_up, norm_own, norm_other, bias_up, 1, Weight(up[1]))
    down_sent = [None, None]
    for i in (1, 0):
        down_sent[i] = down_grad(1, 4 * i, 4)
    down_came = [over_x(sent) for sent in down_sent]
    grad_pre[1], pre_sums[1] = run(
        feed_down_back, grad_own, grad_other, slope[1], Weight(down[1])
    )
    wait_for(up_came[0])
    up_sent[1] = up_grad(1, 4)
    up_came[1] = over_y(up_sent[1])
    back_own, back_sent = run(
        feed_up_back,
        grad_pre,
        Weight(*up),
    )
    back_came = over_core(back_sent)
    up_kept[1] = up_grad(1, 0)
    grad_middle, branch, mixed_kept, mixed_sent, middle_sums = run(
        middle_back, back_own, back_came, middle, grad_own, vectors, out
    )
    grad_mixed = jnp.concatenate([mixed_kept, over_core(mixed_sent)])
    out_grad = lambda which: run(
        weight_grad, 0, 8, mixed_rows, [(branch, 512, which)], block_of=mixed_block
    )
    out_sent = out_grad(1)
    out_came = over_core(out_sent)
    out_kept = out_grad(0)

    def added(kept, came):
        return kept.astype(f32) + came.astype(f32)

    def low_sum(kept, came):
        return added(kept, came).astype(bf16)

    def z_pieces(total):
        return [total[k].astype(bf16) for k in (1, 2, 3)]

    def sum_z(total, pieces):
        result = total[0]
        for k, piece in enumerate(pieces):
            result = result + over_z(piece, k + 1).astype(f32)
        return result

    def qkv_grad(grads, first, part):
        rights = [(grad, 256, 0) for grad in grads]
        return run(weight_grad, first, 4, normed, rights, extra=(out_kept, out_came, part))

    def z_far(total):
        return total[2:].astype(bf16)

    def z_near(total, far_came):
        total = added(total[:2], far_came)
        return total[0], total[1].astype(bf16)

    up_x = low_sum(up_kept[1], up_came[1])
    up_x_came = over_x(up_x)
    down_y = low_sum(down_kept[4:], down_came[1])
    down_y_came = over_y(down_y)
    wait_for(up_x, down_y)
    *heads_other, sums_other = run(team_back, projected[1], grad_mixed, totals[1], 1, block)
    other_y_came = over_y(qkv_grad(heads_other, 4, 1))
    down_total = added(low_sum(after(down_kept[:4], order[0]), down_came[0]), down_y_came)
    down_far = z_far(down_total)
    down_far_came = over_z(down_far, 2)
    wait_for(down_far)
    other_kept = qkv_grad(heads_other, 0, 1)
    *heads_own, sums_own = run(team_back, projected[0], grad_mixed, totals[0], 0, block)
    other_x = low_sum(other_kept, other_y_came)
    other_x_came = over_x(other_x)
    wait_for(other_x)
    own_y_came = over_y(qkv_grad(heads_own, 4, 0))
    up_total = added(low_sum(after(up_kept[0], order[0]), up_came[0]), up_x_came)
    up_far = z_far(up_total)
    up_far_came = over_z(up_far, 2)
    wait_for(up_far)
    fed_own, fed_sent = run(feed_down, act, Weight(*down))
    block_own = jnp.where(
        valid, middle + (fed_own + over_core(fed_sent).astype(f32)) + vectors[5:6], 0.0
    ).astype(bf16)
    down_sum, down_near = z_near(down_total, after(down_far_came, fed_own))
    down_near_came = over_z(down_near, 1)
    wait_for(down_near)
    first_own, first_sent = run(
        project_back, [heads_own, heads_other], Weight(qkv_own, qkv_other)
    )
    first_came = over_core(first_sent)
    up_sum, up_near = z_near(up_total, up_far_came)
    up_near_came = over_z(up_near, 1)
    wait_for(up_near, down_near_came)
    own_kept = qkv_grad(heads_own, 0, 0)
    qkv_total = added(own_kept, own_y_came) + other_x_came.astype(f32)
    qkv_pieces = z_pieces(qkv_total)
    wait_for(*qkv_pieces)
    row_grad, first_sums = run(first_back, first_own, first_came, own_tokens, grad_middle, vectors)

    def to_devices(rows):
        return flipped(jnp.stack([rows[:block], over_x(rows[block:])]), x)

    tokens_grad = to_devices(row_grad)
    block_out = to_devices(block_own)

    def over_pair(total):
        pieces = total.reshape(2, 64, -1)
        rows = flipped(jnp.stack([one_of(pieces, x), over_x(one_of(pieces, 1 - x))]), x)
        return jnp.swapaxes(rows, 0, 1)

    def over_team(total):
        pieces = total.reshape((2, 32) + total.shape[1:])
        rows = flipped(jnp.stack([one_of(pieces, c), over_core(one_of(pieces, 1 - c))]), c)
        return jnp.swapaxes(rows, 0, 1)

    down_sum = added(down_sum, down_near_came)
    up_sum = over_team(over_pair(added(up_sum, up_near_came)))
    up_sum = up_sum.reshape(32, 2, 2, 8, 128).transpose(0, 3, 2, 1, 4).reshape(32, 4096)
    qkv_sum = over_team(over_pair(sum_z(qkv_total, qkv_pieces)))
    out_sum = qkv_sum[..., 768:].reshape(32, width)
    qkv_sum = qkv_sum[..., :768].reshape(32, 2, 2, 3, 4, 64)
    qkv_sum = jnp.transpose(qkv_sum, (0, 1, 2, 4, 3, 5)).reshape(32, 3 * width)

    at_member = jnp.arange(2) == c
    up_vector = flipped(jnp.sum(jnp.stack(pre_sums), axis=1).reshape(2, 8, 128), x)
    up_vector = jnp.where(
        at_member[None, None, :, None], jnp.swapaxes(up_vector, 0, 1)[:, :, None], 0.0
    ).reshape(32, 128)
    middle_sums = jnp.sum(middle_sums, axis=1).reshape(4, 32, 32)
    first_sums = jnp.sum(first_sums, axis=1).reshape(2, 32, 32)
    head_sums = flipped(jnp.sum(jnp.stack([sums_own, sums_other]), axis=3), x)

    def head_vector(kind):
        return jnp.where(at_member[:, None], head_sums[:, :, kind].reshape(1, 512), 0.0).reshape(32, 32)

    totals = jnp.concatenate(
        [middle_sums[i] for i in range(4)]
        + [up_vector, head_vector(0), head_vector(1), first_sums[0], first_sums[1]],
        axis=1,
    )
    for step in (over_core, over_x, over_y, partial(over_z, k=1), partial(over_z, k=2)):
        totals = totals + step(totals)
    totals = one_of(totals, f * 4 + s)
    piece = lambda i: totals[i * 32 : (i + 1) * 32]
    return (
        block_out,
        tokens_grad,
        piece(10),
        piece(11),
        qkv_sum,
        jnp.stack([piece(8), piece(9)]),
        out_sum,
        piece(2),
        piece(0),
        piece(1),
        up_sum,
        totals[128:256],
        down_sum,
        piece(3),
    )


def local(tokens, *others):
    width = tokens.shape[2]
    shards = (lax.axis_size("fsdp"), lax.axis_size("seq"))
    hidden = others[10].shape[1]
    if tokens.shape[0] == 2 and tokens.shape[1] % 256 == 0 and shards == (8, 4) and tokens.shape[1] * 4 <= 1024 and (width, hidden) == (1024, 4096):
        return team_program(tokens, *others)
    return general_program(tokens, *others)


def solution(mesh):
    return jax.shard_map(
        local,
        mesh=mesh,
        in_specs=(
            P("fsdp", "seq", None),
            P("fsdp", "seq", None),
            P("fsdp"),
            P("fsdp"),
            P("fsdp"),
            P("fsdp", None),
            P(None, "fsdp"),
            P("fsdp", None),
            P("fsdp"),
            P("fsdp"),
            P("fsdp"),
            P("fsdp", None),
            P("fsdp"),
            P("fsdp", None),
            P("fsdp"),
        ),
        out_specs=(
            P("fsdp", "seq", None),
            P("fsdp", "seq", None),
            P(("fsdp", "seq")),
            P(("fsdp", "seq")),
            P(("fsdp", "seq"), None),
            P(None, ("fsdp", "seq")),
            P(("fsdp", "seq"), None),
            P(("fsdp", "seq")),
            P(("fsdp", "seq")),
            P(("fsdp", "seq")),
            P(("fsdp", "seq"), None),
            P(("fsdp", "seq")),
            P(("fsdp", "seq"), None),
            P(("fsdp", "seq")),
        ),
        check_vma=False,
    )
```

```python
from functools import partial
import math

import jax
import jax.numpy as jnp
from jax import lax
from jax.experimental import pallas as pl
from jax.experimental.pallas import tpu as pltpu
from jax.sharding import PartitionSpec as P

H = 16


epsilon = 1e-05
f32 = jnp.float32
bf16 = jnp.bfloat16


def layer_norm(values, norm_gain, norm_shift):
    row_mean = jnp.mean(values, axis=-1, keepdims=True)
    centered = values - row_mean
    variance = jnp.mean(centered * centered, axis=-1, keepdims=True)
    return centered * lax.rsqrt(variance + epsilon) * norm_gain + norm_shift


def product(left_side, right_side):
    return jnp.dot(left_side, right_side, preferred_element_type=f32)


def contract_rows(left_side, right_side):
    return lax.dot_general(
        left_side, right_side, (((0,), (0,)), ((), ())), preferred_element_type=f32
    )


def against(left_side, right_side):
    return lax.dot_general(
        left_side, right_side, (((1,), (1,)), ((), ())), preferred_element_type=f32
    )


def head_scores(query_block, key_rows, start_row, slopes, length, score_scale):
    block_size = query_block.shape[1]
    seq_len = key_rows.shape[1]
    row_index = start_row + jnp.arange(block_size)
    columns = jnp.arange(seq_len)
    products = jnp.einsum("hqd,hkd->hqk", query_block, key_rows, preferred_element_type=f32)
    distance = (columns[None, :] - row_index[:, None]).astype(f32)
    allowed = (columns[None, :] <= row_index[:, None]) & (columns[None, :] < length)
    return jnp.where(
        allowed[None], products * score_scale + slopes[:, None, None] * distance, -jnp.inf
    )


def attend(queries, key_rows, value_rows, length, slopes, score_scale):
    head_count, seq_len, head_size = queries.shape
    block_size = math.gcd(512, seq_len)

    def one_block(start_row):
        query_block = lax.dynamic_slice_in_dim(queries, start_row, block_size, 1)
        scores = head_scores(query_block, key_rows, start_row, slopes, length, score_scale)
        largest = jnp.max(scores, axis=-1, keepdims=True)
        log_total = largest + jnp.log(jnp.sum(jnp.exp(scores - largest), axis=-1, keepdims=True))
        attention_probs = jnp.exp(scores - log_total).astype(bf16)
        mixed_rows = jnp.einsum(
            "hqk,hkd->hqd", attention_probs, value_rows, preferred_element_type=f32
        )
        return (mixed_rows.astype(bf16), log_total[..., 0])

    starts = jnp.arange(seq_len // block_size, dtype=jnp.int32) * block_size
    mixed_rows, log_totals = lax.map(one_block, starts)
    return (
        jnp.moveaxis(mixed_rows, 0, 1).reshape(head_count, seq_len, head_size),
        jnp.moveaxis(log_totals, 0, 1).reshape(head_count, seq_len),
    )


def attend_back(queries, key_rows, value_rows, grad_mixed, log_totals, length, slopes, score_scale):
    head_count, seq_len, head_size = queries.shape
    block_size = math.gcd(512, seq_len)

    def one_block(carried, start_row):
        key_sum, value_sum = carried
        query_block = lax.dynamic_slice_in_dim(queries, start_row, block_size, 1)
        grad_block = lax.dynamic_slice_in_dim(grad_mixed, start_row, block_size, 1)
        total_block = lax.dynamic_slice_in_dim(log_totals, start_row, block_size, 1)
        scores = head_scores(query_block, key_rows, start_row, slopes, length, score_scale)
        attention_probs = jnp.exp(scores - total_block[..., None])
        grad_probs = jnp.einsum(
            "hqd,hkd->hqk", grad_block, value_rows, preferred_element_type=f32
        )
        row_inner = jnp.sum(attention_probs * grad_probs, axis=-1, keepdims=True)
        grad_scores = (attention_probs * (grad_probs - row_inner)).astype(bf16)
        query_grad = (
            jnp.einsum("hqk,hkd->hqd", grad_scores, key_rows, preferred_element_type=f32)
            * score_scale
        ).astype(bf16)
        key_sum = (
            key_sum
            + jnp.einsum("hqk,hqd->hkd", grad_scores, query_block, preferred_element_type=f32)
            * score_scale
        )
        value_sum = value_sum + jnp.einsum(
            "hqk,hqd->hkd",
            attention_probs.astype(bf16),
            grad_block,
            preferred_element_type=f32,
        )
        return ((key_sum, value_sum), query_grad)

    starts = jnp.arange(seq_len // block_size, dtype=jnp.int32) * block_size
    empty = jnp.zeros(queries.shape, f32)
    (key_sum, value_sum), query_grads = lax.scan(one_block, (empty, empty), starts)
    query_grad = jnp.moveaxis(query_grads, 0, 1).reshape(head_count, seq_len, head_size)
    return (query_grad, key_sum.astype(bf16), value_sum.astype(bf16))


ACROSS = ((1,), (1,))
PLAIN = ((1,), (0,))
DOWN = ((0,), (0,))

def mm(left_side, right_side, dims):
    return lax.dot_general(left_side, right_side, (dims, ((), ())), preferred_element_type=f32)


def set_bias(length, head, su):
    rows = su.shape[1]
    u = lax.broadcasted_iota(jnp.int32, (rows, 128), 0)
    for h in range(2):
        power = jnp.full((rows, 128), head + (h + 1), jnp.int32).astype(f32)
        slope = jnp.exp2(power * (-8.0 / H))
        su[h] = jnp.where(u < length, u.astype(f32) * slope, -jnp.inf)


def half(value, h):
    lane = lax.broadcasted_iota(jnp.int32, value.shape, 1)
    return jnp.where((lane // 64) == h, value, jnp.zeros_like(value))


def scores(k_ref, q, h, su, nk, block):
    st = mm(k_ref[:nk], half(q, h) * jnp.asarray(0.125, bf16), ACROSS)
    st = st + jnp.concatenate([su[h, :nk]] * (block // 128), axis=1)
    keep = lax.broadcasted_iota(jnp.int32, (block, block), 0) <= lax.broadcasted_iota(
        jnp.int32, (block, block), 1
    )
    tail = jnp.where(keep, st[nk - block :], -jnp.inf)
    return tail if nk == block else jnp.concatenate([st[: nk - block], tail], axis=0)


def exchange(value, axis, bit):
    return lax.ppermute(value, axis, [(i, i ^ bit) for i in range(lax.axis_size(axis))])


def is_set(axis, bit):
    return (lax.axis_index(axis) // bit) % 2


def place(bit):
    return (0 if bit[0] == "fsdp" else 1, -bit[1])


def powers(size):
    return [1 << i for i in range(size.bit_length() - 1)]


def gather_bits(unit, order):
    held, buffer = [], unit
    for bit in order:
        received = exchange(buffer, *bit)
        second = is_set(*bit) == 1
        at = sum(1 for other in held if place(other) < place(bit))
        buffer = jnp.stack(
            [jnp.where(second, received, buffer), jnp.where(second, buffer, received)], axis=at
        )
        held.append(bit)
    return buffer


def scatter_bits(partial_sum, held, order):
    held, buffer = list(held), partial_sum
    for bit in order:
        at, mine = held.index(bit), is_set(*bit)
        sent = lax.dynamic_index_in_dim(buffer, 1 - mine, at, keepdims=False).astype(bf16)
        kept = lax.dynamic_index_in_dim(buffer, mine, at, keepdims=False).astype(f32)
        buffer = kept + exchange(sent, *bit).astype(f32)
        held.remove(bit)
    return buffer


def in_order(pieces, own):
    pieces = list(pieces)
    for bit in powers(len(pieces)):
        second = (own // bit) % 2 == 1
        pieces = [
            jnp.where(second, pieces[i ^ bit], pieces[i]) for i in range(len(pieces))
        ]
    return pieces


class Team:
    def __init__(self, micro_count):
        self.shards = lax.axis_size("seq")
        self.size = self.shards // micro_count
        self.micro_count = micro_count
        self.member = lax.axis_index("seq") % self.size
        self.which = lax.axis_index("seq") // self.size
        self.team_bits = [("seq", bit) for bit in powers(self.size)]
        self.pair_bits = [("seq", self.size * bit) for bit in powers(micro_count)]

    def to_sequences(self, pieces):
        arrived = []
        for offset in range(self.micro_count):
            sent = lax.dynamic_index_in_dim(pieces, self.which ^ offset, 0, keepdims=False)
            arrived.append(sent if offset == 0 else exchange(sent, "seq", offset * self.size))
        return jnp.stack(in_order(arrived, self.which))

    def share(self, own):
        arrived = [own if e == 0 else exchange(own, "seq", e) for e in range(self.size)]
        return jnp.stack(in_order(arrived, self.member), axis=1)

    def swap(self, pieces, axis, onto):
        arrived = []
        for e in range(self.size):
            sent = lax.dynamic_index_in_dim(pieces, self.member ^ e, axis, keepdims=False)
            arrived.append(sent if e == 0 else exchange(sent, "seq", e))
        return jnp.stack(in_order(arrived, self.member), axis=onto)

    def reduce(self, partial_sum):
        total = lax.dynamic_index_in_dim(partial_sum, self.member, 1, keepdims=False)
        for e in range(1, self.size):
            sent = lax.dynamic_index_in_dim(partial_sum, self.member ^ e, 1, keepdims=False)
            total = total + exchange(sent.astype(bf16), "seq", e).astype(f32)
        return total


def general_program(
    tokens,
    cotangent,
    lengths,
    first_gain,
    first_shift,
    qkv_weight,
    qv_bias,
    out_weight,
    out_bias,
    second_gain,
    second_shift,
    up_weight,
    up_bias,
    down_weight,
    down_bias,
):
    micro_count, block_rows, width = tokens.shape
    team = Team(micro_count)
    size, member, which = team.size, team.member, team.which
    shards = team.shards
    fsdp_shards = lax.axis_size("fsdp")
    seq_len = block_rows * shards
    head_size = width // H
    own_heads = H // size
    own_width = own_heads * head_size
    hidden = up_weight.shape[1]
    own_hidden = hidden // size
    fsdp_bits = [("fsdp", bit) for bit in powers(fsdp_shards)]
    line_bits = fsdp_bits[1:] + fsdp_bits[:1]
    pair_bits, team_bits = team.pair_bits, team.team_bits
    rows_first = lambda bits: sorted(bits, key=place)
    split = lambda bits: (2,) * len(bits)

    packed = jnp.concatenate(
        [
            first_gain,
            first_shift,
            second_gain,
            second_shift,
            out_bias,
            down_bias,
            qv_bias[0],
            qv_bias[1],
            up_bias,
        ]
    )
    packed = gather_bits(packed, line_bits).reshape(fsdp_shards, -1).astype(f32)
    part = width // fsdp_shards
    vectors = [packed[:, i * part : (i + 1) * part].reshape(width) for i in range(8)]
    gain_one, shift_one, gain_two, shift_two, bias_out, bias_down, bias_q, bias_v = vectors
    bias_up = packed[:, 8 * part :].reshape(hidden // (size * (hidden // (fsdp_shards * shards))), size, -1)
    bias_up = lax.dynamic_index_in_dim(bias_up, member, 1, keepdims=False).reshape(own_hidden)

    def part_rows(weight, bits, parts_of):
        rows = weight.shape[0] // parts_of
        index = jnp.int32(0)
        for bit in rows_first(bits):
            index = index * 2 + is_set(*bit)
        return lax.dynamic_slice_in_dim(weight, index * rows, rows, 0)

    qkv_own = lax.dynamic_slice_in_dim(qkv_weight, member * 3 * own_width, 3 * own_width, 1)
    qkv_own = jnp.swapaxes(qkv_own.reshape(-1, own_heads, 3, head_size), 1, 2).reshape(-1, 3 * own_width)
    whole_qkv = gather_bits(
        part_rows(qkv_own, pair_bits, micro_count), line_bits + pair_bits
    ).reshape(width, 3 * own_width)
    whole_out = gather_bits(
        part_rows(out_weight, pair_bits + team_bits, shards), line_bits + pair_bits + team_bits
    ).reshape(width, width)
    unit = hidden // (fsdp_shards * shards)
    up_own = lax.dynamic_index_in_dim(
        up_weight.reshape(width // fsdp_shards, hidden // (size * unit), size, unit),
        member,
        2,
        keepdims=False,
    ).reshape(width // fsdp_shards, own_hidden)
    whole_up = gather_bits(up_own, line_bits).reshape(width, own_hidden)
    down_own = lax.dynamic_index_in_dim(
        down_weight.reshape(micro_count, size, unit, width), member, 1, keepdims=False
    ).reshape(micro_count * unit, width)
    whole_down = gather_bits(
        part_rows(down_own, pair_bits, micro_count), line_bits + pair_bits
    ).reshape(own_hidden, width)

    length = lax.dynamic_index_in_dim(lengths, which, 0, keepdims=False)
    own_tokens = team.to_sequences(tokens)
    all_tokens = team.share(own_tokens).reshape(seq_len, width).astype(f32)
    own_rows = micro_count * block_rows
    own_tokens = own_tokens.reshape(own_rows, width).astype(f32)
    own_positions = (
        (jnp.arange(micro_count)[:, None] * size + member) * block_rows
        + jnp.arange(block_rows)[None, :]
    ).reshape(own_rows)
    valid_mask = (own_positions < length).astype(f32)[:, None]
    slopes = jnp.exp2(-((member * own_heads + jnp.arange(own_heads)).astype(f32) + 1.0) * 8.0 / H)
    score_scale = head_size ** (-0.5)

    by_member = (micro_count, size, block_rows)

    normed = layer_norm(all_tokens, gain_one, shift_one).astype(bf16)
    own_bias = lambda vector: lax.dynamic_slice_in_dim(vector, member * own_width, own_width, 0)
    bias_columns = jnp.concatenate([own_bias(bias_q), jnp.zeros((own_width,), f32), own_bias(bias_v)])
    projected = (product(normed, whole_qkv) + bias_columns).astype(bf16)
    split_heads = lambda value: jnp.moveaxis(value.reshape(seq_len, -1, head_size), 1, 0)
    join_heads = lambda value: jnp.moveaxis(value, 0, 1).reshape(seq_len, -1)
    queries, key_rows, value_rows = [
        split_heads(projected[:, i * own_width : (i + 1) * own_width]) for i in range(3)
    ]
    mixed, log_totals = attend(queries, key_rows, value_rows, length, slopes, score_scale)
    mixed = join_heads(mixed)
    mixed_rows = team.swap(mixed.reshape(by_member + (own_width,)), 1, 2).reshape(own_rows, width)
    middle = own_tokens + (product(mixed_rows, whole_out) + bias_out)
    normed_two_own = layer_norm(middle, gain_two, shift_two).astype(bf16)
    normed_two = team.share(normed_two_own.reshape(micro_count, block_rows, width)).reshape(
        seq_len, width
    )
    hidden_pre = product(normed_two, whole_up) + bias_up
    activation = jax.nn.gelu(hidden_pre, approximate=True).astype(bf16)
    fed = team.reduce(product(activation, whole_down).reshape(by_member + (width,)))
    block_own = (valid_mask * (middle + fed.reshape(own_rows, width) + bias_down)).astype(bf16)
    block_out = team.to_sequences(block_own.reshape(micro_count, block_rows, width))

    own_grad = team.to_sequences(cotangent)
    own_grad = jnp.where(
        (valid_mask > 0).reshape(micro_count, block_rows, 1), own_grad, jnp.zeros_like(own_grad)
    )
    grad_low = team.share(own_grad).reshape(seq_len, width)
    grad_out = own_grad.reshape(own_rows, width).astype(f32)
    down_bias_grad = jnp.sum(grad_out, axis=0)
    down_grad = contract_rows(activation, grad_low)
    grad_act = against(grad_low, whole_down)
    gelu_pull = jax.vjp(partial(jax.nn.gelu, approximate=True), hidden_pre)[1]
    grad_pre = gelu_pull(grad_act)[0].astype(bf16)
    up_grad = contract_rows(normed_two, grad_pre)
    up_bias_grad = jnp.sum(grad_pre.astype(f32), axis=0)
    grad_normed_two = team.reduce(
        against(grad_pre, whole_up).reshape(by_member + (width,))
    ).reshape(own_rows, width)
    norm_pull = jax.vjp(layer_norm, middle, gain_two, shift_two)[1]
    middle_part, second_gain_grad, second_shift_grad = norm_pull(grad_normed_two)
    grad_middle = grad_out + middle_part
    grad_branch = grad_middle.astype(bf16)
    out_bias_grad = jnp.sum(grad_branch.astype(f32), axis=0)
    out_grad = contract_rows(mixed_rows, grad_branch)
    grad_mixed_own = against(grad_branch, whole_out).astype(bf16)
    grad_mixed = team.swap(
        grad_mixed_own.reshape(micro_count, block_rows, size, own_width), 2, 1
    ).reshape(seq_len, own_width)
    backs = attend_back(
        queries,
        key_rows,
        value_rows,
        split_heads(grad_mixed),
        log_totals,
        length,
        slopes,
        score_scale,
    )
    grad_qkv = jnp.concatenate([join_heads(back) for back in backs], axis=1)
    qkv_grad = contract_rows(normed, grad_qkv)
    column_sums = jnp.sum(grad_qkv.astype(f32), axis=0).reshape(3, own_width)
    grad_normed = team.reduce(
        against(grad_qkv, whole_qkv).reshape(by_member + (width,))
    ).reshape(own_rows, width)
    first_pull = jax.vjp(layer_norm, own_tokens, gain_one, shift_one)[1]
    token_part, first_gain_grad, first_shift_grad = first_pull(grad_normed)
    row_grad = (grad_middle + token_part).astype(bf16)
    tokens_grad = team.to_sequences(row_grad.reshape(micro_count, block_rows, width))

    row_bits = rows_first(fsdp_bits + pair_bits)
    pair_first = pair_bits + fsdp_bits[:1] + fsdp_bits[:0:-1]
    pair_second = fsdp_bits[:1] + pair_bits + fsdp_bits[:0:-1]
    down_sum = scatter_bits(
        down_grad.reshape(split(row_bits) + (unit, width)), row_bits, pair_first
    )

    def by_columns(grad, order):
        total = scatter_bits(
            grad.reshape(split(row_bits) + (size, -1) + grad.shape[1:]), row_bits, order
        )
        return team.swap(total, 0, 1)

    up_sum = by_columns(up_grad, pair_second)
    up_sum = jnp.swapaxes(up_sum.reshape(-1, size, hidden // (size * unit), unit), 1, 2)
    up_sum = up_sum.reshape(-1, hidden)
    qkv_sum = by_columns(qkv_grad, pair_first).reshape(-1, size, 3, own_heads, head_size)
    qkv_sum = jnp.swapaxes(qkv_sum, 2, 3).reshape(-1, 3 * width)
    all_bits = rows_first(fsdp_bits + pair_bits + team_bits)
    out_sum = scatter_bits(
        out_grad.reshape(split(all_bits) + (-1, width)), all_bits, team_bits[::-1] + pair_first
    )

    devices = fsdp_shards * shards

    def spread(own, count):
        at_member = jnp.arange(size).reshape(1, size, 1) == member
        return jnp.where(at_member, own.reshape(count, 1, -1), 0.0)

    up_vector = spread(up_bias_grad, hidden // (size * unit)).reshape(devices, unit)
    by_team = lambda own: spread(own.reshape(1, own_width), 1).reshape(width)
    vectors = [
        first_gain_grad,
        first_shift_grad,
        second_gain_grad,
        second_shift_grad,
        out_bias_grad,
        down_bias_grad,
        by_team(column_sums[0]),
        by_team(column_sums[2]),
    ]
    buffer = jnp.concatenate([v.reshape(devices, -1) for v in vectors] + [up_vector], axis=1)
    buffer = buffer.reshape(split(all_bits) + (-1,))
    held = list(all_bits)
    for bit in team_bits + pair_first:
        at, mine = held.index(bit), is_set(*bit)
        sent = lax.dynamic_index_in_dim(buffer, 1 - mine, at, keepdims=False)
        kept = lax.dynamic_index_in_dim(buffer, mine, at, keepdims=False)
        buffer = kept + exchange(sent, *bit)
        held.remove(bit)
    each = width // devices
    sums = [buffer[i * each : (i + 1) * each] for i in range(8)]
    return (
        block_out,
        tokens_grad,
        sums[0],
        sums[1],
        qkv_sum,
        jnp.stack([sums[6], sums[7]]),
        out_sum,
        sums[4],
        sums[2],
        sums[3],
        up_sum,
        buffer[8 * each :],
        down_sum,
        sums[5],
    )


WORK = pl.CostEstimate(flops=10000000000, bytes_accessed=20000000, transcendentals=0)


def whole_block(array):
    return pl.BlockSpec(array.shape, lambda *_: (0,) * array.ndim, pipeline_mode=pl.Buffered(1))


def lanes(ref, block):
    return ref[:, pl.ds(pl.multiple_of(block * 128, 128), 128)]


def member_of(order):
    return order[1] & 1


def pair_of(order):
    return order[1] >> 1


def owner(order, i):
    return order[0] ^ ((i & 3) * 2 + (i >> 2))


def mixed_block(order, i):
    return owner(order, i) ^ (member_of(order) * 4 + pair_of(order) * 2)


def natural(order, i):
    return i


def picked(ref, order, first, block_of=owner):
    return jnp.concatenate([lanes(ref, block_of(order, first + i)) for i in range(4)], axis=1)


def flat(ref, start):
    value = ref[start : start + 4, :128]
    return value.reshape(512, value.shape[-1])


class Weight:
    def __init__(self, *parts, orders=None):
        self.parts = parts
        self.orders = orders or [owner] * len(parts)

    def slabs(self):
        found = []
        for pair in self.parts:
            for array, _, columns, which in pair:
                if not any(array is a and (columns, which) == b for a, b in found):
                    found.append((array, (columns, which)))
        return found

    def inputs(self):
        result = []
        for array, (columns, which) in self.slabs():
            spec = pl.BlockSpec(
                array.shape[:2] + (columns,),
                lambda *_, which=which: (0, 0, which),
                pipeline_mode=pl.Buffered(1),
            )
            result.append((array, spec))
        return result

    def tiles(self, columns=0, blocks=0):
        result = []
        for pair in self.parts:
            for array, first, wide, which in pair:
                if columns:
                    shape = (4, 128, columns)
                    place = lambda j, *_, f=first, w=which * (wide // columns): (f // 4, 0, w + j)
                else:
                    shape = (blocks, 128, wide)
                    place = lambda j, *_, f=first, w=which: (f // blocks + j, 0, w)
                result.append((array, pl.BlockSpec(shape, place)))
        return result

    def views(self, refs):
        slabs = self.slabs()

        def find(view):
            array, first, columns, which = view
            at = [array is a and (columns, which) == b for a, b in slabs].index(True)
            return refs[at], first

        return [(find(pair[0]), find(pair[1])) for pair in self.parts]


def grid_call(name, kernel, order, grid, inputs, outputs, scratch=(), limit=24):
    return pl.pallas_call(
        kernel,
        name=name,
        grid_spec=pltpu.PrefetchScalarGridSpec(
            num_scalar_prefetch=1,
            grid=grid,
            in_specs=[spec for _, spec in inputs],
            out_specs=[spec for _, spec in outputs],
            scratch_shapes=list(scratch),
        ),
        out_shape=[shape for shape, _ in outputs],
        compiler_params=pltpu.CompilerParams(vmem_limit_bytes=limit << 20),
        cost_estimate=WORK,
    )(order, *[a for a, _ in inputs])


def shape_of(shape, dtype):
    return jax.ShapeDtypeStruct(shape, dtype)


def normalized(values):
    row_mean = jnp.mean(values, axis=-1, keepdims=True)
    centered = values - row_mean
    rstd = lax.rsqrt(jnp.mean(centered * centered, axis=-1, keepdims=True) + epsilon)
    return centered * rstd, rstd


def first_norm(order, tokens, came, other_mine, other_came, vectors):
    _, block, width = tokens.shape

    def kernel(order, mine_ref, came_ref, other_mine_ref, other_came_ref, vec_ref, out_ref):
        def write(ref):
            xhat, _ = normalized(ref[...].astype(f32))
            out_ref[...] = (xhat * vec_ref[0:1] + vec_ref[1:2]).astype(bf16)

        at = pl.program_id(0)
        for i, ref in enumerate((mine_ref.at[0], came_ref, other_mine_ref, other_came_ref)):
            pl.when(at == i)(partial(write, ref))

    def place(i, o):
        return (((i % 2) ^ pair_of(o)) * 2 + ((i // 2) ^ member_of(o)), 0)

    return grid_call(
        "first_norm",
        kernel,
        order,
        (4,),
        [(tokens, pl.BlockSpec((1, block, width), lambda i, o: (pair_of(o), 0, 0)))]
        + [(a, whole_block(a)) for a in (came, other_mine, other_came, vectors)],
        [(shape_of((4 * block, width), bf16), pl.BlockSpec((block, width), place))],
    )[0]


def matrix(ref):
    value = ref[...]
    return value.reshape(value.shape[0] * value.shape[1], value.shape[2])


def project(order, normed, bias, part, weight, tile=256):
    rows, width = normed.shape
    columns = bias.shape[1]

    def kernel(order, lhs_ref, bias_ref, first_ref, second_ref, out_ref):
        total = mm(picked(lhs_ref, order, 0), matrix(first_ref), PLAIN)
        total = total + mm(picked(lhs_ref, order, 4), matrix(second_ref), PLAIN)
        out_ref[...] = (total + bias_ref[part : part + 1]).astype(bf16)

    return grid_call(
        "project",
        kernel,
        order,
        (columns // tile,),
        [(normed, whole_block(normed)), (bias, pl.BlockSpec((2, tile), lambda j, o: (0, j)))]
        + weight.tiles(columns=tile),
        [(shape_of((rows, columns), bf16), pl.BlockSpec((rows, tile), lambda j, o: (0, j)))],
    )[0]


def out_and_norm(order, mixed, tokens, vectors, weight, block=256):
    rows, width = mixed.shape

    def kernel(order, lhs_ref, tok_ref, vec_ref, *rest):
        middle_ref, norm_ref = rest[-2:]
        left = [picked(lhs_ref, order, i, mixed_block) for i in (0, 4)]
        for at, views in enumerate(weight.views(rest[:-2])):
            total = sum(mm(l, flat(*view), PLAIN) for l, view in zip(left, views))
            start = pl.multiple_of((member_of(order) ^ at) * (width // 2), 128)
            middle_ref[:, pl.ds(start, width // 2)] = total
        middle = tok_ref[...].astype(f32) + (middle_ref[...] + vec_ref[4:5])
        middle_ref[...] = middle
        xhat, _ = normalized(middle)
        norm_ref[...] = (xhat * vec_ref[2:3] + vec_ref[3:4]).astype(bf16)

    row = pl.BlockSpec((block, width), lambda i, o: (i, 0))
    return grid_call(
        "out_and_norm",
        kernel,
        order,
        (rows // block,),
        [(mixed, row), (tokens, row)]
        + [(vectors, whole_block(vectors))]
        + weight.inputs(),
        [(shape_of((rows, width), f32), row), (shape_of((rows, width), bf16), row)],
    )


ROOT = math.sqrt(2.0 / math.pi)


def gelu_and_slope(z):
    inner = jnp.tanh(ROOT * (z + 0.044715 * (z * z * z)))
    half_up = 0.5 * (1.0 + inner)
    slope = half_up + 0.5 * z * (1.0 - inner * inner) * (ROOT * (1.0 + 3 * 0.044715 * (z * z)))
    return z * half_up, slope


def feed_up(order, normed, bias, part, weight, tile=256):
    rows, width = normed.shape
    columns = bias.shape[1]

    def kernel(order, lhs_ref, bias_ref, first_ref, second_ref, act_ref, slope_ref):
        total = mm(picked(lhs_ref, order, 0), matrix(first_ref), PLAIN)
        total = total + mm(picked(lhs_ref, order, 4), matrix(second_ref), PLAIN)
        act, slope = gelu_and_slope(total + bias_ref[part : part + 1])
        act_ref[...] = act.astype(bf16)
        slope_ref[...] = slope.astype(bf16)

    out = pl.BlockSpec((rows, tile), lambda j, o: (0, j))
    return grid_call(
        "feed_up",
        kernel,
        order,
        (columns // tile,),
        [(normed, whole_block(normed)), (bias, pl.BlockSpec((2, tile), lambda j, o: (0, j)))]
        + weight.tiles(columns=tile),
        [(shape_of((rows, columns), bf16), out)] * 2,
    )


def own_and_sent(rows, width, tile):
    place = (lambda j, h, o: (0, j)) if tile < width else (lambda j, h, o: (0, 0))
    spec = pl.BlockSpec((rows, tile), place)
    return [(shape_of((rows, width), f32), spec), (shape_of((rows, width), bf16), spec)]


def half_rows(ref):
    rows = ref.shape[0] // 2
    return pl.ds(pl.multiple_of(pl.program_id(1) * rows, rows), rows)


def keep_or_send(own_ref, sent_ref, values):
    def save(ref):
        for where, value in values:
            ref[where] = value.astype(ref.dtype)

    pl.when(pl.program_id(1) == 0)(partial(save, own_ref))
    pl.when(pl.program_id(1) == 1)(partial(save, sent_ref))


def spread(order, totals):
    found = []
    for half, total in enumerate(totals):
        for k in range(2):
            block = owner(order, 4 * half + 2 * pl.program_id(0) + k)
            here = pl.ds(pl.multiple_of(block * 128, 128), 128)
            found.append(((slice(None), here), total[:, 128 * k : 128 * (k + 1)]))
    return found


def feed_down(order, acts, weight, tile=256):
    rows, columns = acts[0].shape
    width = 1024

    def kernel(order, first_act, second_act, *rest):
        weights, own_ref, sent_ref = rest[:4], rest[4], rest[5]
        here = half_rows(first_act)
        total = 0.0
        for part, act_ref in enumerate((first_act, second_act)):
            for half in range(2):
                left = picked(act_ref.at[here], order, 4 * half)
                total = total + mm(left, matrix(weights[2 * part + half]), PLAIN)
        keep_or_send(own_ref, sent_ref, [(Ellipsis, total)])

    return grid_call(
        "feed_down",
        kernel,
        order,
        (width // tile, 2),
        [(act, whole_block(act)) for act in acts] + weight.tiles(columns=tile),
        own_and_sent(rows // 2, width, tile),
    )


def feed_down_back(order, grad, slope, weight):
    rows, width = grad.shape
    columns = slope.shape[1]

    def kernel(order, lhs_ref, slope_ref, first_ref, second_ref, out_ref, sum_ref):
        @pl.when((pl.program_id(0) == 0) & (pl.program_id(1) == 0))
        def _():
            sum_ref[...] = jnp.zeros_like(sum_ref)

        here = half_rows(lhs_ref)
        left = lhs_ref[here]
        totals = [mm(left, matrix(ref), ACROSS) for ref in (first_ref, second_ref)]
        for (_, place), total in spread(order, totals):
            low = (total * slope_ref[here, place].astype(f32)).astype(bf16)
            out_ref[here, place] = low
            sum_ref[:, place] += rows_of_eight(low.astype(f32))

    return grid_call(
        "feed_down_back",
        kernel,
        order,
        (2, 2),
        [(grad, whole_block(grad)), (slope, whole_block(slope))] + weight.tiles(blocks=2),
        [
            (shape_of((rows, columns), bf16), pl.BlockSpec((rows, columns), lambda i, h, o: (0, 0))),
            (shape_of((8, columns), f32), pl.BlockSpec((8, columns), lambda i, h, o: (0, 0))),
        ],
    )


def feed_up_back(order, grads, weight):
    rows, columns = grads[0].shape
    width = 1024

    def kernel(order, first_grad, second_grad, *rest):
        weights, own_ref, sent_ref = rest[:4], rest[4], rest[5]
        here = half_rows(first_grad)
        totals = [
            mm(first_grad[here], matrix(weights[half]), ACROSS)
            + mm(second_grad[here], matrix(weights[2 + half]), ACROSS)
            for half in range(2)
        ]
        keep_or_send(own_ref, sent_ref, spread(order, totals))

    return grid_call(
        "feed_up_back",
        kernel,
        order,
        (2, 2),
        [(grad, whole_block(grad)) for grad in grads] + weight.tiles(blocks=2),
        own_and_sent(rows // 2, width, width),
    )


def rows_of_eight(value):
    return jnp.sum(value.reshape(value.shape[0] // 8, 8, value.shape[1]), axis=0)


def norm_back(xhat, rstd, grad_norm, gain):
    scaled = grad_norm * gain
    return rstd * (
        scaled
        - jnp.mean(scaled, axis=-1, keepdims=True)
        - xhat * jnp.mean(scaled * xhat, axis=-1, keepdims=True)
    )


def middle_back(order, own, came, middle, grad_out, vectors, weight, block=256):
    rows, width = middle.shape
    half_width = width // 2

    def kernel(order, own_ref, came_ref, middle_ref, dy_ref, vec_ref, *rest):
        grad_ref, branch_ref, keep_ref, sent_ref, sum_ref, tmp, low_ref = rest[-7:]

        @pl.when(pl.program_id(0) == 0)
        def _():
            sum_ref[...] = jnp.zeros_like(sum_ref)

        grad_norm = own_ref[...] + came_ref[...].astype(f32)
        xhat, rstd = normalized(middle_ref[...])
        grad_out = dy_ref[...].astype(f32)
        grad_middle = grad_out + norm_back(xhat, rstd, grad_norm, vec_ref[2:3])
        grad_ref[...] = grad_middle
        low = grad_middle.astype(bf16)
        low_ref[...] = low
        sum_ref[0] += rows_of_eight(grad_norm * xhat)
        sum_ref[1] += rows_of_eight(grad_norm)
        sum_ref[2] += rows_of_eight(low.astype(f32))
        sum_ref[3] += rows_of_eight(grad_out)
        views = weight.views(rest[:-7])
        member = member_of(order)
        for i in range(4):
            from_ = i ^ (member * 2 + pair_of(order))
            branch_ref[:, 256 * i : 256 * i + 256] = low_ref[:, pl.ds(pl.multiple_of(from_ * 256, 128), 256)]
        for half in range(2):
            total = 0.0
            for at, pair in enumerate(views):
                start = pl.multiple_of((member ^ at) * half_width, 128)
                total = total + mm(low_ref[:, pl.ds(start, half_width)], flat(*pair[half]), ACROSS)
            for k in range(4):
                here = pl.ds(pl.multiple_of(mixed_block(order, 4 * half + k) * 128, 128), 128)
                tmp[:, here] = total[:, 128 * k : 128 * (k + 1)].astype(bf16)
        keep_ref[...] = tmp[:, :half_width]
        sent_ref[...] = tmp[:, half_width:]

    row = pl.BlockSpec((block, width), lambda i, o: (i, 0))
    part = pl.BlockSpec((block, half_width), lambda i, o: (i, 0))
    return grid_call(
        "middle_back",
        kernel,
        order,
        (rows // block,),
        [(own, row), (came, row), (middle, row), (grad_out, row), (vectors, whole_block(vectors))]
        + weight.inputs(),
        [
            (shape_of((rows, width), f32), row),
            (shape_of((rows, width), bf16), row),
            (shape_of((rows, half_width), bf16), part),
            (shape_of((rows, half_width), bf16), part),
            (shape_of((4, 8, width), f32), pl.BlockSpec((4, 8, width), lambda i, o: (0, 0, 0))),
        ],
        scratch=[pltpu.VMEM((block, width), bf16)] * 2,
    )


def project_back(order, grads, weight):
    rows = grads[0][0].shape[0]
    block = rows // 4
    width = 1024
    given = [g for half in grads for g in half]

    def kernel(order, *rest):
        weights, own_ref, sent_ref = rest[6:10], rest[10], rest[11]

        def left(part):
            found = []
            for k in range(2):
                at = (k ^ pair_of(order)) * 2 + (pl.program_id(1) ^ member_of(order))
                here = pl.ds(pl.multiple_of(at * block, block), block)
                found.append(
                    jnp.concatenate([r[here] for r in rest[3 * part : 3 * part + 3]], axis=1)
                )
            return jnp.concatenate(found)

        lefts = [left(0), left(1)]
        totals = [
            mm(lefts[0], matrix(weights[half]), ACROSS)
            + mm(lefts[1], matrix(weights[2 + half]), ACROSS)
            for half in range(2)
        ]
        keep_or_send(own_ref, sent_ref, spread(order, totals))

    return grid_call(
        "project_back",
        kernel,
        order,
        (2, 2),
        [(g, whole_block(g)) for g in given] + weight.tiles(blocks=2),
        own_and_sent(rows // 2, width, width),
    )


def first_back(order, own, came, tokens, grad_middle, vectors, block=256):
    rows, width = own.shape

    def kernel(order, own_ref, came_ref, tok_ref, mid_ref, vec_ref, out_ref, sum_ref):
        @pl.when(pl.program_id(0) == 0)
        def _():
            sum_ref[...] = jnp.zeros_like(sum_ref)

        grad_norm = own_ref[...] + came_ref[...].astype(f32)
        xhat, rstd = normalized(tok_ref[...].astype(f32))
        total = mid_ref[...] + norm_back(xhat, rstd, grad_norm, vec_ref[0:1])
        out_ref[...] = total.astype(bf16)
        sum_ref[0] += rows_of_eight(grad_norm * xhat)
        sum_ref[1] += rows_of_eight(grad_norm)

    row = pl.BlockSpec((block, width), lambda i, o: (i, 0))
    return grid_call(
        "first_back",
        kernel,
        order,
        (rows // block,),
        [(own, row), (came, row), (tokens, row), (grad_middle, row), (vectors, whole_block(vectors))],
        [
            (shape_of((rows, width), bf16), row),
            (shape_of((2, 8, width), f32), pl.BlockSpec((2, 8, width), lambda i, o: (0, 0, 0))),
        ],
    )


def weight_grad(order, first, count, left, rights, block_of=owner, extra=None):
    wide = sum(columns for _, columns, _ in rights)
    extra = extra or ()
    more = extra[0].shape[2] if extra else 0
    together = 4

    def kernel(order, left_ref, *rest):
        right_refs, out_ref = rest[: len(rights)], rest[-1]
        at = first + together * pl.program_id(0)
        lefts = [lanes(left_ref, block_of(order, at + k)) for k in range(together)]
        picked_left = jnp.concatenate(lefts, axis=1)
        start = 0
        for ref in right_refs:
            total = mm(picked_left, ref[...], DOWN)
            width = total.shape[1]
            out_ref[:, :, start : start + width] = total.reshape(together, 128, width).astype(bf16)
            start += width
        if extra:
            kept, came = rest[len(rights) : -1]
            out_ref[:, :, start:] = (kept[...].astype(f32) + came[...].astype(f32)).astype(bf16)

    def right_spec(array, columns, which):
        return pl.BlockSpec(
            (array.shape[0], columns), lambda *_: (0, which), pipeline_mode=pl.Buffered(1)
        )

    def extra_spec(array, which):
        return pl.BlockSpec(
            (together, 128, more // 2), lambda i, o: (first // together + i, 0, which)
        )

    return grid_call(
        "weight_grad",
        kernel,
        order,
        (count // together,),
        [(left, whole_block(left))]
        + [(right[0], right_spec(*right)) for right in rights]
        + [(a, extra_spec(a, extra[2])) for a in extra[:2]],
        [
            (
                shape_of((count, 128, wide + more // 2), bf16),
                pl.BlockSpec((together, 128, wide + more // 2), lambda i, o: (i, 0, 0)),
            )
        ],
    )[0]


def head_of(order, part):
    return member_of(order) * 8 + (pair_of(order) ^ part) * 4 + 2 * pl.program_id(0)


def team_attend_kernel(part, order, q_ref, k_ref, v_ref, o_ref, total_ref, vt, su):
    at = pl.program_id(1)
    block = q_ref.shape[0]

    @pl.when(at == 0)
    def _():
        vt[...] = v_ref[...].T
        set_bias(order[2], head_of(order, part), su)

    def branch(b):
        nk = (b + 1) * block
        q = q_ref[...]
        outs, totals = [], []
        for h in range(2):
            st = scores(k_ref, q, h, su, nk, block)
            m = jnp.max(st, axis=0, keepdims=True)
            p = jnp.exp(st - m)
            l = jnp.sum(p, axis=0, keepdims=True)
            ot = mm(vt[64 * h : 64 * h + 64, :nk], p.astype(bf16), PLAIN)
            outs.append(ot / l)
            totals.append(m + jnp.log(l))
        o_ref[...] = jnp.concatenate(outs, axis=0).T.astype(bf16)
        total_ref[0] = jnp.concatenate(totals + [jnp.zeros((6, block), f32)], axis=0)

    for b in range(k_ref.shape[0] // block):
        pl.when(at == b)(partial(branch, b))


def kept_place(i, o):
    return ((i % 2) ^ member_of(o)) * 2 + ((i // 2) ^ pair_of(o))


def team_attend(order, qkv, part, block):
    rows = qkv.shape[0]
    whole = lambda kind: pl.BlockSpec((rows, 128), lambda p, i, o: (0, 2 * kind + p))
    return pl.pallas_call(
        partial(team_attend_kernel, part),
        name="team_attend",
        grid_spec=pltpu.PrefetchScalarGridSpec(
            num_scalar_prefetch=1,
            grid=(2, rows // block),
            in_specs=[pl.BlockSpec((block, 128), lambda p, i, o: (i, p)), whole(1), whole(2)],
            out_specs=[
                pl.BlockSpec((block, 128), lambda p, i, o: (kept_place(i, o), p)),
                pl.BlockSpec((1, 8, block), lambda p, i, o: (p, 0, i)),
            ],
            scratch_shapes=[pltpu.VMEM((128, rows), bf16), pltpu.VMEM((2, rows, 128), f32)],
        ),
        out_shape=[shape_of((rows, 256), bf16), shape_of((2, 8, rows), f32)],
        compiler_params=pltpu.CompilerParams(vmem_limit_bytes=16 << 20),
        cost_estimate=WORK,
    )(order, qkv, qkv, qkv)


def team_back_kernel(
    part, order, q_ref, k_ref, v_ref, g_ref, total_ref, dq_ref, dk_ref, dv_ref, sum_ref,
    kt, su, dk, dv
):
    at = pl.program_id(1)
    block = q_ref.shape[0]
    blocks = k_ref.shape[0] // block

    @pl.when(at == 0)
    def _():
        kt[...] = k_ref[...].T
        set_bias(order[2], head_of(order, part), su)
        dk[...] = jnp.zeros_like(dk)
        dv[...] = jnp.zeros_like(dv)
        sum_ref[...] = jnp.zeros_like(sum_ref)

    def branch(b):
        nk = (b + 1) * block
        q, g = q_ref[...], g_ref[...]
        outs, dks, dvs = [], [], []
        for h in range(2):
            st = scores(k_ref, q, h, su, nk, block)
            p = jnp.exp(st - total_ref[0, h : h + 1])
            gm = half(g, h)
            dp = mm(v_ref[:nk], gm, ACROSS)
            inner = jnp.sum(p * dp, axis=0, keepdims=True)
            ds = (p * (dp - inner)).astype(bf16)
            outs.append(mm(kt[64 * h : 64 * h + 64, :nk], ds, PLAIN))
            dks.append(mm(ds, half(q, h), PLAIN))
            dvs.append(mm(p.astype(bf16), gm, PLAIN))
        low = (jnp.concatenate(outs, axis=0).T * 0.125).astype(bf16)
        dq_ref[...] = low
        sum_ref[0, 0] += rows_of_eight(low.astype(f32))
        dk[:nk] += dks[0] + dks[1]
        dv[:nk] += dvs[0] + dvs[1]

    for b in range(blocks):
        pl.when(at == b)(partial(branch, b))

    @pl.when(at == blocks - 1)
    def _():
        dk_ref[...] = (dk[...] * 0.125).astype(bf16)
        low = dv[...].astype(bf16)
        dv_ref[...] = low
        sum_ref[0, 1] = rows_of_eight(low.astype(f32))


def team_back(order, qkv, grad, totals, part, block):
    rows = qkv.shape[0]
    whole = lambda kind: pl.BlockSpec((rows, 128), lambda p, i, o: (0, 2 * kind + p))
    by_rows = pl.BlockSpec((block, 128), lambda p, i, o: (i, p))
    by_head = pl.BlockSpec((rows, 128), lambda p, i, o: (0, p))
    return pl.pallas_call(
        partial(team_back_kernel, part),
        name="team_back",
        grid_spec=pltpu.PrefetchScalarGridSpec(
            num_scalar_prefetch=1,
            grid=(2, rows // block),
            in_specs=[
                by_rows,
                whole(1),
                whole(2),
                pl.BlockSpec((block, 128), lambda p, i, o: (kept_place(i, o), 2 * part + p)),
                pl.BlockSpec((1, 8, block), lambda p, i, o: (p, 0, i)),
            ],
            out_specs=[
                by_rows,
                by_head,
                by_head,
                pl.BlockSpec((1, 2, 8, 128), lambda p, i, o: (p, 0, 0, 0)),
            ],
            scratch_shapes=[
                pltpu.VMEM((128, rows), bf16),
                pltpu.VMEM((2, rows, 128), f32),
                pltpu.VMEM((rows, 128), f32),
                pltpu.VMEM((rows, 128), f32),
            ],
        ),
        out_shape=[shape_of((rows, 256), bf16)] * 3 + [shape_of((2, 2, 8, 128), f32)],
        compiler_params=pltpu.CompilerParams(vmem_limit_bytes=24 << 20),
        cost_estimate=WORK,
    )(order, qkv, qkv, qkv, grad, totals)


def joined(first, second):
    count, rows, width = first.shape

    def kernel(first_ref, second_ref, out_ref):
        out_ref[:count] = first_ref[...]
        out_ref[count:] = second_ref[...]

    return pl.pallas_call(
        kernel,
        name="joined",
        out_shape=shape_of((2 * count, rows, width), first.dtype),
        compiler_params=pltpu.CompilerParams(vmem_limit_bytes=12 << 20),
        cost_estimate=WORK,
    )(first, second)


def qkv_unit(order, qkv_weight, packed):
    def kernel(order, qkv_ref, packed_ref, unit_ref):
        unit_ref[0, :128] = jnp.concatenate(
            [
                qkv_ref[:, n * 192 + kind * 64 : n * 192 + kind * 64 + 64]
                for kind in range(3)
                for n in range(4)
            ],
            axis=1,
        )
        unit_ref[0, 128:] = jnp.concatenate([packed_ref[...], jnp.zeros((16, 640), bf16)], axis=1)

    share = lambda i, o: (0, member_of(o) * 2 + pair_of(o))
    return grid_call(
        "qkv_unit",
        kernel,
        order,
        (1,),
        [(qkv_weight, pl.BlockSpec((128, 768), share)), (packed, whole_block(packed))],
        [(shape_of((1, 144, 768), bf16), pl.BlockSpec((1, 144, 768), lambda i, o: (0, 0, 0)))],
    )[0]


def other_units(order, out_weight, up_weight, down_weight):
    def kernel(order, out_ref, up_ref, down_ref, out_unit, own_unit, other_unit, down_unit):
        c, x = member_of(order), pair_of(order)
        out_unit[0] = out_ref[...]
        for i in range(8):
            own_unit[0, :, 128 * i : 128 * i + 128] = lanes(up_ref, i * 4 + x * 2 + c)
            other_unit[0, :, 128 * i : 128 * i + 128] = lanes(up_ref, i * 4 + (1 - x) * 2 + c)
        down_unit[0] = down_ref[...]

    shapes = [(1, 128, 512), (1, 128, 1024), (1, 128, 1024), (1, 128, 1024)]
    return grid_call(
        "other_units",
        kernel,
        order,
        (1,),
        [
            (out_weight, pl.BlockSpec((128, 512), lambda i, o: (0, member_of(o)))),
            (up_weight, whole_block(up_weight)),
            (down_weight, pl.BlockSpec((128, 1024), lambda i, o: (o[1], 0))),
        ],
        [(shape_of(s, bf16), pl.BlockSpec(s, lambda i, o: (0, 0, 0))) for s in shapes],
    )


def unpacked(order, mine, came):
    def kernel(order, mine_ref, came_ref, vec_ref, qkv_ref, up_ref, tmp):
        c, x = member_of(order), pair_of(order)
        for i in range(8):
            values = (mine_ref if i < 4 else came_ref)[i % 4].astype(f32)
            start = owner(order, i) * 128
            vec_ref[:, pl.ds(pl.multiple_of(start, 128), 128)] = values
            tmp[i] = values
            for part in range(2):
                row = tmp[i, pl.ds(8 + (x ^ part) * 2 + c, 1)]
                up_ref[part : part + 1, pl.ds(pl.multiple_of(start, 128), 128)] = row
        for part in range(2):
            here = pl.ds(pl.multiple_of(c * 512 + (x ^ part) * 256, 128), 256)
            qkv_ref[part : part + 1] = jnp.concatenate(
                [vec_ref[6:7, here], jnp.zeros((1, 256), f32), vec_ref[7:8, here]], axis=1
            )

    spec = pl.BlockSpec((4, 16, 128), lambda i, o: (0, 8, 0))
    shapes = [(16, 1024), (2, 768), (2, 1024)]
    return grid_call(
        "unpacked",
        kernel,
        order,
        (1,),
        [(mine, spec), (came, spec)],
        [(shape_of(s, f32), pl.BlockSpec(s, lambda i, o: (0, 0))) for s in shapes],
        scratch=[pltpu.VMEM((8, 16, 128), f32)],
    )


def vector_sums(order, middle, pre, heads, first):
    def kernel(order, middle_ref, pre_own, pre_other, own_ref, other_ref, first_ref, out_ref):
        c, x = member_of(order), pair_of(order)
        out_ref[...] = jnp.zeros_like(out_ref)
        for i in range(4):
            out_ref[i : i + 1] = jnp.sum(middle_ref[i], axis=0, keepdims=True)
        for i in range(2):
            out_ref[4 + i : 5 + i] = jnp.sum(first_ref[i], axis=0, keepdims=True)
        for part, ref in enumerate((own_ref, other_ref)):
            for pair in range(2):
                start = (c * 4 + (x ^ part) * 2 + pair) * 128
                here = pl.ds(pl.multiple_of(start, 128), 128)
                for kind in range(2):
                    total = jnp.sum(ref[pair, kind], axis=0, keepdims=True)
                    out_ref[6 + kind : 7 + kind, here] = total
        for part, ref in enumerate((pre_own, pre_other)):
            total = jnp.sum(ref[...], axis=0, keepdims=True)
            for i in range(8):
                start = (i % 2) * 512 + (x ^ part) * 256 + c * 128
                here = pl.ds(pl.multiple_of(start, 128), 128)
                row = 8 + i // 2
                out_ref[row : row + 1, here] = total[:, 128 * i : 128 * i + 128]

    arrays = (middle,) + tuple(pre) + tuple(heads) + (first,)
    return grid_call(
        "vector_sums",
        kernel,
        order,
        (1,),
        [(a, whole_block(a)) for a in arrays],
        [(shape_of((12, 1024), f32), pl.BlockSpec((12, 1024), lambda i, o: (0, 0)))],
    )[0]


def one_of(pair, index):
    return lax.dynamic_index_in_dim(pair, index, 0, keepdims=False)


def flipped(pair, index):
    return jnp.where(index == 0, pair, pair[::-1])


def after(value, *earlier):
    return lax.optimization_barrier((value,) + earlier)[0]


def team_program(
    tokens,
    cotangent,
    lengths,
    first_gain,
    first_shift,
    qkv_weight,
    qv_bias,
    out_weight,
    out_bias,
    second_gain,
    second_shift,
    up_weight,
    up_bias,
    down_weight,
    down_bias,
):
    _, block, width = tokens.shape
    own_rows = 2 * block
    f, s = lax.axis_index("fsdp"), lax.axis_index("seq")
    x, c = s // 2, s % 2
    over_x = lambda v: exchange(v, "seq", 2)
    over_y = lambda v: exchange(v, "fsdp", 1)
    over_z = lambda v, k: exchange(v, "fsdp", 2 * k)

    length = one_of(lengths, x)

    def over_core(value):
        return lax.cond(length > 0, lambda v: exchange(v, "seq", 1), lambda v: v, value)

    order = jnp.stack([f, s, length]).astype(jnp.int32)

    order = [jnp.stack([f, s, length]).astype(jnp.int32)]

    def wait_for(*values):
        order[0] = after(order[0], *values)

    def run(kernel, *operands, **options):
        result = kernel(order[0], *operands, **options)
        wait_for(result[0] if isinstance(result, (list, tuple)) else result)
        return result

    def join(first, second):
        result = joined(after(first, order[0]), second)
        wait_for(result)
        return result

    full = lambda a, b: ((a, 0, a.shape[2], 0), (b, 0, b.shape[2], 0))

    packed = [first_gain, first_shift, second_gain, second_shift, out_bias, down_bias, qv_bias, up_bias]
    packed = jnp.concatenate([v.reshape(-1, 128) for v in packed] + [jnp.zeros((4, 128), bf16)])
    unit_qkv = run(qkv_unit, qkv_weight, packed)
    tokens_came = over_x(one_of(tokens, 1 - x))
    unit_out, unit_up, unit_up_other, unit_down = run(
        other_units, out_weight, up_weight, down_weight
    )
    own_mine = one_of(tokens, x)
    other_mine, other_came = over_core(own_mine), over_core(tokens_came)
    grad_came = over_x(one_of(after(cotangent, tokens_came), 1 - x))
    z_qkv = join(unit_qkv, over_z(unit_qkv, 1))
    z_out = over_z(after(unit_out, z_qkv), 1)
    own_tokens = jnp.concatenate([own_mine, tokens_came])
    wait_for(other_mine, other_came)
    z_qkv = join(z_qkv, over_z(z_qkv, 2))
    y_qkv, xz_qkv = over_y(z_qkv), over_x(z_qkv)
    z_out = join(unit_out, z_out)
    z_out_came = over_z(z_out, 2)
    z_up = over_z(after(unit_up, z_out), 1)

    blocks_at = (jnp.arange(2) ^ x) * 2 + c
    valid = ((blocks_at[:, None] * block + jnp.arange(block)) < length).reshape(own_rows, 1)
    grad_own = jnp.concatenate([one_of(cotangent, x), grad_came])
    grad_own = jnp.where(valid, grad_own, jnp.zeros_like(grad_own))
    grad_other = over_core(grad_own)
    grad_all = jnp.concatenate([grad_own, grad_other])
    wait_for(grad_all)
    z_up = join(unit_up, z_up)
    z_up_came = over_z(z_up, 2)
    z_out = join(z_out, z_out_came)
    y_out = over_y(z_out)
    z_down = over_z(after(unit_down, z_up), 1)
    xy_qkv = over_x(y_qkv)
    qkv_own, qkv_other = full(z_qkv, y_qkv), full(xz_qkv, xy_qkv)
    vectors, bias_qkv, bias_up = run(unpacked, z_qkv, y_qkv)
    normed = run(first_norm, tokens, tokens_came, other_mine, other_came, vectors)
    projected = [None, None]
    mixed, totals = [None, None], [None, None]
    projected[0] = run(project, normed, bias_qkv, 0, Weight(qkv_own))
    mixed[0], totals[0] = run(team_attend, projected[0], 0, block)
    z_up = join(z_up, z_up_came)
    y_up = over_y(z_up)
    z_down = join(unit_down, z_down)
    z_down_came = over_z(z_down, 2)
    z_up_other = over_z(after(unit_up_other, z_down), 1)
    z_out_other, y_out_other = over_core(z_out), over_core(y_out)
    projected[1] = run(project, normed, bias_qkv, 1, Weight(qkv_other))
    wait_for(z_out_other, y_out_other)
    mixed[1], totals[1] = run(team_attend, projected[1], 1, block)
    z_down = join(z_down, z_down_came)
    y_down, xz_down = over_y(z_down), over_x(z_down)
    z_up_other = join(unit_up_other, z_up_other)
    z_up_other_came = over_z(z_up_other, 2)
    out = Weight(full(z_out, y_out), full(z_out_other, y_out_other))
    sent = jnp.concatenate([m[own_rows:] for m in mixed], axis=1)
    mixed_rows = jnp.concatenate([m[:own_rows] for m in mixed] + [over_core(sent)], axis=1)
    middle, norm_own = run(out_and_norm, mixed_rows, own_tokens, vectors, out)
    norm_other = over_core(norm_own)
    wait_for(norm_other)
    norm_all = jnp.concatenate([norm_own, norm_other])

    act, slope, grad_pre, pre_sums = ([None, None] for _ in range(4))
    up_sent, up_kept, up_came = ([None, None] for _ in range(3))

    def up_grad(part, first):
        return run(weight_grad, first, 4, norm_all, [(grad_pre[part], 1024, 0)])

    def down_grad(part, first, count):
        return run(weight_grad, first, count, act[part], [(grad_all, 1024, 0)])

    act[0], slope[0] = run(feed_up, norm_all, bias_up, 0, Weight(full(z_up, y_up)))
    z_up_other = join(z_up_other, z_up_other_came)
    y_up_other = over_y(z_up_other)
    down_kept = down_grad(0, 0, 8)
    up = [full(z_up, y_up), full(z_up_other, y_up_other)]
    xy_down = over_x(y_down)
    down = [full(z_down, y_down), full(xz_down, xy_down)]
    grad_pre[0], pre_sums[0] = run(
        feed_down_back, grad_all, slope[0], Weight(down[0])
    )
    up_sent[0] = up_grad(0, 4)
    up_came[0] = over_y(up_sent[0])
    up_kept[0] = up_grad(0, 0)
    act[1], slope[1] = run(feed_up, norm_all, bias_up, 1, Weight(up[1]))
    down_sent = [None, None]
    for i in (1, 0):
        down_sent[i] = down_grad(1, 4 * i, 4)
    down_came = [over_x(sent) for sent in down_sent]
    grad_pre[1], pre_sums[1] = run(
        feed_down_back, grad_all, slope[1], Weight(down[1])
    )
    wait_for(up_came[0])
    up_sent[1] = up_grad(1, 4)
    up_came[1] = over_y(up_sent[1])
    back_own, back_sent = run(
        feed_up_back,
        grad_pre,
        Weight(*up),
    )
    back_came = over_core(back_sent)
    up_kept[1] = up_grad(1, 0)
    grad_middle, branch, mixed_kept, mixed_sent, middle_sums = run(
        middle_back, back_own, back_came, middle, grad_own, vectors, out
    )
    grad_mixed = jnp.concatenate([mixed_kept, over_core(mixed_sent)])
    out_grad = lambda which: run(
        weight_grad, 0, 8, mixed_rows, [(branch, 512, which)], block_of=mixed_block
    )
    out_sent = out_grad(1)
    out_came = over_core(out_sent)
    out_kept = out_grad(0)

    def added(kept, came):
        return kept.astype(f32) + came.astype(f32)

    def low_sum(kept, came):
        return added(kept, came).astype(bf16)

    def z_pieces(total):
        return [total[k].astype(bf16) for k in (1, 2, 3)]

    def sum_z(total, pieces):
        result = total[0]
        for k, piece in enumerate(pieces):
            result = result + over_z(piece, k + 1).astype(f32)
        return result

    def qkv_grad(grads, first, part):
        rights = [(grad, 256, 0) for grad in grads]
        return run(weight_grad, first, 4, normed, rights, extra=(out_kept, out_came, part))

    def z_far(total):
        return total[2:].astype(bf16)

    def z_near(total, far_came):
        total = added(total[:2], far_came)
        return total[0], total[1].astype(bf16)

    up_x = low_sum(up_kept[1], up_came[1])
    up_x_came = over_x(up_x)
    down_y = low_sum(down_kept[4:], down_came[1])
    down_y_came = over_y(down_y)
    wait_for(up_x, down_y)
    *heads_other, sums_other = run(team_back, projected[1], grad_mixed, totals[1], 1, block)
    other_y_came = over_y(qkv_grad(heads_other, 4, 1))
    down_total = added(low_sum(after(down_kept[:4], order[0]), down_came[0]), down_y_came)
    down_far = z_far(down_total)
    down_far_came = over_z(down_far, 2)
    wait_for(down_far)
    other_kept = qkv_grad(heads_other, 0, 1)
    *heads_own, sums_own = run(team_back, projected[0], grad_mixed, totals[0], 0, block)
    other_x = low_sum(other_kept, other_y_came)
    other_x_came = over_x(other_x)
    wait_for(other_x)
    own_y_came = over_y(qkv_grad(heads_own, 4, 0))
    up_total = added(low_sum(after(up_kept[0], order[0]), up_came[0]), up_x_came)
    up_far = z_far(up_total)
    up_far_came = over_z(up_far, 2)
    wait_for(up_far)
    fed_own, fed_sent = run(feed_down, act, Weight(*down))
    block_own = jnp.where(
        valid, middle + (fed_own + over_core(fed_sent).astype(f32)) + vectors[5:6], 0.0
    ).astype(bf16)
    down_sum, down_near = z_near(down_total, after(down_far_came, fed_own))
    down_near_came = over_z(down_near, 1)
    wait_for(down_near)
    first_own, first_sent = run(
        project_back, [heads_own, heads_other], Weight(qkv_own, qkv_other)
    )
    first_came = over_core(first_sent)
    up_sum, up_near = z_near(up_total, up_far_came)
    up_near_came = over_z(up_near, 1)
    wait_for(up_near, down_near_came)
    own_kept = qkv_grad(heads_own, 0, 0)
    qkv_total = added(own_kept, own_y_came) + other_x_came.astype(f32)
    qkv_pieces = z_pieces(qkv_total)
    wait_for(*qkv_pieces)
    row_grad, first_sums = run(first_back, first_own, first_came, own_tokens, grad_middle, vectors)

    def to_devices(rows):
        return flipped(jnp.stack([rows[:block], over_x(rows[block:])]), x)

    tokens_grad = to_devices(row_grad)
    block_out = to_devices(block_own)

    def over_pair(total):
        pieces = total.reshape(2, 64, -1)
        rows = flipped(jnp.stack([one_of(pieces, x), over_x(one_of(pieces, 1 - x))]), x)
        return jnp.swapaxes(rows, 0, 1)

    def over_team(total):
        pieces = total.reshape((2, 32) + total.shape[1:])
        rows = flipped(jnp.stack([one_of(pieces, c), over_core(one_of(pieces, 1 - c))]), c)
        return jnp.swapaxes(rows, 0, 1)

    down_sum = added(down_sum, down_near_came)
    up_sum = over_team(over_pair(added(up_sum, up_near_came)))
    up_sum = up_sum.reshape(32, 2, 2, 8, 128).transpose(0, 3, 2, 1, 4).reshape(32, 4096)
    qkv_sum = over_team(over_pair(sum_z(qkv_total, qkv_pieces)))
    out_sum = qkv_sum[..., 768:].reshape(32, width)
    qkv_sum = qkv_sum[..., :768].reshape(32, 2, 2, 3, 4, 64)
    qkv_sum = jnp.transpose(qkv_sum, (0, 1, 2, 4, 3, 5)).reshape(32, 3 * width)

    sums = run(vector_sums, middle_sums, pre_sums, (sums_own, sums_other), first_sums)
    for step in (over_core, over_x, over_y, partial(over_z, k=1), partial(over_z, k=2)):
        sums = sums + step(sums)
    place = f * 4 + s
    pieces = lax.dynamic_slice(sums[:8], (0, place * 32), (8, 32))
    up_piece = lax.dynamic_slice(sums[8:].reshape(4096), (place * 128,), (128,))
    return (
        block_out,
        tokens_grad,
        pieces[4],
        pieces[5],
        qkv_sum,
        pieces[6:8],
        out_sum,
        pieces[2],
        pieces[0],
        pieces[1],
        up_sum,
        up_piece,
        down_sum,
        pieces[3],
    )


def local(tokens, *others):
    width = tokens.shape[2]
    shards = (lax.axis_size("fsdp"), lax.axis_size("seq"))
    hidden = others[10].shape[1]
    if tokens.shape[0] == 2 and tokens.shape[1] % 256 == 0 and shards == (8, 4) and tokens.shape[1] * 4 <= 1024 and (width, hidden) == (1024, 4096):
        return team_program(tokens, *others)
    return general_program(tokens, *others)


def solution(mesh):
    return jax.shard_map(
        local,
        mesh=mesh,
        in_specs=(
            P("fsdp", "seq", None),
            P("fsdp", "seq", None),
            P("fsdp"),
            P("fsdp"),
            P("fsdp"),
            P("fsdp", None),
            P(None, "fsdp"),
            P("fsdp", None),
            P("fsdp"),
            P("fsdp"),
            P("fsdp"),
            P("fsdp", None),
            P("fsdp"),
            P("fsdp", None),
            P("fsdp"),
        ),
        out_specs=(
            P("fsdp", "seq", None),
            P("fsdp", "seq", None),
            P(("fsdp", "seq")),
            P(("fsdp", "seq")),
            P(("fsdp", "seq"), None),
            P(None, ("fsdp", "seq")),
            P(("fsdp", "seq"), None),
            P(("fsdp", "seq")),
            P(("fsdp", "seq")),
            P(("fsdp", "seq")),
            P(("fsdp", "seq"), None),
            P(("fsdp", "seq")),
            P(("fsdp", "seq"), None),
            P(("fsdp", "seq")),
        ),
        check_vma=False,
    )
```

```python
from functools import partial
import math

import jax
import jax.numpy as jnp
from jax import lax
from jax.experimental import pallas as pl
from jax.experimental.pallas import tpu as pltpu
from jax.sharding import PartitionSpec as P

H = 16


epsilon = 1e-05
f32 = jnp.float32
bf16 = jnp.bfloat16


def layer_norm(values, norm_gain, norm_shift):
    row_mean = jnp.mean(values, axis=-1, keepdims=True)
    centered = values - row_mean
    variance = jnp.mean(centered * centered, axis=-1, keepdims=True)
    return centered * lax.rsqrt(variance + epsilon) * norm_gain + norm_shift


def product(left_side, right_side):
    return jnp.dot(left_side, right_side, preferred_element_type=f32)


def contract_rows(left_side, right_side):
    return lax.dot_general(
        left_side, right_side, (((0,), (0,)), ((), ())), preferred_element_type=f32
    )


def against(left_side, right_side):
    return lax.dot_general(
        left_side, right_side, (((1,), (1,)), ((), ())), preferred_element_type=f32
    )


def head_scores(query_block, key_rows, start_row, slopes, length, score_scale):
    block_size = query_block.shape[1]
    seq_len = key_rows.shape[1]
    row_index = start_row + jnp.arange(block_size)
    columns = jnp.arange(seq_len)
    products = jnp.einsum("hqd,hkd->hqk", query_block, key_rows, preferred_element_type=f32)
    distance = (columns[None, :] - row_index[:, None]).astype(f32)
    allowed = (columns[None, :] <= row_index[:, None]) & (columns[None, :] < length)
    return jnp.where(
        allowed[None], products * score_scale + slopes[:, None, None] * distance, -jnp.inf
    )


def attend(queries, key_rows, value_rows, length, slopes, score_scale):
    head_count, seq_len, head_size = queries.shape
    block_size = math.gcd(512, seq_len)

    def one_block(start_row):
        query_block = lax.dynamic_slice_in_dim(queries, start_row, block_size, 1)
        scores = head_scores(query_block, key_rows, start_row, slopes, length, score_scale)
        largest = jnp.max(scores, axis=-1, keepdims=True)
        log_total = largest + jnp.log(jnp.sum(jnp.exp(scores - largest), axis=-1, keepdims=True))
        attention_probs = jnp.exp(scores - log_total).astype(bf16)
        mixed_rows = jnp.einsum(
            "hqk,hkd->hqd", attention_probs, value_rows, preferred_element_type=f32
        )
        return (mixed_rows.astype(bf16), log_total[..., 0])

    starts = jnp.arange(seq_len // block_size, dtype=jnp.int32) * block_size
    mixed_rows, log_totals = lax.map(one_block, starts)
    return (
        jnp.moveaxis(mixed_rows, 0, 1).reshape(head_count, seq_len, head_size),
        jnp.moveaxis(log_totals, 0, 1).reshape(head_count, seq_len),
    )


def attend_back(queries, key_rows, value_rows, grad_mixed, log_totals, length, slopes, score_scale):
    head_count, seq_len, head_size = queries.shape
    block_size = math.gcd(512, seq_len)

    def one_block(carried, start_row):
        key_sum, value_sum = carried
        query_block = lax.dynamic_slice_in_dim(queries, start_row, block_size, 1)
        grad_block = lax.dynamic_slice_in_dim(grad_mixed, start_row, block_size, 1)
        total_block = lax.dynamic_slice_in_dim(log_totals, start_row, block_size, 1)
        scores = head_scores(query_block, key_rows, start_row, slopes, length, score_scale)
        attention_probs = jnp.exp(scores - total_block[..., None])
        grad_probs = jnp.einsum(
            "hqd,hkd->hqk", grad_block, value_rows, preferred_element_type=f32
        )
        row_inner = jnp.sum(attention_probs * grad_probs, axis=-1, keepdims=True)
        grad_scores = (attention_probs * (grad_probs - row_inner)).astype(bf16)
        query_grad = (
            jnp.einsum("hqk,hkd->hqd", grad_scores, key_rows, preferred_element_type=f32)
            * score_scale
        ).astype(bf16)
        key_sum = (
            key_sum
            + jnp.einsum("hqk,hqd->hkd", grad_scores, query_block, preferred_element_type=f32)
            * score_scale
        )
        value_sum = value_sum + jnp.einsum(
            "hqk,hqd->hkd",
            attention_probs.astype(bf16),
            grad_block,
            preferred_element_type=f32,
        )
        return ((key_sum, value_sum), query_grad)

    starts = jnp.arange(seq_len // block_size, dtype=jnp.int32) * block_size
    empty = jnp.zeros(queries.shape, f32)
    (key_sum, value_sum), query_grads = lax.scan(one_block, (empty, empty), starts)
    query_grad = jnp.moveaxis(query_grads, 0, 1).reshape(head_count, seq_len, head_size)
    return (query_grad, key_sum.astype(bf16), value_sum.astype(bf16))


ACROSS = ((1,), (1,))
PLAIN = ((1,), (0,))
DOWN = ((0,), (0,))

def mm(left_side, right_side, dims):
    return lax.dot_general(left_side, right_side, (dims, ((), ())), preferred_element_type=f32)


def set_bias(length, head, su):
    rows = su.shape[1]
    u = lax.broadcasted_iota(jnp.int32, (rows, 128), 0)
    for h in range(2):
        power = jnp.full((rows, 128), head + (h + 1), jnp.int32).astype(f32)
        slope = jnp.exp2(power * (-8.0 / H))
        su[h] = jnp.where(u < length, u.astype(f32) * slope, -jnp.inf)


def half(value, h):
    lane = lax.broadcasted_iota(jnp.int32, value.shape, 1)
    return jnp.where((lane // 64) == h, value, jnp.zeros_like(value))


def scores(k_ref, q, h, su, nk, block):
    st = mm(k_ref[:nk], half(q, h) * jnp.asarray(0.125, bf16), ACROSS)
    st = st + jnp.concatenate([su[h, :nk]] * (block // 128), axis=1)
    keep = lax.broadcasted_iota(jnp.int32, (block, block), 0) <= lax.broadcasted_iota(
        jnp.int32, (block, block), 1
    )
    tail = jnp.where(keep, st[nk - block :], -jnp.inf)
    return tail if nk == block else jnp.concatenate([st[: nk - block], tail], axis=0)


def exchange(value, axis, bit):
    return lax.ppermute(value, axis, [(i, i ^ bit) for i in range(lax.axis_size(axis))])


def is_set(axis, bit):
    return (lax.axis_index(axis) // bit) % 2


def place(bit):
    return (0 if bit[0] == "fsdp" else 1, -bit[1])


def powers(size):
    return [1 << i for i in range(size.bit_length() - 1)]


def gather_bits(unit, order):
    held, buffer = [], unit
    for bit in order:
        received = exchange(buffer, *bit)
        second = is_set(*bit) == 1
        at = sum(1 for other in held if place(other) < place(bit))
        buffer = jnp.stack(
            [jnp.where(second, received, buffer), jnp.where(second, buffer, received)], axis=at
        )
        held.append(bit)
    return buffer


def scatter_bits(partial_sum, held, order):
    held, buffer = list(held), partial_sum
    for bit in order:
        at, mine = held.index(bit), is_set(*bit)
        sent = lax.dynamic_index_in_dim(buffer, 1 - mine, at, keepdims=False).astype(bf16)
        kept = lax.dynamic_index_in_dim(buffer, mine, at, keepdims=False).astype(f32)
        buffer = kept + exchange(sent, *bit).astype(f32)
        held.remove(bit)
    return buffer


def in_order(pieces, own):
    pieces = list(pieces)
    for bit in powers(len(pieces)):
        second = (own // bit) % 2 == 1
        pieces = [
            jnp.where(second, pieces[i ^ bit], pieces[i]) for i in range(len(pieces))
        ]
    return pieces


class Team:
    def __init__(self, micro_count):
        self.shards = lax.axis_size("seq")
        self.size = self.shards // micro_count
        self.micro_count = micro_count
        self.member = lax.axis_index("seq") % self.size
        self.which = lax.axis_index("seq") // self.size
        self.team_bits = [("seq", bit) for bit in powers(self.size)]
        self.pair_bits = [("seq", self.size * bit) for bit in powers(micro_count)]

    def to_sequences(self, pieces):
        arrived = []
        for offset in range(self.micro_count):
            sent = lax.dynamic_index_in_dim(pieces, self.which ^ offset, 0, keepdims=False)
            arrived.append(sent if offset == 0 else exchange(sent, "seq", offset * self.size))
        return jnp.stack(in_order(arrived, self.which))

    def share(self, own):
        arrived = [own if e == 0 else exchange(own, "seq", e) for e in range(self.size)]
        return jnp.stack(in_order(arrived, self.member), axis=1)

    def swap(self, pieces, axis, onto):
        arrived = []
        for e in range(self.size):
            sent = lax.dynamic_index_in_dim(pieces, self.member ^ e, axis, keepdims=False)
            arrived.append(sent if e == 0 else exchange(sent, "seq", e))
        return jnp.stack(in_order(arrived, self.member), axis=onto)

    def reduce(self, partial_sum):
        total = lax.dynamic_index_in_dim(partial_sum, self.member, 1, keepdims=False)
        for e in range(1, self.size):
            sent = lax.dynamic_index_in_dim(partial_sum, self.member ^ e, 1, keepdims=False)
            total = total + exchange(sent.astype(bf16), "seq", e).astype(f32)
        return total


def general_program(
    tokens,
    cotangent,
    lengths,
    first_gain,
    first_shift,
    qkv_weight,
    qv_bias,
    out_weight,
    out_bias,
    second_gain,
    second_shift,
    up_weight,
    up_bias,
    down_weight,
    down_bias,
):
    micro_count, block_rows, width = tokens.shape
    team = Team(micro_count)
    size, member, which = team.size, team.member, team.which
    shards = team.shards
    fsdp_shards = lax.axis_size("fsdp")
    seq_len = block_rows * shards
    head_size = width // H
    own_heads = H // size
    own_width = own_heads * head_size
    hidden = up_weight.shape[1]
    own_hidden = hidden // size
    fsdp_bits = [("fsdp", bit) for bit in powers(fsdp_shards)]
    line_bits = fsdp_bits[1:] + fsdp_bits[:1]
    pair_bits, team_bits = team.pair_bits, team.team_bits
    rows_first = lambda bits: sorted(bits, key=place)
    split = lambda bits: (2,) * len(bits)

    packed = jnp.concatenate(
        [
            first_gain,
            first_shift,
            second_gain,
            second_shift,
            out_bias,
            down_bias,
            qv_bias[0],
            qv_bias[1],
            up_bias,
        ]
    )
    packed = gather_bits(packed, line_bits).reshape(fsdp_shards, -1).astype(f32)
    part = width // fsdp_shards
    vectors = [packed[:, i * part : (i + 1) * part].reshape(width) for i in range(8)]
    gain_one, shift_one, gain_two, shift_two, bias_out, bias_down, bias_q, bias_v = vectors
    bias_up = packed[:, 8 * part :].reshape(hidden // (size * (hidden // (fsdp_shards * shards))), size, -1)
    bias_up = lax.dynamic_index_in_dim(bias_up, member, 1, keepdims=False).reshape(own_hidden)

    def part_rows(weight, bits, parts_of):
        rows = weight.shape[0] // parts_of
        index = jnp.int32(0)
        for bit in rows_first(bits):
            index = index * 2 + is_set(*bit)
        return lax.dynamic_slice_in_dim(weight, index * rows, rows, 0)

    qkv_own = lax.dynamic_slice_in_dim(qkv_weight, member * 3 * own_width, 3 * own_width, 1)
    qkv_own = jnp.swapaxes(qkv_own.reshape(-1, own_heads, 3, head_size), 1, 2).reshape(-1, 3 * own_width)
    whole_qkv = gather_bits(
        part_rows(qkv_own, pair_bits, micro_count), line_bits + pair_bits
    ).reshape(width, 3 * own_width)
    whole_out = gather_bits(
        part_rows(out_weight, pair_bits + team_bits, shards), line_bits + pair_bits + team_bits
    ).reshape(width, width)
    unit = hidden // (fsdp_shards * shards)
    up_own = lax.dynamic_index_in_dim(
        up_weight.reshape(width // fsdp_shards, hidden // (size * unit), size, unit),
        member,
        2,
        keepdims=False,
    ).reshape(width // fsdp_shards, own_hidden)
    whole_up = gather_bits(up_own, line_bits).reshape(width, own_hidden)
    down_own = lax.dynamic_index_in_dim(
        down_weight.reshape(micro_count, size, unit, width), member, 1, keepdims=False
    ).reshape(micro_count * unit, width)
    whole_down = gather_bits(
        part_rows(down_own, pair_bits, micro_count), line_bits + pair_bits
    ).reshape(own_hidden, width)

    length = lax.dynamic_index_in_dim(lengths, which, 0, keepdims=False)
    own_tokens = team.to_sequences(tokens)
    all_tokens = team.share(own_tokens).reshape(seq_len, width).astype(f32)
    own_rows = micro_count * block_rows
    own_tokens = own_tokens.reshape(own_rows, width).astype(f32)
    own_positions = (
        (jnp.arange(micro_count)[:, None] * size + member) * block_rows
        + jnp.arange(block_rows)[None, :]
    ).reshape(own_rows)
    valid_mask = (own_positions < length).astype(f32)[:, None]
    slopes = jnp.exp2(-((member * own_heads + jnp.arange(own_heads)).astype(f32) + 1.0) * 8.0 / H)
    score_scale = head_size ** (-0.5)

    by_member = (micro_count, size, block_rows)

    normed = layer_norm(all_tokens, gain_one, shift_one).astype(bf16)
    own_bias = lambda vector: lax.dynamic_slice_in_dim(vector, member * own_width, own_width, 0)
    bias_columns = jnp.concatenate([own_bias(bias_q), jnp.zeros((own_width,), f32), own_bias(bias_v)])
    projected = (product(normed, whole_qkv) + bias_columns).astype(bf16)
    split_heads = lambda value: jnp.moveaxis(value.reshape(seq_len, -1, head_size), 1, 0)
    join_heads = lambda value: jnp.moveaxis(value, 0, 1).reshape(seq_len, -1)
    queries, key_rows, value_rows = [
        split_heads(projected[:, i * own_width : (i + 1) * own_width]) for i in range(3)
    ]
    mixed, log_totals = attend(queries, key_rows, value_rows, length, slopes, score_scale)
    mixed = join_heads(mixed)
    mixed_rows = team.swap(mixed.reshape(by_member + (own_width,)), 1, 2).reshape(own_rows, width)
    middle = own_tokens + (product(mixed_rows, whole_out) + bias_out)
    normed_two_own = layer_norm(middle, gain_two, shift_two).astype(bf16)
    normed_two = team.share(normed_two_own.reshape(micro_count, block_rows, width)).reshape(
        seq_len, width
    )
    hidden_pre = product(normed_two, whole_up) + bias_up
    activation = jax.nn.gelu(hidden_pre, approximate=True).astype(bf16)
    fed = team.reduce(product(activation, whole_down).reshape(by_member + (width,)))
    block_own = (valid_mask * (middle + fed.reshape(own_rows, width) + bias_down)).astype(bf16)
    block_out = team.to_sequences(block_own.reshape(micro_count, block_rows, width))

    own_grad = team.to_sequences(cotangent)
    own_grad = jnp.where(
        (valid_mask > 0).reshape(micro_count, block_rows, 1), own_grad, jnp.zeros_like(own_grad)
    )
    grad_low = team.share(own_grad).reshape(seq_len, width)
    grad_out = own_grad.reshape(own_rows, width).astype(f32)
    down_bias_grad = jnp.sum(grad_out, axis=0)
    down_grad = contract_rows(activation, grad_low)
    grad_act = against(grad_low, whole_down)
    gelu_pull = jax.vjp(partial(jax.nn.gelu, approximate=True), hidden_pre)[1]
    grad_pre = gelu_pull(grad_act)[0].astype(bf16)
    up_grad = contract_rows(normed_two, grad_pre)
    up_bias_grad = jnp.sum(grad_pre.astype(f32), axis=0)
    grad_normed_two = team.reduce(
        against(grad_pre, whole_up).reshape(by_member + (width,))
    ).reshape(own_rows, width)
    norm_pull = jax.vjp(layer_norm, middle, gain_two, shift_two)[1]
    middle_part, second_gain_grad, second_shift_grad = norm_pull(grad_normed_two)
    grad_middle = grad_out + middle_part
    grad_branch = grad_middle.astype(bf16)
    out_bias_grad = jnp.sum(grad_branch.astype(f32), axis=0)
    out_grad = contract_rows(mixed_rows, grad_branch)
    grad_mixed_own = against(grad_branch, whole_out).astype(bf16)
    grad_mixed = team.swap(
        grad_mixed_own.reshape(micro_count, block_rows, size, own_width), 2, 1
    ).reshape(seq_len, own_width)
    backs = attend_back(
        queries,
        key_rows,
        value_rows,
        split_heads(grad_mixed),
        log_totals,
        length,
        slopes,
        score_scale,
    )
    grad_qkv = jnp.concatenate([join_heads(back) for back in backs], axis=1)
    qkv_grad = contract_rows(normed, grad_qkv)
    column_sums = jnp.sum(grad_qkv.astype(f32), axis=0).reshape(3, own_width)
    grad_normed = team.reduce(
        against(grad_qkv, whole_qkv).reshape(by_member + (width,))
    ).reshape(own_rows, width)
    first_pull = jax.vjp(layer_norm, own_tokens, gain_one, shift_one)[1]
    token_part, first_gain_grad, first_shift_grad = first_pull(grad_normed)
    row_grad = (grad_middle + token_part).astype(bf16)
    tokens_grad = team.to_sequences(row_grad.reshape(micro_count, block_rows, width))

    row_bits = rows_first(fsdp_bits + pair_bits)
    pair_first = pair_bits + fsdp_bits[:1] + fsdp_bits[:0:-1]
    pair_second = fsdp_bits[:1] + pair_bits + fsdp_bits[:0:-1]
    down_sum = scatter_bits(
        down_grad.reshape(split(row_bits) + (unit, width)), row_bits, pair_first
    )

    def by_columns(grad, order):
        total = scatter_bits(
            grad.reshape(split(row_bits) + (size, -1) + grad.shape[1:]), row_bits, order
        )
        return team.swap(total, 0, 1)

    up_sum = by_columns(up_grad, pair_second)
    up_sum = jnp.swapaxes(up_sum.reshape(-1, size, hidden // (size * unit), unit), 1, 2)
    up_sum = up_sum.reshape(-1, hidden)
    qkv_sum = by_columns(qkv_grad, pair_first).reshape(-1, size, 3, own_heads, head_size)
    qkv_sum = jnp.swapaxes(qkv_sum, 2, 3).reshape(-1, 3 * width)
    all_bits = rows_first(fsdp_bits + pair_bits + team_bits)
    out_sum = scatter_bits(
        out_grad.reshape(split(all_bits) + (-1, width)), all_bits, team_bits[::-1] + pair_first
    )

    devices = fsdp_shards * shards

    def spread(own, count):
        at_member = jnp.arange(size).reshape(1, size, 1) == member
        return jnp.where(at_member, own.reshape(count, 1, -1), 0.0)

    up_vector = spread(up_bias_grad, hidden // (size * unit)).reshape(devices, unit)
    by_team = lambda own: spread(own.reshape(1, own_width), 1).reshape(width)
    vectors = [
        first_gain_grad,
        first_shift_grad,
        second_gain_grad,
        second_shift_grad,
        out_bias_grad,
        down_bias_grad,
        by_team(column_sums[0]),
        by_team(column_sums[2]),
    ]
    buffer = jnp.concatenate([v.reshape(devices, -1) for v in vectors] + [up_vector], axis=1)
    buffer = buffer.reshape(split(all_bits) + (-1,))
    held = list(all_bits)
    for bit in team_bits + pair_first:
        at, mine = held.index(bit), is_set(*bit)
        sent = lax.dynamic_index_in_dim(buffer, 1 - mine, at, keepdims=False)
        kept = lax.dynamic_index_in_dim(buffer, mine, at, keepdims=False)
        buffer = kept + exchange(sent, *bit)
        held.remove(bit)
    each = width // devices
    sums = [buffer[i * each : (i + 1) * each] for i in range(8)]
    return (
        block_out,
        tokens_grad,
        sums[0],
        sums[1],
        qkv_sum,
        jnp.stack([sums[6], sums[7]]),
        out_sum,
        sums[4],
        sums[2],
        sums[3],
        up_sum,
        buffer[8 * each :],
        down_sum,
        sums[5],
    )


WORK = pl.CostEstimate(flops=10000000000, bytes_accessed=20000000, transcendentals=0)


def whole_block(array):
    return pl.BlockSpec(array.shape, lambda *_: (0,) * array.ndim, pipeline_mode=pl.Buffered(1))


def lanes(ref, block):
    return ref[:, pl.ds(pl.multiple_of(block * 128, 128), 128)]


def member_of(order):
    return order[1] & 1


def pair_of(order):
    return order[1] >> 1


def owner(order, i):
    return order[0] ^ ((i & 3) * 2 + (i >> 2))


def mixed_block(order, i):
    return owner(order, i) ^ (member_of(order) * 4 + pair_of(order) * 2)


def natural(order, i):
    return i


def picked(ref, order, first, block_of=owner):
    return jnp.concatenate([lanes(ref, block_of(order, first + i)) for i in range(4)], axis=1)


def flat(ref, start):
    value = ref[start : start + 4, :128]
    return value.reshape(512, value.shape[-1])


class Weight:
    def __init__(self, *parts, orders=None):
        self.parts = parts
        self.orders = orders or [owner] * len(parts)

    def slabs(self):
        found = []
        for pair in self.parts:
            for array, _, columns, which in pair:
                if not any(array is a and (columns, which) == b for a, b in found):
                    found.append((array, (columns, which)))
        return found

    def inputs(self):
        result = []
        for array, (columns, which) in self.slabs():
            spec = pl.BlockSpec(
                array.shape[:2] + (columns,),
                lambda *_, which=which: (0, 0, which),
                pipeline_mode=pl.Buffered(1),
            )
            result.append((array, spec))
        return result

    def tiles(self, columns=0, blocks=0):
        result = []
        for pair in self.parts:
            for array, first, wide, which in pair:
                if columns:
                    shape = (4, 128, columns)
                    place = lambda j, *_, f=first, w=which * (wide // columns): (f // 4, 0, w + j)
                else:
                    shape = (blocks, 128, wide)
                    place = lambda j, *_, f=first, w=which: (f // blocks + j, 0, w)
                result.append((array, pl.BlockSpec(shape, place)))
        return result

    def views(self, refs):
        slabs = self.slabs()

        def find(view):
            array, first, columns, which = view
            at = [array is a and (columns, which) == b for a, b in slabs].index(True)
            return refs[at], first

        return [(find(pair[0]), find(pair[1])) for pair in self.parts]


def grid_call(name, kernel, order, grid, inputs, outputs, scratch=(), limit=24):
    return pl.pallas_call(
        kernel,
        name=name,
        grid_spec=pltpu.PrefetchScalarGridSpec(
            num_scalar_prefetch=1,
            grid=grid,
            in_specs=[spec for _, spec in inputs],
            out_specs=[spec for _, spec in outputs],
            scratch_shapes=list(scratch),
        ),
        out_shape=[shape for shape, _ in outputs],
        compiler_params=pltpu.CompilerParams(vmem_limit_bytes=limit << 20),
        cost_estimate=WORK,
    )(order, *[a for a, _ in inputs])


def shape_of(shape, dtype):
    return jax.ShapeDtypeStruct(shape, dtype)


def normalized(values):
    row_mean = jnp.mean(values, axis=-1, keepdims=True)
    centered = values - row_mean
    rstd = lax.rsqrt(jnp.mean(centered * centered, axis=-1, keepdims=True) + epsilon)
    return centered * rstd, rstd


def first_norm(order, tokens, came, other_mine, other_came, vectors):
    _, block, width = tokens.shape

    def kernel(order, mine_ref, came_ref, other_mine_ref, other_came_ref, vec_ref, out_ref):
        def write(ref):
            xhat, _ = normalized(ref[...].astype(f32))
            out_ref[...] = (xhat * vec_ref[0:1] + vec_ref[1:2]).astype(bf16)

        at = pl.program_id(0)
        for i, ref in enumerate((mine_ref.at[0], came_ref, other_mine_ref, other_came_ref)):
            pl.when(at == i)(partial(write, ref))

    def place(i, o):
        return (((i % 2) ^ pair_of(o)) * 2 + ((i // 2) ^ member_of(o)), 0)

    return grid_call(
        "first_norm",
        kernel,
        order,
        (4,),
        [(tokens, pl.BlockSpec((1, block, width), lambda i, o: (pair_of(o), 0, 0)))]
        + [(a, whole_block(a)) for a in (came, other_mine, other_came, vectors)],
        [(shape_of((4 * block, width), bf16), pl.BlockSpec((block, width), place))],
    )[0]


def matrix(ref):
    value = ref[...]
    return value.reshape(value.shape[0] * value.shape[1], value.shape[2])


def project(order, normed, bias, part, weight, tile=256):
    rows, width = normed.shape
    columns = bias.shape[1]

    def kernel(order, lhs_ref, bias_ref, first_ref, second_ref, out_ref):
        total = mm(picked(lhs_ref, order, 0), matrix(first_ref), PLAIN)
        total = total + mm(picked(lhs_ref, order, 4), matrix(second_ref), PLAIN)
        out_ref[...] = (total + bias_ref[part : part + 1]).astype(bf16)

    return grid_call(
        "project",
        kernel,
        order,
        (columns // tile,),
        [(normed, whole_block(normed)), (bias, pl.BlockSpec((2, tile), lambda j, o: (0, j)))]
        + weight.tiles(columns=tile),
        [(shape_of((rows, columns), bf16), pl.BlockSpec((rows, tile), lambda j, o: (0, j)))],
    )[0]


def out_and_norm(order, mixed, tokens, vectors, weight, block=256):
    rows, width = mixed.shape

    def kernel(order, lhs_ref, tok_ref, vec_ref, *rest):
        middle_ref, norm_ref = rest[-2:]
        left = [picked(lhs_ref, order, i, mixed_block) for i in (0, 4)]
        for at, views in enumerate(weight.views(rest[:-2])):
            total = sum(mm(l, flat(*view), PLAIN) for l, view in zip(left, views))
            start = pl.multiple_of((member_of(order) ^ at) * (width // 2), 128)
            middle_ref[:, pl.ds(start, width // 2)] = total
        middle = tok_ref[...].astype(f32) + (middle_ref[...] + vec_ref[4:5])
        middle_ref[...] = middle
        xhat, _ = normalized(middle)
        norm_ref[...] = (xhat * vec_ref[2:3] + vec_ref[3:4]).astype(bf16)

    row = pl.BlockSpec((block, width), lambda i, o: (i, 0))
    return grid_call(
        "out_and_norm",
        kernel,
        order,
        (rows // block,),
        [(mixed, row), (tokens, row)]
        + [(vectors, whole_block(vectors))]
        + weight.inputs(),
        [(shape_of((rows, width), f32), row), (shape_of((rows, width), bf16), row)],
    )


ROOT = math.sqrt(2.0 / math.pi)


def gelu_and_slope(z):
    inner = jnp.tanh(ROOT * (z + 0.044715 * (z * z * z)))
    half_up = 0.5 * (1.0 + inner)
    slope = half_up + 0.5 * z * (1.0 - inner * inner) * (ROOT * (1.0 + 3 * 0.044715 * (z * z)))
    return z * half_up, slope


def feed_up(order, normed, bias, part, weight, tile=256):
    rows, width = normed.shape
    columns = bias.shape[1]

    def kernel(order, lhs_ref, bias_ref, first_ref, second_ref, act_ref, slope_ref):
        total = mm(picked(lhs_ref, order, 0), matrix(first_ref), PLAIN)
        total = total + mm(picked(lhs_ref, order, 4), matrix(second_ref), PLAIN)
        act, slope = gelu_and_slope(total + bias_ref[part : part + 1])
        act_ref[...] = act.astype(bf16)
        slope_ref[...] = slope.astype(bf16)

    out = pl.BlockSpec((rows, tile), lambda j, o: (0, j))
    return grid_call(
        "feed_up",
        kernel,
        order,
        (columns // tile,),
        [(normed, whole_block(normed)), (bias, pl.BlockSpec((2, tile), lambda j, o: (0, j)))]
        + weight.tiles(columns=tile),
        [(shape_of((rows, columns), bf16), out)] * 2,
    )


def own_and_sent(rows, width, tile):
    place = (lambda j, h, o: (0, j)) if tile < width else (lambda j, h, o: (0, 0))
    spec = pl.BlockSpec((rows, tile), place)
    return [(shape_of((rows, width), f32), spec), (shape_of((rows, width), bf16), spec)]


def half_rows(ref):
    rows = ref.shape[0] // 2
    return pl.ds(pl.multiple_of(pl.program_id(1) * rows, rows), rows)


def keep_or_send(own_ref, sent_ref, values):
    def save(ref):
        for where, value in values:
            ref[where] = value.astype(ref.dtype)

    pl.when(pl.program_id(1) == 0)(partial(save, own_ref))
    pl.when(pl.program_id(1) == 1)(partial(save, sent_ref))


def spread(order, totals):
    found = []
    for half, total in enumerate(totals):
        for k in range(2):
            block = owner(order, 4 * half + 2 * pl.program_id(0) + k)
            here = pl.ds(pl.multiple_of(block * 128, 128), 128)
            found.append(((slice(None), here), total[:, 128 * k : 128 * (k + 1)]))
    return found


def feed_down(order, acts, weight, tile=256):
    rows, columns = acts[0].shape
    width = 1024

    def kernel(order, first_act, second_act, *rest):
        weights, own_ref, sent_ref = rest[:4], rest[4], rest[5]
        here = half_rows(first_act)
        total = 0.0
        for part, act_ref in enumerate((first_act, second_act)):
            for half in range(2):
                left = picked(act_ref.at[here], order, 4 * half)
                total = total + mm(left, matrix(weights[2 * part + half]), PLAIN)
        keep_or_send(own_ref, sent_ref, [(Ellipsis, total)])

    return grid_call(
        "feed_down",
        kernel,
        order,
        (width // tile, 2),
        [(act, whole_block(act)) for act in acts] + weight.tiles(columns=tile),
        own_and_sent(rows // 2, width, tile),
    )


def feed_down_back(order, grad, slope, weight):
    rows, width = grad.shape
    columns = slope.shape[1]

    def kernel(order, lhs_ref, slope_ref, first_ref, second_ref, out_ref, sum_ref):
        @pl.when((pl.program_id(0) == 0) & (pl.program_id(1) == 0))
        def _():
            sum_ref[...] = jnp.zeros_like(sum_ref)

        here = half_rows(lhs_ref)
        left = lhs_ref[here]
        totals = [mm(left, matrix(ref), ACROSS) for ref in (first_ref, second_ref)]
        for (_, place), total in spread(order, totals):
            low = (total * slope_ref[here, place].astype(f32)).astype(bf16)
            out_ref[here, place] = low
            sum_ref[:, place] += rows_of_eight(low.astype(f32))

    return grid_call(
        "feed_down_back",
        kernel,
        order,
        (2, 2),
        [(grad, whole_block(grad)), (slope, whole_block(slope))] + weight.tiles(blocks=2),
        [
            (shape_of((rows, columns), bf16), pl.BlockSpec((rows, columns), lambda i, h, o: (0, 0))),
            (shape_of((8, columns), f32), pl.BlockSpec((8, columns), lambda i, h, o: (0, 0))),
        ],
    )


def feed_up_back(order, grads, weight):
    rows, columns = grads[0].shape
    width = 1024

    def kernel(order, first_grad, second_grad, *rest):
        weights, own_ref, sent_ref = rest[:4], rest[4], rest[5]
        here = half_rows(first_grad)
        totals = [
            mm(first_grad[here], matrix(weights[half]), ACROSS)
            + mm(second_grad[here], matrix(weights[2 + half]), ACROSS)
            for half in range(2)
        ]
        keep_or_send(own_ref, sent_ref, spread(order, totals))

    return grid_call(
        "feed_up_back",
        kernel,
        order,
        (2, 2),
        [(grad, whole_block(grad)) for grad in grads] + weight.tiles(blocks=2),
        own_and_sent(rows // 2, width, width),
    )


def rows_of_eight(value):
    return jnp.sum(value.reshape(value.shape[0] // 8, 8, value.shape[1]), axis=0)


def norm_back(xhat, rstd, grad_norm, gain):
    scaled = grad_norm * gain
    return rstd * (
        scaled
        - jnp.mean(scaled, axis=-1, keepdims=True)
        - xhat * jnp.mean(scaled * xhat, axis=-1, keepdims=True)
    )


def middle_back(order, own, came, middle, grad_out, vectors, weight, block=256):
    rows, width = middle.shape
    half_width = width // 2

    def kernel(order, own_ref, came_ref, middle_ref, dy_ref, vec_ref, *rest):
        grad_ref, branch_ref, keep_ref, sent_ref, sum_ref, tmp, low_ref = rest[-7:]

        @pl.when(pl.program_id(0) == 0)
        def _():
            sum_ref[...] = jnp.zeros_like(sum_ref)

        grad_norm = own_ref[...] + came_ref[...].astype(f32)
        xhat, rstd = normalized(middle_ref[...])
        grad_out = dy_ref[...].astype(f32)
        grad_middle = grad_out + norm_back(xhat, rstd, grad_norm, vec_ref[2:3])
        grad_ref[...] = grad_middle
        low = grad_middle.astype(bf16)
        low_ref[...] = low
        sum_ref[0] += rows_of_eight(grad_norm * xhat)
        sum_ref[1] += rows_of_eight(grad_norm)
        sum_ref[2] += rows_of_eight(low.astype(f32))
        sum_ref[3] += rows_of_eight(grad_out)
        views = weight.views(rest[:-7])
        member = member_of(order)
        for i in range(4):
            from_ = i ^ (member * 2 + pair_of(order))
            branch_ref[:, 256 * i : 256 * i + 256] = low_ref[:, pl.ds(pl.multiple_of(from_ * 256, 128), 256)]
        for half in range(2):
            total = 0.0
            for at, pair in enumerate(views):
                start = pl.multiple_of((member ^ at) * half_width, 128)
                total = total + mm(low_ref[:, pl.ds(start, half_width)], flat(*pair[half]), ACROSS)
            for k in range(4):
                here = pl.ds(pl.multiple_of(mixed_block(order, 4 * half + k) * 128, 128), 128)
                tmp[:, here] = total[:, 128 * k : 128 * (k + 1)].astype(bf16)
        keep_ref[...] = tmp[:, :half_width]
        sent_ref[...] = tmp[:, half_width:]

    row = pl.BlockSpec((block, width), lambda i, o: (i, 0))
    part = pl.BlockSpec((block, half_width), lambda i, o: (i, 0))
    return grid_call(
        "middle_back",
        kernel,
        order,
        (rows // block,),
        [(own, row), (came, row), (middle, row), (grad_out, row), (vectors, whole_block(vectors))]
        + weight.inputs(),
        [
            (shape_of((rows, width), f32), row),
            (shape_of((rows, width), bf16), row),
            (shape_of((rows, half_width), bf16), part),
            (shape_of((rows, half_width), bf16), part),
            (shape_of((4, 8, width), f32), pl.BlockSpec((4, 8, width), lambda i, o: (0, 0, 0))),
        ],
        scratch=[pltpu.VMEM((block, width), bf16)] * 2,
    )


def project_back(order, grads, weight):
    rows = grads[0][0].shape[0]
    block = rows // 4
    width = 1024
    given = [g for half in grads for g in half]

    def kernel(order, *rest):
        weights, own_ref, sent_ref = rest[6:10], rest[10], rest[11]

        def left(part):
            found = []
            for k in range(2):
                at = (k ^ pair_of(order)) * 2 + (pl.program_id(1) ^ member_of(order))
                here = pl.ds(pl.multiple_of(at * block, block), block)
                found.append(
                    jnp.concatenate([r[here] for r in rest[3 * part : 3 * part + 3]], axis=1)
                )
            return jnp.concatenate(found)

        lefts = [left(0), left(1)]
        totals = [
            mm(lefts[0], matrix(weights[half]), ACROSS)
            + mm(lefts[1], matrix(weights[2 + half]), ACROSS)
            for half in range(2)
        ]
        keep_or_send(own_ref, sent_ref, spread(order, totals))

    return grid_call(
        "project_back",
        kernel,
        order,
        (2, 2),
        [(g, whole_block(g)) for g in given] + weight.tiles(blocks=2),
        own_and_sent(rows // 2, width, width),
    )


def first_back(order, own, came, tokens, grad_middle, vectors, block=256):
    rows, width = own.shape

    def kernel(order, own_ref, came_ref, tok_ref, mid_ref, vec_ref, out_ref, sum_ref):
        @pl.when(pl.program_id(0) == 0)
        def _():
            sum_ref[...] = jnp.zeros_like(sum_ref)

        grad_norm = own_ref[...] + came_ref[...].astype(f32)
        xhat, rstd = normalized(tok_ref[...].astype(f32))
        total = mid_ref[...] + norm_back(xhat, rstd, grad_norm, vec_ref[0:1])
        out_ref[...] = total.astype(bf16)
        sum_ref[0] += rows_of_eight(grad_norm * xhat)
        sum_ref[1] += rows_of_eight(grad_norm)

    row = pl.BlockSpec((block, width), lambda i, o: (i, 0))
    return grid_call(
        "first_back",
        kernel,
        order,
        (rows // block,),
        [(own, row), (came, row), (tokens, row), (grad_middle, row), (vectors, whole_block(vectors))],
        [
            (shape_of((rows, width), bf16), row),
            (shape_of((2, 8, width), f32), pl.BlockSpec((2, 8, width), lambda i, o: (0, 0, 0))),
        ],
    )


def weight_grad(order, first, count, left, rights, block_of=owner, extra=None):
    wide = sum(columns for _, columns, _ in rights)
    extra = extra or ()
    more = extra[0].shape[2] if extra else 0
    together = 4

    def kernel(order, left_ref, *rest):
        right_refs, out_ref = rest[: len(rights)], rest[-1]
        at = first + together * pl.program_id(0)
        lefts = [lanes(left_ref, block_of(order, at + k)) for k in range(together)]
        picked_left = jnp.concatenate(lefts, axis=1)
        start = 0
        for ref in right_refs:
            total = mm(picked_left, ref[...], DOWN)
            width = total.shape[1]
            out_ref[:, :, start : start + width] = total.reshape(together, 128, width).astype(bf16)
            start += width
        if extra:
            kept, came = rest[len(rights) : -1]
            out_ref[:, :, start:] = (kept[...].astype(f32) + came[...].astype(f32)).astype(bf16)

    def right_spec(array, columns, which):
        return pl.BlockSpec(
            (array.shape[0], columns), lambda *_: (0, which), pipeline_mode=pl.Buffered(1)
        )

    def extra_spec(array, which):
        return pl.BlockSpec(
            (together, 128, more // 2), lambda i, o: (first // together + i, 0, which)
        )

    return grid_call(
        "weight_grad",
        kernel,
        order,
        (count // together,),
        [(left, whole_block(left))]
        + [(right[0], right_spec(*right)) for right in rights]
        + [(a, extra_spec(a, extra[2])) for a in extra[:2]],
        [
            (
                shape_of((count, 128, wide + more // 2), bf16),
                pl.BlockSpec((together, 128, wide + more // 2), lambda i, o: (i, 0, 0)),
            )
        ],
    )[0]


def head_of(order, part):
    return member_of(order) * 8 + (pair_of(order) ^ part) * 4 + 2 * pl.program_id(0)


def team_attend_kernel(part, order, q_ref, k_ref, v_ref, o_ref, total_ref, vt, su):
    at = pl.program_id(1)
    block = q_ref.shape[0]

    @pl.when(at == 0)
    def _():
        vt[...] = v_ref[...].T
        set_bias(order[2], head_of(order, part), su)

    def branch(b):
        nk = (b + 1) * block
        q = q_ref[...]
        outs, totals = [], []
        found = [scores(k_ref, q, h, su, nk, block) for h in range(2)]
        for h, st in enumerate(found):
            m = jnp.max(st, axis=0, keepdims=True)
            p = jnp.exp(st - m)
            l = jnp.sum(p, axis=0, keepdims=True)
            ot = mm(vt[64 * h : 64 * h + 64, :nk], p.astype(bf16), PLAIN)
            outs.append(ot / l)
            totals.append(m + jnp.log(l))
        o_ref[...] = jnp.concatenate(outs, axis=0).T.astype(bf16)
        total_ref[0] = jnp.concatenate(totals + [jnp.zeros((6, block), f32)], axis=0)

    for b in range(k_ref.shape[0] // block):
        pl.when(at == b)(partial(branch, b))


def kept_place(i, o):
    return ((i % 2) ^ member_of(o)) * 2 + ((i // 2) ^ pair_of(o))


def team_attend(order, qkv, part, block):
    rows = qkv.shape[0]
    whole = lambda kind: pl.BlockSpec((rows, 128), lambda p, i, o: (0, 2 * kind + p))
    return pl.pallas_call(
        partial(team_attend_kernel, part),
        name="team_attend",
        grid_spec=pltpu.PrefetchScalarGridSpec(
            num_scalar_prefetch=1,
            grid=(2, rows // block),
            in_specs=[pl.BlockSpec((block, 128), lambda p, i, o: (i, p)), whole(1), whole(2)],
            out_specs=[
                pl.BlockSpec((block, 128), lambda p, i, o: (kept_place(i, o), p)),
                pl.BlockSpec((1, 8, block), lambda p, i, o: (p, 0, i)),
            ],
            scratch_shapes=[pltpu.VMEM((128, rows), bf16), pltpu.VMEM((2, rows, 128), f32)],
        ),
        out_shape=[shape_of((rows, 256), bf16), shape_of((2, 8, rows), f32)],
        compiler_params=pltpu.CompilerParams(vmem_limit_bytes=16 << 20),
        cost_estimate=WORK,
    )(order, qkv, qkv, qkv)


def team_back_kernel(
    part, order, q_ref, k_ref, v_ref, g_ref, total_ref, dq_ref, dk_ref, dv_ref, sum_ref,
    kt, su, dk, dv
):
    at = pl.program_id(1)
    block = q_ref.shape[0]
    blocks = k_ref.shape[0] // block

    @pl.when(at == 0)
    def _():
        kt[...] = k_ref[...].T
        set_bias(order[2], head_of(order, part), su)
        dk[...] = jnp.zeros_like(dk)
        dv[...] = jnp.zeros_like(dv)
        sum_ref[...] = jnp.zeros_like(sum_ref)

    def branch(b):
        nk = (b + 1) * block
        q, g = q_ref[...], g_ref[...]
        outs, dks, dvs = [], [], []
        found = [scores(k_ref, q, h, su, nk, block) for h in range(2)]
        halves = [half(g, h) for h in range(2)]
        products = [mm(v_ref[:nk], gm, ACROSS) for gm in halves]
        for h in range(2):
            p = jnp.exp(found[h] - total_ref[0, h : h + 1])
            gm, dp = halves[h], products[h]
            inner = jnp.sum(p * dp, axis=0, keepdims=True)
            ds = (p * (dp - inner)).astype(bf16)
            outs.append(mm(kt[64 * h : 64 * h + 64, :nk], ds, PLAIN))
            dks.append(mm(ds, half(q, h), PLAIN))
            dvs.append(mm(p.astype(bf16), gm, PLAIN))
        low = (jnp.concatenate(outs, axis=0).T * 0.125).astype(bf16)
        dq_ref[...] = low
        sum_ref[0, 0] += rows_of_eight(low.astype(f32))
        dk[:nk] += dks[0] + dks[1]
        dv[:nk] += dvs[0] + dvs[1]

    for b in range(blocks):
        pl.when(at == b)(partial(branch, b))

    @pl.when(at == blocks - 1)
    def _():
        dk_ref[...] = (dk[...] * 0.125).astype(bf16)
        low = dv[...].astype(bf16)
        dv_ref[...] = low
        sum_ref[0, 1] = rows_of_eight(low.astype(f32))


def team_back(order, qkv, grad, totals, part, block):
    rows = qkv.shape[0]
    whole = lambda kind: pl.BlockSpec((rows, 128), lambda p, i, o: (0, 2 * kind + p))
    by_rows = pl.BlockSpec((block, 128), lambda p, i, o: (i, p))
    by_head = pl.BlockSpec((rows, 128), lambda p, i, o: (0, p))
    return pl.pallas_call(
        partial(team_back_kernel, part),
        name="team_back",
        grid_spec=pltpu.PrefetchScalarGridSpec(
            num_scalar_prefetch=1,
            grid=(2, rows // block),
            in_specs=[
                by_rows,
                whole(1),
                whole(2),
                pl.BlockSpec((block, 128), lambda p, i, o: (kept_place(i, o), 2 * part + p)),
                pl.BlockSpec((1, 8, block), lambda p, i, o: (p, 0, i)),
            ],
            out_specs=[
                by_rows,
                by_head,
                by_head,
                pl.BlockSpec((1, 2, 8, 128), lambda p, i, o: (p, 0, 0, 0)),
            ],
            scratch_shapes=[
                pltpu.VMEM((128, rows), bf16),
                pltpu.VMEM((2, rows, 128), f32),
                pltpu.VMEM((rows, 128), f32),
                pltpu.VMEM((rows, 128), f32),
            ],
        ),
        out_shape=[shape_of((rows, 256), bf16)] * 3 + [shape_of((2, 2, 8, 128), f32)],
        compiler_params=pltpu.CompilerParams(vmem_limit_bytes=24 << 20),
        cost_estimate=WORK,
    )(order, qkv, qkv, qkv, grad, totals)


def joined(first, second):
    count, rows, width = first.shape

    def kernel(first_ref, second_ref, out_ref):
        out_ref[:count] = first_ref[...]
        out_ref[count:] = second_ref[...]

    return pl.pallas_call(
        kernel,
        name="joined",
        out_shape=shape_of((2 * count, rows, width), first.dtype),
        compiler_params=pltpu.CompilerParams(vmem_limit_bytes=12 << 20),
        cost_estimate=WORK,
    )(first, second)


def qkv_unit(order, qkv_weight, packed):
    def kernel(order, qkv_ref, packed_ref, unit_ref):
        unit_ref[0, :128] = jnp.concatenate(
            [
                qkv_ref[:, n * 192 + kind * 64 : n * 192 + kind * 64 + 64]
                for kind in range(3)
                for n in range(4)
            ],
            axis=1,
        )
        unit_ref[0, 128:] = jnp.concatenate([packed_ref[...], jnp.zeros((16, 640), bf16)], axis=1)

    share = lambda i, o: (0, member_of(o) * 2 + pair_of(o))
    return grid_call(
        "qkv_unit",
        kernel,
        order,
        (1,),
        [(qkv_weight, pl.BlockSpec((128, 768), share)), (packed, whole_block(packed))],
        [(shape_of((1, 144, 768), bf16), pl.BlockSpec((1, 144, 768), lambda i, o: (0, 0, 0)))],
    )[0]


def other_units(order, out_weight, up_weight, down_weight):
    def kernel(order, out_ref, up_ref, down_ref, out_unit, own_unit, other_unit, down_unit):
        c, x = member_of(order), pair_of(order)
        out_unit[0] = out_ref[...]
        for i in range(8):
            own_unit[0, :, 128 * i : 128 * i + 128] = lanes(up_ref, i * 4 + x * 2 + c)
            other_unit[0, :, 128 * i : 128 * i + 128] = lanes(up_ref, i * 4 + (1 - x) * 2 + c)
        down_unit[0] = down_ref[...]

    shapes = [(1, 128, 512), (1, 128, 1024), (1, 128, 1024), (1, 128, 1024)]
    return grid_call(
        "other_units",
        kernel,
        order,
        (1,),
        [
            (out_weight, pl.BlockSpec((128, 512), lambda i, o: (0, member_of(o)))),
            (up_weight, whole_block(up_weight)),
            (down_weight, pl.BlockSpec((128, 1024), lambda i, o: (o[1], 0))),
        ],
        [(shape_of(s, bf16), pl.BlockSpec(s, lambda i, o: (0, 0, 0))) for s in shapes],
    )


def unpacked(order, mine, came):
    def kernel(order, mine_ref, came_ref, vec_ref, qkv_ref, up_ref, tmp):
        c, x = member_of(order), pair_of(order)
        for i in range(8):
            values = (mine_ref if i < 4 else came_ref)[i % 4].astype(f32)
            start = owner(order, i) * 128
            vec_ref[:, pl.ds(pl.multiple_of(start, 128), 128)] = values
            tmp[i] = values
            for part in range(2):
                row = tmp[i, pl.ds(8 + (x ^ part) * 2 + c, 1)]
                up_ref[part : part + 1, pl.ds(pl.multiple_of(start, 128), 128)] = row
        for part in range(2):
            here = pl.ds(pl.multiple_of(c * 512 + (x ^ part) * 256, 128), 256)
            qkv_ref[part : part + 1] = jnp.concatenate(
                [vec_ref[6:7, here], jnp.zeros((1, 256), f32), vec_ref[7:8, here]], axis=1
            )

    spec = pl.BlockSpec((4, 16, 128), lambda i, o: (0, 8, 0))
    shapes = [(16, 1024), (2, 768), (2, 1024)]
    return grid_call(
        "unpacked",
        kernel,
        order,
        (1,),
        [(mine, spec), (came, spec)],
        [(shape_of(s, f32), pl.BlockSpec(s, lambda i, o: (0, 0))) for s in shapes],
        scratch=[pltpu.VMEM((8, 16, 128), f32)],
    )


def vector_sums(order, middle, pre, heads, first):
    def kernel(order, middle_ref, pre_own, pre_other, own_ref, other_ref, first_ref, out_ref):
        c, x = member_of(order), pair_of(order)
        out_ref[...] = jnp.zeros_like(out_ref)
        for i in range(4):
            out_ref[i : i + 1] = jnp.sum(middle_ref[i], axis=0, keepdims=True)
        for i in range(2):
            out_ref[4 + i : 5 + i] = jnp.sum(first_ref[i], axis=0, keepdims=True)
        for part, ref in enumerate((own_ref, other_ref)):
            for pair in range(2):
                start = (c * 4 + (x ^ part) * 2 + pair) * 128
                here = pl.ds(pl.multiple_of(start, 128), 128)
                for kind in range(2):
                    total = jnp.sum(ref[pair, kind], axis=0, keepdims=True)
                    out_ref[6 + kind : 7 + kind, here] = total
        for part, ref in enumerate((pre_own, pre_other)):
            total = jnp.sum(ref[...], axis=0, keepdims=True)
            for i in range(8):
                start = (i % 2) * 512 + (x ^ part) * 256 + c * 128
                here = pl.ds(pl.multiple_of(start, 128), 128)
                row = 8 + i // 2
                out_ref[row : row + 1, here] = total[:, 128 * i : 128 * i + 128]

    arrays = (middle,) + tuple(pre) + tuple(heads) + (first,)
    return grid_call(
        "vector_sums",
        kernel,
        order,
        (1,),
        [(a, whole_block(a)) for a in arrays],
        [(shape_of((12, 1024), f32), pl.BlockSpec((12, 1024), lambda i, o: (0, 0)))],
    )[0]


def one_of(pair, index):
    return lax.dynamic_index_in_dim(pair, index, 0, keepdims=False)


def flipped(pair, index):
    return jnp.where(index == 0, pair, pair[::-1])


def after(value, *earlier):
    return lax.optimization_barrier((value,) + earlier)[0]


def team_program(
    tokens,
    cotangent,
    lengths,
    first_gain,
    first_shift,
    qkv_weight,
    qv_bias,
    out_weight,
    out_bias,
    second_gain,
    second_shift,
    up_weight,
    up_bias,
    down_weight,
    down_bias,
):
    _, block, width = tokens.shape
    own_rows = 2 * block
    f, s = lax.axis_index("fsdp"), lax.axis_index("seq")
    x, c = s // 2, s % 2
    over_x = lambda v: exchange(v, "seq", 2)
    over_y = lambda v: exchange(v, "fsdp", 1)
    over_z = lambda v, k: exchange(v, "fsdp", 2 * k)

    length = one_of(lengths, x)

    def over_core(value):
        return lax.cond(length > 0, lambda v: exchange(v, "seq", 1), lambda v: v, value)

    order = jnp.stack([f, s, length]).astype(jnp.int32)

    order = [jnp.stack([f, s, length]).astype(jnp.int32)]

    def wait_for(*values):
        order[0] = after(order[0], *values)

    def run(kernel, *operands, **options):
        result = kernel(order[0], *operands, **options)
        wait_for(result[0] if isinstance(result, (list, tuple)) else result)
        return result

    def join(first, second):
        result = joined(after(first, order[0]), second)
        wait_for(result)
        return result

    full = lambda a, b: ((a, 0, a.shape[2], 0), (b, 0, b.shape[2], 0))

    packed = [first_gain, first_shift, second_gain, second_shift, out_bias, down_bias, qv_bias, up_bias]
    packed = jnp.concatenate([v.reshape(-1, 128) for v in packed] + [jnp.zeros((4, 128), bf16)])
    unit_qkv = run(qkv_unit, qkv_weight, packed)
    tokens_came = over_x(one_of(tokens, 1 - x))
    unit_out, unit_up, unit_up_other, unit_down = run(
        other_units, out_weight, up_weight, down_weight
    )
    own_mine = one_of(tokens, x)
    other_mine, other_came = over_core(own_mine), over_core(tokens_came)
    grad_came = over_x(one_of(after(cotangent, tokens_came), 1 - x))
    z_qkv = join(unit_qkv, over_z(unit_qkv, 1))
    z_out = over_z(after(unit_out, z_qkv), 1)
    own_tokens = jnp.concatenate([own_mine, tokens_came])
    wait_for(other_mine, other_came)
    z_qkv = join(z_qkv, over_z(z_qkv, 2))
    y_qkv, xz_qkv = over_y(z_qkv), over_x(z_qkv)
    z_out = join(unit_out, z_out)
    z_out_came = over_z(z_out, 2)
    z_up = over_z(after(unit_up, z_out), 1)

    blocks_at = (jnp.arange(2) ^ x) * 2 + c
    valid = ((blocks_at[:, None] * block + jnp.arange(block)) < length).reshape(own_rows, 1)
    grad_own = jnp.concatenate([one_of(cotangent, x), grad_came])
    grad_own = jnp.where(valid, grad_own, jnp.zeros_like(grad_own))
    grad_other = over_core(grad_own)
    grad_all = jnp.concatenate([grad_own, grad_other])
    wait_for(grad_all)
    z_up = join(unit_up, z_up)
    z_up_came = over_z(z_up, 2)
    z_out = join(z_out, z_out_came)
    y_out = over_y(z_out)
    z_down = over_z(after(unit_down, z_up), 1)
    xy_qkv = over_x(y_qkv)
    qkv_own, qkv_other = full(z_qkv, y_qkv), full(xz_qkv, xy_qkv)
    vectors, bias_qkv, bias_up = run(unpacked, z_qkv, y_qkv)
    normed = run(first_norm, tokens, tokens_came, other_mine, other_came, vectors)
    projected = [None, None]
    mixed, totals = [None, None], [None, None]
    wait_for(xz_qkv)
    projected[0] = run(project, normed, bias_qkv, 0, Weight(qkv_own))
    mixed[0], totals[0] = run(team_attend, projected[0], 0, block)
    z_up = join(z_up, z_up_came)
    y_up = over_y(z_up)
    z_down = join(unit_down, z_down)
    z_down_came = over_z(z_down, 2)
    z_up_other = over_z(after(unit_up_other, z_down), 1)
    projected[1] = run(project, normed, bias_qkv, 1, Weight(qkv_other))
    mixed[1], totals[1] = run(team_attend, projected[1], 1, block)
    z_out_other, y_out_other = over_core(after(z_out, order[0])), over_core(after(y_out, order[0]))
    z_down = join(z_down, z_down_came)
    y_down, xz_down = over_y(z_down), over_x(z_down)
    z_up_other = join(unit_up_other, z_up_other)
    z_up_other_came = over_z(z_up_other, 2)
    out = Weight(full(z_out, y_out), full(z_out_other, y_out_other))
    sent = jnp.concatenate([m[own_rows:] for m in mixed], axis=1)
    mixed_rows = jnp.concatenate([m[:own_rows] for m in mixed] + [over_core(sent)], axis=1)
    middle, norm_own = run(out_and_norm, mixed_rows, own_tokens, vectors, out)
    norm_other = over_core(norm_own)
    wait_for(norm_other)
    norm_all = jnp.concatenate([norm_own, norm_other])

    act, slope, grad_pre, pre_sums = ([None, None] for _ in range(4))
    up_sent, up_kept, up_came = ([None, None] for _ in range(3))

    def up_grad(part, first):
        return run(weight_grad, first, 4, norm_all, [(grad_pre[part], 1024, 0)])

    def down_grad(part, first, count):
        return run(weight_grad, first, count, act[part], [(grad_all, 1024, 0)])

    act[0], slope[0] = run(feed_up, norm_all, bias_up, 0, Weight(full(z_up, y_up)))
    z_up_other = join(z_up_other, z_up_other_came)
    y_up_other = over_y(z_up_other)
    down_kept = down_grad(0, 0, 8)
    up = [full(z_up, y_up), full(z_up_other, y_up_other)]
    xy_down = over_x(y_down)
    down = [full(z_down, y_down), full(xz_down, xy_down)]
    grad_pre[0], pre_sums[0] = run(
        feed_down_back, grad_all, slope[0], Weight(down[0])
    )
    up_sent[0] = up_grad(0, 4)
    up_came[0] = over_y(up_sent[0])
    up_kept[0] = up_grad(0, 0)
    act[1], slope[1] = run(feed_up, norm_all, bias_up, 1, Weight(up[1]))
    down_sent = [None, None]
    for i in (1, 0):
        down_sent[i] = down_grad(1, 4 * i, 4)
    down_came = [over_x(sent) for sent in down_sent]
    grad_pre[1], pre_sums[1] = run(
        feed_down_back, grad_all, slope[1], Weight(down[1])
    )
    wait_for(up_came[0])
    up_sent[1] = up_grad(1, 4)
    up_came[1] = over_y(up_sent[1])
    back_own, back_sent = run(
        feed_up_back,
        grad_pre,
        Weight(*up),
    )
    back_came = over_core(back_sent)
    up_kept[1] = up_grad(1, 0)
    grad_middle, branch, mixed_kept, mixed_sent, middle_sums = run(
        middle_back, back_own, back_came, middle, grad_own, vectors, out
    )
    grad_mixed = jnp.concatenate([mixed_kept, over_core(mixed_sent)])
    out_grad = lambda which: run(
        weight_grad, 0, 8, mixed_rows, [(branch, 512, which)], block_of=mixed_block
    )
    out_sent = out_grad(1)
    out_came = over_core(out_sent)
    out_kept = out_grad(0)

    def added(kept, came):
        return kept.astype(f32) + came.astype(f32)

    def low_sum(kept, came):
        return added(kept, came).astype(bf16)

    def z_pieces(total):
        return [total[k].astype(bf16) for k in (1, 2, 3)]

    def sum_z(total, pieces):
        result = total[0]
        for k, piece in enumerate(pieces):
            result = result + over_z(piece, k + 1).astype(f32)
        return result

    def qkv_grad(grads, first, part):
        rights = [(grad, 256, 0) for grad in grads]
        return run(weight_grad, first, 4, normed, rights, extra=(out_kept, out_came, part))

    def z_far(total):
        return total[2:].astype(bf16)

    def z_near(total, far_came):
        total = added(total[:2], far_came)
        return total[0], total[1].astype(bf16)

    up_x = low_sum(up_kept[1], up_came[1])
    up_x_came = over_x(up_x)
    down_y = low_sum(down_kept[4:], down_came[1])
    down_y_came = over_y(down_y)
    wait_for(up_x, down_y)
    *heads_other, sums_other = run(team_back, projected[1], grad_mixed, totals[1], 1, block)
    other_y_came = over_y(qkv_grad(heads_other, 4, 1))
    down_total = added(low_sum(after(down_kept[:4], order[0]), down_came[0]), down_y_came)
    down_far = z_far(down_total)
    down_far_came = over_z(down_far, 2)
    wait_for(down_far)
    other_kept = qkv_grad(heads_other, 0, 1)
    *heads_own, sums_own = run(team_back, projected[0], grad_mixed, totals[0], 0, block)
    other_x = low_sum(other_kept, other_y_came)
    other_x_came = over_x(other_x)
    wait_for(other_x)
    own_y_came = over_y(qkv_grad(heads_own, 4, 0))
    up_total = added(low_sum(after(up_kept[0], order[0]), up_came[0]), up_x_came)
    up_far = z_far(up_total)
    up_far_came = over_z(up_far, 2)
    wait_for(up_far)
    first_own, first_sent = run(
        project_back, [heads_own, heads_other], Weight(qkv_own, qkv_other)
    )
    first_came = over_core(first_sent)
    fed_own, fed_sent = run(feed_down, act, Weight(*down))
    block_own = jnp.where(
        valid, middle + (fed_own + over_core(fed_sent).astype(f32)) + vectors[5:6], 0.0
    ).astype(bf16)
    down_sum, down_near = z_near(down_total, after(down_far_came, fed_own))
    down_near_came = over_z(down_near, 1)
    wait_for(down_near)
    up_sum, up_near = z_near(up_total, up_far_came)
    up_near_came = over_z(up_near, 1)
    wait_for(up_near, down_near_came)
    own_kept = qkv_grad(heads_own, 0, 0)
    qkv_total = added(own_kept, own_y_came) + other_x_came.astype(f32)
    qkv_pieces = z_pieces(qkv_total)
    wait_for(*qkv_pieces)
    row_grad, first_sums = run(first_back, first_own, first_came, own_tokens, grad_middle, vectors)

    def to_devices(rows):
        return flipped(jnp.stack([rows[:block], over_x(rows[block:])]), x)

    tokens_grad = to_devices(row_grad)
    block_out = to_devices(block_own)

    def over_pair(total):
        pieces = total.reshape(2, 64, -1)
        rows = flipped(jnp.stack([one_of(pieces, x), over_x(one_of(pieces, 1 - x))]), x)
        return jnp.swapaxes(rows, 0, 1)

    def over_team(total):
        pieces = total.reshape((2, 32) + total.shape[1:])
        rows = flipped(jnp.stack([one_of(pieces, c), over_core(one_of(pieces, 1 - c))]), c)
        return jnp.swapaxes(rows, 0, 1)

    down_sum = added(down_sum, down_near_came)
    up_sum = over_team(over_pair(added(up_sum, up_near_came)))
    up_sum = up_sum.reshape(32, 2, 2, 8, 128).transpose(0, 3, 2, 1, 4).reshape(32, 4096)
    qkv_sum = over_team(over_pair(sum_z(qkv_total, qkv_pieces)))
    out_sum = qkv_sum[..., 768:].reshape(32, width)
    qkv_sum = qkv_sum[..., :768].reshape(32, 2, 2, 3, 4, 64)
    qkv_sum = jnp.transpose(qkv_sum, (0, 1, 2, 4, 3, 5)).reshape(32, 3 * width)

    sums = run(vector_sums, middle_sums, pre_sums, (sums_own, sums_other), first_sums)
    for step in (over_core, over_x, over_y, partial(over_z, k=1), partial(over_z, k=2)):
        sums = sums + step(sums)
    place = f * 4 + s
    pieces = lax.dynamic_slice(sums[:8], (0, place * 32), (8, 32))
    up_piece = lax.dynamic_slice(sums[8:].reshape(4096), (place * 128,), (128,))
    return (
        block_out,
        tokens_grad,
        pieces[4],
        pieces[5],
        qkv_sum,
        pieces[6:8],
        out_sum,
        pieces[2],
        pieces[0],
        pieces[1],
        up_sum,
        up_piece,
        down_sum,
        pieces[3],
    )


def local(tokens, *others):
    width = tokens.shape[2]
    shards = (lax.axis_size("fsdp"), lax.axis_size("seq"))
    hidden = others[10].shape[1]
    if tokens.shape[0] == 2 and tokens.shape[1] % 256 == 0 and shards == (8, 4) and tokens.shape[1] * 4 <= 1024 and (width, hidden) == (1024, 4096):
        return team_program(tokens, *others)
    return general_program(tokens, *others)


def solution(mesh):
    return jax.shard_map(
        local,
        mesh=mesh,
        in_specs=(
            P("fsdp", "seq", None),
            P("fsdp", "seq", None),
            P("fsdp"),
            P("fsdp"),
            P("fsdp"),
            P("fsdp", None),
            P(None, "fsdp"),
            P("fsdp", None),
            P("fsdp"),
            P("fsdp"),
            P("fsdp"),
            P("fsdp", None),
            P("fsdp"),
            P("fsdp", None),
            P("fsdp"),
        ),
        out_specs=(
            P("fsdp", "seq", None),
            P("fsdp", "seq", None),
            P(("fsdp", "seq")),
            P(("fsdp", "seq")),
            P(("fsdp", "seq"), None),
            P(None, ("fsdp", "seq")),
            P(("fsdp", "seq"), None),
            P(("fsdp", "seq")),
            P(("fsdp", "seq")),
            P(("fsdp", "seq")),
            P(("fsdp", "seq"), None),
            P(("fsdp", "seq")),
            P(("fsdp", "seq"), None),
            P(("fsdp", "seq")),
        ),
        check_vma=False,
    )
```

```python
from functools import partial
import math

import jax
import jax.numpy as jnp
from jax import lax
from jax.experimental import pallas as pl
from jax.experimental.pallas import tpu as pltpu
from jax.sharding import PartitionSpec as P

H = 16


epsilon = 1e-05
f32 = jnp.float32
bf16 = jnp.bfloat16


def layer_norm(values, norm_gain, norm_shift):
    row_mean = jnp.mean(values, axis=-1, keepdims=True)
    centered = values - row_mean
    variance = jnp.mean(centered * centered, axis=-1, keepdims=True)
    return centered * lax.rsqrt(variance + epsilon) * norm_gain + norm_shift


def product(left_side, right_side):
    return jnp.dot(left_side, right_side, preferred_element_type=f32)


def contract_rows(left_side, right_side):
    return lax.dot_general(
        left_side, right_side, (((0,), (0,)), ((), ())), preferred_element_type=f32
    )


def against(left_side, right_side):
    return lax.dot_general(
        left_side, right_side, (((1,), (1,)), ((), ())), preferred_element_type=f32
    )


def head_scores(query_block, key_rows, start_row, slopes, length, score_scale):
    block_size = query_block.shape[1]
    seq_len = key_rows.shape[1]
    row_index = start_row + jnp.arange(block_size)
    columns = jnp.arange(seq_len)
    products = jnp.einsum("hqd,hkd->hqk", query_block, key_rows, preferred_element_type=f32)
    distance = (columns[None, :] - row_index[:, None]).astype(f32)
    allowed = (columns[None, :] <= row_index[:, None]) & (columns[None, :] < length)
    return jnp.where(
        allowed[None], products * score_scale + slopes[:, None, None] * distance, -jnp.inf
    )


def attend(queries, key_rows, value_rows, length, slopes, score_scale):
    head_count, seq_len, head_size = queries.shape
    block_size = math.gcd(512, seq_len)

    def one_block(start_row):
        query_block = lax.dynamic_slice_in_dim(queries, start_row, block_size, 1)
        scores = head_scores(query_block, key_rows, start_row, slopes, length, score_scale)
        largest = jnp.max(scores, axis=-1, keepdims=True)
        log_total = largest + jnp.log(jnp.sum(jnp.exp(scores - largest), axis=-1, keepdims=True))
        attention_probs = jnp.exp(scores - log_total).astype(bf16)
        mixed_rows = jnp.einsum(
            "hqk,hkd->hqd", attention_probs, value_rows, preferred_element_type=f32
        )
        return (mixed_rows.astype(bf16), log_total[..., 0])

    starts = jnp.arange(seq_len // block_size, dtype=jnp.int32) * block_size
    mixed_rows, log_totals = lax.map(one_block, starts)
    return (
        jnp.moveaxis(mixed_rows, 0, 1).reshape(head_count, seq_len, head_size),
        jnp.moveaxis(log_totals, 0, 1).reshape(head_count, seq_len),
    )


def attend_back(queries, key_rows, value_rows, grad_mixed, log_totals, length, slopes, score_scale):
    head_count, seq_len, head_size = queries.shape
    block_size = math.gcd(512, seq_len)

    def one_block(carried, start_row):
        key_sum, value_sum = carried
        query_block = lax.dynamic_slice_in_dim(queries, start_row, block_size, 1)
        grad_block = lax.dynamic_slice_in_dim(grad_mixed, start_row, block_size, 1)
        total_block = lax.dynamic_slice_in_dim(log_totals, start_row, block_size, 1)
        scores = head_scores(query_block, key_rows, start_row, slopes, length, score_scale)
        attention_probs = jnp.exp(scores - total_block[..., None])
        grad_probs = jnp.einsum(
            "hqd,hkd->hqk", grad_block, value_rows, preferred_element_type=f32
        )
        row_inner = jnp.sum(attention_probs * grad_probs, axis=-1, keepdims=True)
        grad_scores = (attention_probs * (grad_probs - row_inner)).astype(bf16)
        query_grad = (
            jnp.einsum("hqk,hkd->hqd", grad_scores, key_rows, preferred_element_type=f32)
            * score_scale
        ).astype(bf16)
        key_sum = (
            key_sum
            + jnp.einsum("hqk,hqd->hkd", grad_scores, query_block, preferred_element_type=f32)
            * score_scale
        )
        value_sum = value_sum + jnp.einsum(
            "hqk,hqd->hkd",
            attention_probs.astype(bf16),
            grad_block,
            preferred_element_type=f32,
        )
        return ((key_sum, value_sum), query_grad)

    starts = jnp.arange(seq_len // block_size, dtype=jnp.int32) * block_size
    empty = jnp.zeros(queries.shape, f32)
    (key_sum, value_sum), query_grads = lax.scan(one_block, (empty, empty), starts)
    query_grad = jnp.moveaxis(query_grads, 0, 1).reshape(head_count, seq_len, head_size)
    return (query_grad, key_sum.astype(bf16), value_sum.astype(bf16))


ACROSS = ((1,), (1,))
PLAIN = ((1,), (0,))
DOWN = ((0,), (0,))

def mm(left_side, right_side, dims):
    return lax.dot_general(left_side, right_side, (dims, ((), ())), preferred_element_type=f32)


def set_bias(length, head, su):
    rows = su.shape[1]
    u = lax.broadcasted_iota(jnp.int32, (rows, 128), 0)
    for h in range(2):
        power = jnp.full((rows, 128), head + (h + 1), jnp.int32).astype(f32)
        slope = jnp.exp2(power * (-8.0 / H))
        su[h] = jnp.where(u < length, u.astype(f32) * slope, -jnp.inf)


def half(value, h):
    lane = lax.broadcasted_iota(jnp.int32, value.shape, 1)
    return jnp.where((lane // 64) == h, value, jnp.zeros_like(value))


def scores(k_ref, q, h, su, nk, block):
    st = mm(k_ref[:nk], half(q, h) * jnp.asarray(0.125, bf16), ACROSS)
    st = st + jnp.concatenate([su[h, :nk]] * (block // 128), axis=1)
    keep = lax.broadcasted_iota(jnp.int32, (block, block), 0) <= lax.broadcasted_iota(
        jnp.int32, (block, block), 1
    )
    tail = jnp.where(keep, st[nk - block :], -jnp.inf)
    return tail if nk == block else jnp.concatenate([st[: nk - block], tail], axis=0)


def exchange(value, axis, bit):
    return lax.ppermute(value, axis, [(i, i ^ bit) for i in range(lax.axis_size(axis))])


def is_set(axis, bit):
    return (lax.axis_index(axis) // bit) % 2


def place(bit):
    return (0 if bit[0] == "fsdp" else 1, -bit[1])


def powers(size):
    return [1 << i for i in range(size.bit_length() - 1)]


def gather_bits(unit, order):
    held, buffer = [], unit
    for bit in order:
        received = exchange(buffer, *bit)
        second = is_set(*bit) == 1
        at = sum(1 for other in held if place(other) < place(bit))
        buffer = jnp.stack(
            [jnp.where(second, received, buffer), jnp.where(second, buffer, received)], axis=at
        )
        held.append(bit)
    return buffer


def scatter_bits(partial_sum, held, order):
    held, buffer = list(held), partial_sum
    for bit in order:
        at, mine = held.index(bit), is_set(*bit)
        sent = lax.dynamic_index_in_dim(buffer, 1 - mine, at, keepdims=False).astype(bf16)
        kept = lax.dynamic_index_in_dim(buffer, mine, at, keepdims=False).astype(f32)
        buffer = kept + exchange(sent, *bit).astype(f32)
        held.remove(bit)
    return buffer


def in_order(pieces, own):
    pieces = list(pieces)
    for bit in powers(len(pieces)):
        second = (own // bit) % 2 == 1
        pieces = [
            jnp.where(second, pieces[i ^ bit], pieces[i]) for i in range(len(pieces))
        ]
    return pieces


class Team:
    def __init__(self, micro_count):
        self.shards = lax.axis_size("seq")
        self.size = self.shards // micro_count
        self.micro_count = micro_count
        self.member = lax.axis_index("seq") % self.size
        self.which = lax.axis_index("seq") // self.size
        self.team_bits = [("seq", bit) for bit in powers(self.size)]
        self.pair_bits = [("seq", self.size * bit) for bit in powers(micro_count)]

    def to_sequences(self, pieces):
        arrived = []
        for offset in range(self.micro_count):
            sent = lax.dynamic_index_in_dim(pieces, self.which ^ offset, 0, keepdims=False)
            arrived.append(sent if offset == 0 else exchange(sent, "seq", offset * self.size))
        return jnp.stack(in_order(arrived, self.which))

    def share(self, own):
        arrived = [own if e == 0 else exchange(own, "seq", e) for e in range(self.size)]
        return jnp.stack(in_order(arrived, self.member), axis=1)

    def swap(self, pieces, axis, onto):
        arrived = []
        for e in range(self.size):
            sent = lax.dynamic_index_in_dim(pieces, self.member ^ e, axis, keepdims=False)
            arrived.append(sent if e == 0 else exchange(sent, "seq", e))
        return jnp.stack(in_order(arrived, self.member), axis=onto)

    def reduce(self, partial_sum):
        total = lax.dynamic_index_in_dim(partial_sum, self.member, 1, keepdims=False)
        for e in range(1, self.size):
            sent = lax.dynamic_index_in_dim(partial_sum, self.member ^ e, 1, keepdims=False)
            total = total + exchange(sent.astype(bf16), "seq", e).astype(f32)
        return total


def general_program(
    tokens,
    cotangent,
    lengths,
    first_gain,
    first_shift,
    qkv_weight,
    qv_bias,
    out_weight,
    out_bias,
    second_gain,
    second_shift,
    up_weight,
    up_bias,
    down_weight,
    down_bias,
):
    micro_count, block_rows, width = tokens.shape
    team = Team(micro_count)
    size, member, which = team.size, team.member, team.which
    shards = team.shards
    fsdp_shards = lax.axis_size("fsdp")
    seq_len = block_rows * shards
    head_size = width // H
    own_heads = H // size
    own_width = own_heads * head_size
    hidden = up_weight.shape[1]
    own_hidden = hidden // size
    fsdp_bits = [("fsdp", bit) for bit in powers(fsdp_shards)]
    line_bits = fsdp_bits[1:] + fsdp_bits[:1]
    pair_bits, team_bits = team.pair_bits, team.team_bits
    rows_first = lambda bits: sorted(bits, key=place)
    split = lambda bits: (2,) * len(bits)

    packed = jnp.concatenate(
        [
            first_gain,
            first_shift,
            second_gain,
            second_shift,
            out_bias,
            down_bias,
            qv_bias[0],
            qv_bias[1],
            up_bias,
        ]
    )
    packed = gather_bits(packed, line_bits).reshape(fsdp_shards, -1).astype(f32)
    part = width // fsdp_shards
    vectors = [packed[:, i * part : (i + 1) * part].reshape(width) for i in range(8)]
    gain_one, shift_one, gain_two, shift_two, bias_out, bias_down, bias_q, bias_v = vectors
    bias_up = packed[:, 8 * part :].reshape(hidden // (size * (hidden // (fsdp_shards * shards))), size, -1)
    bias_up = lax.dynamic_index_in_dim(bias_up, member, 1, keepdims=False).reshape(own_hidden)

    def part_rows(weight, bits, parts_of):
        rows = weight.shape[0] // parts_of
        index = jnp.int32(0)
        for bit in rows_first(bits):
            index = index * 2 + is_set(*bit)
        return lax.dynamic_slice_in_dim(weight, index * rows, rows, 0)

    qkv_own = lax.dynamic_slice_in_dim(qkv_weight, member * 3 * own_width, 3 * own_width, 1)
    qkv_own = jnp.swapaxes(qkv_own.reshape(-1, own_heads, 3, head_size), 1, 2).reshape(-1, 3 * own_width)
    whole_qkv = gather_bits(
        part_rows(qkv_own, pair_bits, micro_count), line_bits + pair_bits
    ).reshape(width, 3 * own_width)
    whole_out = gather_bits(
        part_rows(out_weight, pair_bits + team_bits, shards), line_bits + pair_bits + team_bits
    ).reshape(width, width)
    unit = hidden // (fsdp_shards * shards)
    up_own = lax.dynamic_index_in_dim(
        up_weight.reshape(width // fsdp_shards, hidden // (size * unit), size, unit),
        member,
        2,
        keepdims=False,
    ).reshape(width // fsdp_shards, own_hidden)
    whole_up = gather_bits(up_own, line_bits).reshape(width, own_hidden)
    down_own = lax.dynamic_index_in_dim(
        down_weight.reshape(micro_count, size, unit, width), member, 1, keepdims=False
    ).reshape(micro_count * unit, width)
    whole_down = gather_bits(
        part_rows(down_own, pair_bits, micro_count), line_bits + pair_bits
    ).reshape(own_hidden, width)

    length = lax.dynamic_index_in_dim(lengths, which, 0, keepdims=False)
    own_tokens = team.to_sequences(tokens)
    all_tokens = team.share(own_tokens).reshape(seq_len, width).astype(f32)
    own_rows = micro_count * block_rows
    own_tokens = own_tokens.reshape(own_rows, width).astype(f32)
    own_positions = (
        (jnp.arange(micro_count)[:, None] * size + member) * block_rows
        + jnp.arange(block_rows)[None, :]
    ).reshape(own_rows)
    valid_mask = (own_positions < length).astype(f32)[:, None]
    slopes = jnp.exp2(-((member * own_heads + jnp.arange(own_heads)).astype(f32) + 1.0) * 8.0 / H)
    score_scale = head_size ** (-0.5)

    by_member = (micro_count, size, block_rows)

    normed = layer_norm(all_tokens, gain_one, shift_one).astype(bf16)
    own_bias = lambda vector: lax.dynamic_slice_in_dim(vector, member * own_width, own_width, 0)
    bias_columns = jnp.concatenate([own_bias(bias_q), jnp.zeros((own_width,), f32), own_bias(bias_v)])
    projected = (product(normed, whole_qkv) + bias_columns).astype(bf16)
    split_heads = lambda value: jnp.moveaxis(value.reshape(seq_len, -1, head_size), 1, 0)
    join_heads = lambda value: jnp.moveaxis(value, 0, 1).reshape(seq_len, -1)
    queries, key_rows, value_rows = [
        split_heads(projected[:, i * own_width : (i + 1) * own_width]) for i in range(3)
    ]
    mixed, log_totals = attend(queries, key_rows, value_rows, length, slopes, score_scale)
    mixed = join_heads(mixed)
    mixed_rows = team.swap(mixed.reshape(by_member + (own_width,)), 1, 2).reshape(own_rows, width)
    middle = own_tokens + (product(mixed_rows, whole_out) + bias_out)
    normed_two_own = layer_norm(middle, gain_two, shift_two).astype(bf16)
    normed_two = team.share(normed_two_own.reshape(micro_count, block_rows, width)).reshape(
        seq_len, width
    )
    hidden_pre = product(normed_two, whole_up) + bias_up
    activation = jax.nn.gelu(hidden_pre, approximate=True).astype(bf16)
    fed = team.reduce(product(activation, whole_down).reshape(by_member + (width,)))
    block_own = (valid_mask * (middle + fed.reshape(own_rows, width) + bias_down)).astype(bf16)
    block_out = team.to_sequences(block_own.reshape(micro_count, block_rows, width))

    own_grad = team.to_sequences(cotangent)
    own_grad = jnp.where(
        (valid_mask > 0).reshape(micro_count, block_rows, 1), own_grad, jnp.zeros_like(own_grad)
    )
    grad_low = team.share(own_grad).reshape(seq_len, width)
    grad_out = own_grad.reshape(own_rows, width).astype(f32)
    down_bias_grad = jnp.sum(grad_out, axis=0)
    down_grad = contract_rows(activation, grad_low)
    grad_act = against(grad_low, whole_down)
    gelu_pull = jax.vjp(partial(jax.nn.gelu, approximate=True), hidden_pre)[1]
    grad_pre = gelu_pull(grad_act)[0].astype(bf16)
    up_grad = contract_rows(normed_two, grad_pre)
    up_bias_grad = jnp.sum(grad_pre.astype(f32), axis=0)
    grad_normed_two = team.reduce(
        against(grad_pre, whole_up).reshape(by_member + (width,))
    ).reshape(own_rows, width)
    norm_pull = jax.vjp(layer_norm, middle, gain_two, shift_two)[1]
    middle_part, second_gain_grad, second_shift_grad = norm_pull(grad_normed_two)
    grad_middle = grad_out + middle_part
    grad_branch = grad_middle.astype(bf16)
    out_bias_grad = jnp.sum(grad_branch.astype(f32), axis=0)
    out_grad = contract_rows(mixed_rows, grad_branch)
    grad_mixed_own = against(grad_branch, whole_out).astype(bf16)
    grad_mixed = team.swap(
        grad_mixed_own.reshape(micro_count, block_rows, size, own_width), 2, 1
    ).reshape(seq_len, own_width)
    backs = attend_back(
        queries,
        key_rows,
        value_rows,
        split_heads(grad_mixed),
        log_totals,
        length,
        slopes,
        score_scale,
    )
    grad_qkv = jnp.concatenate([join_heads(back) for back in backs], axis=1)
    qkv_grad = contract_rows(normed, grad_qkv)
    column_sums = jnp.sum(grad_qkv.astype(f32), axis=0).reshape(3, own_width)
    grad_normed = team.reduce(
        against(grad_qkv, whole_qkv).reshape(by_member + (width,))
    ).reshape(own_rows, width)
    first_pull = jax.vjp(layer_norm, own_tokens, gain_one, shift_one)[1]
    token_part, first_gain_grad, first_shift_grad = first_pull(grad_normed)
    row_grad = (grad_middle + token_part).astype(bf16)
    tokens_grad = team.to_sequences(row_grad.reshape(micro_count, block_rows, width))

    row_bits = rows_first(fsdp_bits + pair_bits)
    pair_first = pair_bits + fsdp_bits[:1] + fsdp_bits[:0:-1]
    pair_second = fsdp_bits[:1] + pair_bits + fsdp_bits[:0:-1]
    down_sum = scatter_bits(
        down_grad.reshape(split(row_bits) + (unit, width)), row_bits, pair_first
    )

    def by_columns(grad, order):
        total = scatter_bits(
            grad.reshape(split(row_bits) + (size, -1) + grad.shape[1:]), row_bits, order
        )
        return team.swap(total, 0, 1)

    up_sum = by_columns(up_grad, pair_second)
    up_sum = jnp.swapaxes(up_sum.reshape(-1, size, hidden // (size * unit), unit), 1, 2)
    up_sum = up_sum.reshape(-1, hidden)
    qkv_sum = by_columns(qkv_grad, pair_first).reshape(-1, size, 3, own_heads, head_size)
    qkv_sum = jnp.swapaxes(qkv_sum, 2, 3).reshape(-1, 3 * width)
    all_bits = rows_first(fsdp_bits + pair_bits + team_bits)
    out_sum = scatter_bits(
        out_grad.reshape(split(all_bits) + (-1, width)), all_bits, team_bits[::-1] + pair_first
    )

    devices = fsdp_shards * shards

    def spread(own, count):
        at_member = jnp.arange(size).reshape(1, size, 1) == member
        return jnp.where(at_member, own.reshape(count, 1, -1), 0.0)

    up_vector = spread(up_bias_grad, hidden // (size * unit)).reshape(devices, unit)
    by_team = lambda own: spread(own.reshape(1, own_width), 1).reshape(width)
    vectors = [
        first_gain_grad,
        first_shift_grad,
        second_gain_grad,
        second_shift_grad,
        out_bias_grad,
        down_bias_grad,
        by_team(column_sums[0]),
        by_team(column_sums[2]),
    ]
    buffer = jnp.concatenate([v.reshape(devices, -1) for v in vectors] + [up_vector], axis=1)
    buffer = buffer.reshape(split(all_bits) + (-1,))
    held = list(all_bits)
    for bit in team_bits + pair_first:
        at, mine = held.index(bit), is_set(*bit)
        sent = lax.dynamic_index_in_dim(buffer, 1 - mine, at, keepdims=False)
        kept = lax.dynamic_index_in_dim(buffer, mine, at, keepdims=False)
        buffer = kept + exchange(sent, *bit)
        held.remove(bit)
    each = width // devices
    sums = [buffer[i * each : (i + 1) * each] for i in range(8)]
    return (
        block_out,
        tokens_grad,
        sums[0],
        sums[1],
        qkv_sum,
        jnp.stack([sums[6], sums[7]]),
        out_sum,
        sums[4],
        sums[2],
        sums[3],
        up_sum,
        buffer[8 * each :],
        down_sum,
        sums[5],
    )


WORK = pl.CostEstimate(flops=4000000000, bytes_accessed=8000000, transcendentals=0)


def whole_block(array):
    return pl.BlockSpec(array.shape, lambda *_: (0,) * array.ndim, pipeline_mode=pl.Buffered(1))


def lanes(ref, block):
    return ref[:, pl.ds(pl.multiple_of(block * 128, 128), 128)]


def member_of(order):
    return order[1] & 1


def pair_of(order):
    return order[1] >> 1


def owner(order, i):
    return order[0] ^ ((i & 3) * 2 + (i >> 2))


def mixed_block(order, i):
    return owner(order, i) ^ (member_of(order) * 4 + pair_of(order) * 2)


def natural(order, i):
    return i


def picked(ref, order, first, block_of=owner):
    return jnp.concatenate([lanes(ref, block_of(order, first + i)) for i in range(4)], axis=1)


def flat(ref, start):
    value = ref[start : start + 4, :128]
    return value.reshape(512, value.shape[-1])


class Weight:
    def __init__(self, *parts, orders=None):
        self.parts = parts
        self.orders = orders or [owner] * len(parts)

    def slabs(self):
        found = []
        for pair in self.parts:
            for array, _, columns, which in pair:
                if not any(array is a and (columns, which) == b for a, b in found):
                    found.append((array, (columns, which)))
        return found

    def inputs(self):
        result = []
        for array, (columns, which) in self.slabs():
            spec = pl.BlockSpec(
                array.shape[:2] + (columns,),
                lambda *_, which=which: (0, 0, which),
                pipeline_mode=pl.Buffered(1),
            )
            result.append((array, spec))
        return result

    def tiles(self, columns=0, blocks=0):
        result = []
        for pair in self.parts:
            for array, first, wide, which in pair:
                if columns:
                    shape = (4, 128, columns)
                    place = lambda j, *_, f=first, w=which * (wide // columns): (f // 4, 0, w + j)
                else:
                    shape = (blocks, 128, wide)
                    place = lambda j, *_, f=first, w=which: (f // blocks + j, 0, w)
                result.append((array, pl.BlockSpec(shape, place)))
        return result

    def views(self, refs):
        slabs = self.slabs()

        def find(view):
            array, first, columns, which = view
            at = [array is a and (columns, which) == b for a, b in slabs].index(True)
            return refs[at], first

        return [(find(pair[0]), find(pair[1])) for pair in self.parts]


def grid_call(name, kernel, order, grid, inputs, outputs, scratch=(), limit=24):
    return pl.pallas_call(
        kernel,
        name=name,
        grid_spec=pltpu.PrefetchScalarGridSpec(
            num_scalar_prefetch=1,
            grid=grid,
            in_specs=[spec for _, spec in inputs],
            out_specs=[spec for _, spec in outputs],
            scratch_shapes=list(scratch),
        ),
        out_shape=[shape for shape, _ in outputs],
        compiler_params=pltpu.CompilerParams(vmem_limit_bytes=limit << 20),
        cost_estimate=WORK,
    )(order, *[a for a, _ in inputs])


def shape_of(shape, dtype):
    return jax.ShapeDtypeStruct(shape, dtype)


def normalized(values):
    row_mean = jnp.mean(values, axis=-1, keepdims=True)
    centered = values - row_mean
    rstd = lax.rsqrt(jnp.mean(centered * centered, axis=-1, keepdims=True) + epsilon)
    return centered * rstd, rstd


def first_norm(order, tokens, came, other_mine, other_came, vectors):
    _, block, width = tokens.shape

    def kernel(order, mine_ref, came_ref, other_mine_ref, other_came_ref, vec_ref, out_ref):
        def write(ref):
            xhat, _ = normalized(ref[...].astype(f32))
            out_ref[...] = (xhat * vec_ref[0:1] + vec_ref[1:2]).astype(bf16)

        at = pl.program_id(0)
        for i, ref in enumerate((mine_ref.at[0], came_ref, other_mine_ref, other_came_ref)):
            pl.when(at == i)(partial(write, ref))

    def place(i, o):
        return (((i % 2) ^ pair_of(o)) * 2 + ((i // 2) ^ member_of(o)), 0)

    return grid_call(
        "first_norm",
        kernel,
        order,
        (4,),
        [(tokens, pl.BlockSpec((1, block, width), lambda i, o: (pair_of(o), 0, 0)))]
        + [(a, whole_block(a)) for a in (came, other_mine, other_came, vectors)],
        [(shape_of((4 * block, width), bf16), pl.BlockSpec((block, width), place))],
    )[0]


def matrix(ref):
    value = ref[...]
    return value.reshape(value.shape[0] * value.shape[1], value.shape[2])


def project(order, normed, bias, part, weight, tile=256):
    rows, width = normed.shape
    columns = bias.shape[1]

    def kernel(order, lhs_ref, bias_ref, first_ref, second_ref, out_ref):
        total = mm(picked(lhs_ref, order, 0), matrix(first_ref), PLAIN)
        total = total + mm(picked(lhs_ref, order, 4), matrix(second_ref), PLAIN)
        out_ref[...] = (total + bias_ref[part : part + 1]).astype(bf16)

    return grid_call(
        "project",
        kernel,
        order,
        (columns // tile,),
        [(normed, whole_block(normed)), (bias, pl.BlockSpec((2, tile), lambda j, o: (0, j)))]
        + weight.tiles(columns=tile),
        [(shape_of((rows, columns), bf16), pl.BlockSpec((rows, tile), lambda j, o: (0, j)))],
    )[0]


def out_and_norm(order, mixed, tokens, vectors, weight, block=256):
    rows, width = mixed.shape

    def kernel(order, lhs_ref, tok_ref, vec_ref, *rest):
        middle_ref, norm_ref = rest[-2:]
        left = [picked(lhs_ref, order, i, mixed_block) for i in (0, 4)]
        for at, views in enumerate(weight.views(rest[:-2])):
            total = sum(mm(l, flat(*view), PLAIN) for l, view in zip(left, views))
            start = pl.multiple_of((member_of(order) ^ at) * (width // 2), 128)
            middle_ref[:, pl.ds(start, width // 2)] = total
        middle = tok_ref[...].astype(f32) + (middle_ref[...] + vec_ref[4:5])
        middle_ref[...] = middle
        xhat, _ = normalized(middle)
        norm_ref[...] = (xhat * vec_ref[2:3] + vec_ref[3:4]).astype(bf16)

    row = pl.BlockSpec((block, width), lambda i, o: (i, 0))
    return grid_call(
        "out_and_norm",
        kernel,
        order,
        (rows // block,),
        [(mixed, row), (tokens, row)]
        + [(vectors, whole_block(vectors))]
        + weight.inputs(),
        [(shape_of((rows, width), f32), row), (shape_of((rows, width), bf16), row)],
    )


ROOT = math.sqrt(2.0 / math.pi)


def gelu_and_slope(z):
    inner = jnp.tanh(ROOT * (z + 0.044715 * (z * z * z)))
    half_up = 0.5 * (1.0 + inner)
    slope = half_up + 0.5 * z * (1.0 - inner * inner) * (ROOT * (1.0 + 3 * 0.044715 * (z * z)))
    return z * half_up, slope


def feed_up(order, normed, bias, part, weight, tile=256):
    rows, width = normed.shape
    columns = bias.shape[1]

    def kernel(order, lhs_ref, bias_ref, first_ref, second_ref, act_ref, slope_ref):
        total = mm(picked(lhs_ref, order, 0), matrix(first_ref), PLAIN)
        total = total + mm(picked(lhs_ref, order, 4), matrix(second_ref), PLAIN)
        act, slope = gelu_and_slope(total + bias_ref[part : part + 1])
        act_ref[...] = act.astype(bf16)
        slope_ref[...] = slope.astype(bf16)

    out = pl.BlockSpec((rows, tile), lambda j, o: (0, j))
    return grid_call(
        "feed_up",
        kernel,
        order,
        (columns // tile,),
        [(normed, whole_block(normed)), (bias, pl.BlockSpec((2, tile), lambda j, o: (0, j)))]
        + weight.tiles(columns=tile),
        [(shape_of((rows, columns), bf16), out)] * 2,
    )


def own_and_sent(rows, width, tile):
    place = (lambda j, h, o: (0, j)) if tile < width else (lambda j, h, o: (0, 0))
    spec = pl.BlockSpec((rows, tile), place)
    return [(shape_of((rows, width), f32), spec), (shape_of((rows, width), bf16), spec)]


def half_rows(ref):
    rows = ref.shape[0] // 2
    return pl.ds(pl.multiple_of(pl.program_id(1) * rows, rows), rows)


def keep_or_send(own_ref, sent_ref, values):
    def save(ref):
        for where, value in values:
            ref[where] = value.astype(ref.dtype)

    pl.when(pl.program_id(1) == 0)(partial(save, own_ref))
    pl.when(pl.program_id(1) == 1)(partial(save, sent_ref))


def spread(order, totals):
    found = []
    for half, total in enumerate(totals):
        for k in range(2):
            block = owner(order, 4 * half + 2 * pl.program_id(0) + k)
            here = pl.ds(pl.multiple_of(block * 128, 128), 128)
            found.append(((slice(None), here), total[:, 128 * k : 128 * (k + 1)]))
    return found


def feed_down(order, acts, weight, tile=256):
    rows, columns = acts[0].shape
    width = 1024

    def kernel(order, first_act, second_act, *rest):
        weights, own_ref, sent_ref = rest[:4], rest[4], rest[5]
        here = half_rows(first_act)
        total = 0.0
        for part, act_ref in enumerate((first_act, second_act)):
            for half in range(2):
                left = picked(act_ref.at[here], order, 4 * half)
                total = total + mm(left, matrix(weights[2 * part + half]), PLAIN)
        keep_or_send(own_ref, sent_ref, [(Ellipsis, total)])

    return grid_call(
        "feed_down",
        kernel,
        order,
        (width // tile, 2),
        [(act, whole_block(act)) for act in acts] + weight.tiles(columns=tile),
        own_and_sent(rows // 2, width, tile),
    )


def feed_down_back(order, grad, slope, weight):
    rows, width = grad.shape
    columns = slope.shape[1]

    def kernel(order, lhs_ref, slope_ref, first_ref, second_ref, out_ref, sum_ref):
        @pl.when((pl.program_id(0) == 0) & (pl.program_id(1) == 0))
        def _():
            sum_ref[...] = jnp.zeros_like(sum_ref)

        here = half_rows(lhs_ref)
        left = lhs_ref[here]
        totals = [mm(left, matrix(ref), ACROSS) for ref in (first_ref, second_ref)]
        for (_, place), total in spread(order, totals):
            low = (total * slope_ref[here, place].astype(f32)).astype(bf16)
            out_ref[here, place] = low
            sum_ref[:, place] += rows_of_eight(low.astype(f32))

    return grid_call(
        "feed_down_back",
        kernel,
        order,
        (2, 2),
        [(grad, whole_block(grad)), (slope, whole_block(slope))] + weight.tiles(blocks=2),
        [
            (shape_of((rows, columns), bf16), pl.BlockSpec((rows, columns), lambda i, h, o: (0, 0))),
            (shape_of((8, columns), f32), pl.BlockSpec((8, columns), lambda i, h, o: (0, 0))),
        ],
    )


def feed_up_back(order, grads, weight):
    rows, columns = grads[0].shape
    width = 1024

    def kernel(order, first_grad, second_grad, *rest):
        weights, own_ref, sent_ref = rest[:4], rest[4], rest[5]
        here = half_rows(first_grad)
        totals = [
            mm(first_grad[here], matrix(weights[half]), ACROSS)
            + mm(second_grad[here], matrix(weights[2 + half]), ACROSS)
            for half in range(2)
        ]
        keep_or_send(own_ref, sent_ref, spread(order, totals))

    return grid_call(
        "feed_up_back",
        kernel,
        order,
        (2, 2),
        [(grad, whole_block(grad)) for grad in grads] + weight.tiles(blocks=2),
        own_and_sent(rows // 2, width, width),
    )


def rows_of_eight(value):
    return jnp.sum(value.reshape(value.shape[0] // 8, 8, value.shape[1]), axis=0)


def norm_back(xhat, rstd, grad_norm, gain):
    scaled = grad_norm * gain
    return rstd * (
        scaled
        - jnp.mean(scaled, axis=-1, keepdims=True)
        - xhat * jnp.mean(scaled * xhat, axis=-1, keepdims=True)
    )


def middle_back(order, own, came, middle, grad_out, vectors, weight, block=256):
    rows, width = middle.shape
    half_width = width // 2

    def kernel(order, own_ref, came_ref, middle_ref, dy_ref, vec_ref, *rest):
        grad_ref, branch_ref, keep_ref, sent_ref, sum_ref, tmp, low_ref = rest[-7:]

        @pl.when(pl.program_id(0) == 0)
        def _():
            sum_ref[...] = jnp.zeros_like(sum_ref)

        grad_norm = own_ref[...] + came_ref[...].astype(f32)
        xhat, rstd = normalized(middle_ref[...])
        grad_out = dy_ref[...].astype(f32)
        grad_middle = grad_out + norm_back(xhat, rstd, grad_norm, vec_ref[2:3])
        grad_ref[...] = grad_middle
        low = grad_middle.astype(bf16)
        low_ref[...] = low
        sum_ref[0] += rows_of_eight(grad_norm * xhat)
        sum_ref[1] += rows_of_eight(grad_norm)
        sum_ref[2] += rows_of_eight(low.astype(f32))
        sum_ref[3] += rows_of_eight(grad_out)
        views = weight.views(rest[:-7])
        member = member_of(order)
        for i in range(4):
            from_ = i ^ (member * 2 + pair_of(order))
            branch_ref[:, 256 * i : 256 * i + 256] = low_ref[:, pl.ds(pl.multiple_of(from_ * 256, 128), 256)]
        for half in range(2):
            total = 0.0
            for at, pair in enumerate(views):
                start = pl.multiple_of((member ^ at) * half_width, 128)
                total = total + mm(low_ref[:, pl.ds(start, half_width)], flat(*pair[half]), ACROSS)
            for k in range(4):
                here = pl.ds(pl.multiple_of(mixed_block(order, 4 * half + k) * 128, 128), 128)
                tmp[:, here] = total[:, 128 * k : 128 * (k + 1)].astype(bf16)
        keep_ref[...] = tmp[:, :half_width]
        sent_ref[...] = tmp[:, half_width:]

    row = pl.BlockSpec((block, width), lambda i, o: (i, 0))
    part = pl.BlockSpec((block, half_width), lambda i, o: (i, 0))
    return grid_call(
        "middle_back",
        kernel,
        order,
        (rows // block,),
        [(own, row), (came, row), (middle, row), (grad_out, row), (vectors, whole_block(vectors))]
        + weight.inputs(),
        [
            (shape_of((rows, width), f32), row),
            (shape_of((rows, width), bf16), row),
            (shape_of((rows, half_width), bf16), part),
            (shape_of((rows, half_width), bf16), part),
            (shape_of((4, 8, width), f32), pl.BlockSpec((4, 8, width), lambda i, o: (0, 0, 0))),
        ],
        scratch=[pltpu.VMEM((block, width), bf16)] * 2,
    )


def project_back(order, grads, weight):
    rows = grads[0][0].shape[0]
    block = rows // 4
    width = 1024
    given = [g for half in grads for g in half]

    def kernel(order, *rest):
        weights, own_ref, sent_ref = rest[6:10], rest[10], rest[11]

        def left(part):
            found = []
            for k in range(2):
                at = (k ^ pair_of(order)) * 2 + (pl.program_id(1) ^ member_of(order))
                here = pl.ds(pl.multiple_of(at * block, block), block)
                found.append(
                    jnp.concatenate([r[here] for r in rest[3 * part : 3 * part + 3]], axis=1)
                )
            return jnp.concatenate(found)

        lefts = [left(0), left(1)]
        totals = [
            mm(lefts[0], matrix(weights[half]), ACROSS)
            + mm(lefts[1], matrix(weights[2 + half]), ACROSS)
            for half in range(2)
        ]
        keep_or_send(own_ref, sent_ref, spread(order, totals))

    return grid_call(
        "project_back",
        kernel,
        order,
        (2, 2),
        [(g, whole_block(g)) for g in given] + weight.tiles(blocks=2),
        own_and_sent(rows // 2, width, width),
    )


def first_back(order, own, came, tokens, grad_middle, vectors, block=256):
    rows, width = own.shape

    def kernel(order, own_ref, came_ref, tok_ref, mid_ref, vec_ref, out_ref, sum_ref):
        @pl.when(pl.program_id(0) == 0)
        def _():
            sum_ref[...] = jnp.zeros_like(sum_ref)

        grad_norm = own_ref[...] + came_ref[...].astype(f32)
        xhat, rstd = normalized(tok_ref[...].astype(f32))
        total = mid_ref[...] + norm_back(xhat, rstd, grad_norm, vec_ref[0:1])
        out_ref[...] = total.astype(bf16)
        sum_ref[0] += rows_of_eight(grad_norm * xhat)
        sum_ref[1] += rows_of_eight(grad_norm)

    row = pl.BlockSpec((block, width), lambda i, o: (i, 0))
    return grid_call(
        "first_back",
        kernel,
        order,
        (rows // block,),
        [(own, row), (came, row), (tokens, row), (grad_middle, row), (vectors, whole_block(vectors))],
        [
            (shape_of((rows, width), bf16), row),
            (shape_of((2, 8, width), f32), pl.BlockSpec((2, 8, width), lambda i, o: (0, 0, 0))),
        ],
    )


def weight_grad(order, first, count, left, rights, block_of=owner, extra=None):
    wide = sum(columns for _, columns, _ in rights)
    extra = extra or ()
    more = extra[0].shape[2] if extra else 0
    together = 4

    def kernel(order, left_ref, *rest):
        right_refs, out_ref = rest[: len(rights)], rest[-1]
        at = first + together * pl.program_id(0)
        lefts = [lanes(left_ref, block_of(order, at + k)) for k in range(together)]
        picked_left = jnp.concatenate(lefts, axis=1)
        start = 0
        for ref in right_refs:
            total = mm(picked_left, ref[...], DOWN)
            width = total.shape[1]
            out_ref[:, :, start : start + width] = total.reshape(together, 128, width).astype(bf16)
            start += width
        if extra:
            kept, came = rest[len(rights) : -1]
            out_ref[:, :, start:] = (kept[...].astype(f32) + came[...].astype(f32)).astype(bf16)

    def right_spec(array, columns, which):
        return pl.BlockSpec(
            (array.shape[0], columns), lambda *_: (0, which), pipeline_mode=pl.Buffered(1)
        )

    def extra_spec(array, which):
        return pl.BlockSpec(
            (together, 128, more // 2), lambda i, o: (first // together + i, 0, which)
        )

    return grid_call(
        "weight_grad",
        kernel,
        order,
        (count // together,),
        [(left, whole_block(left))]
        + [(right[0], right_spec(*right)) for right in rights]
        + [(a, extra_spec(a, extra[2])) for a in extra[:2]],
        [
            (
                shape_of((count, 128, wide + more // 2), bf16),
                pl.BlockSpec((together, 128, wide + more // 2), lambda i, o: (i, 0, 0)),
            )
        ],
    )[0]


def head_of(order, part):
    return member_of(order) * 8 + (pair_of(order) ^ part) * 4 + 2 * pl.program_id(0)


def team_attend_kernel(part, order, q_ref, k_ref, v_ref, o_ref, total_ref, vt, su):
    at = pl.program_id(1)
    block = q_ref.shape[0]

    @pl.when(at == 0)
    def _():
        vt[...] = v_ref[...].T
        set_bias(order[2], head_of(order, part), su)

    def branch(b):
        nk = (b + 1) * block
        q = q_ref[...]
        outs, totals = [], []
        found = [scores(k_ref, q, h, su, nk, block) for h in range(2)]
        for h, st in enumerate(found):
            m = jnp.max(st, axis=0, keepdims=True)
            p = jnp.exp(st - m)
            l = jnp.sum(p, axis=0, keepdims=True)
            ot = mm(vt[64 * h : 64 * h + 64, :nk], p.astype(bf16), PLAIN)
            outs.append(ot / l)
            totals.append(m + jnp.log(l))
        o_ref[...] = jnp.concatenate(outs, axis=0).T.astype(bf16)
        total_ref[0] = jnp.concatenate(totals + [jnp.zeros((6, block), f32)], axis=0)

    for b in range(k_ref.shape[0] // block):
        pl.when(at == b)(partial(branch, b))


def kept_place(i, o):
    return ((i % 2) ^ member_of(o)) * 2 + ((i // 2) ^ pair_of(o))


def team_attend(order, qkv, part, block):
    rows = qkv.shape[0]
    whole = lambda kind: pl.BlockSpec((rows, 128), lambda p, i, o: (0, 2 * kind + p))
    return pl.pallas_call(
        partial(team_attend_kernel, part),
        name="team_attend",
        grid_spec=pltpu.PrefetchScalarGridSpec(
            num_scalar_prefetch=1,
            grid=(2, rows // block),
            in_specs=[pl.BlockSpec((block, 128), lambda p, i, o: (i, p)), whole(1), whole(2)],
            out_specs=[
                pl.BlockSpec((block, 128), lambda p, i, o: (kept_place(i, o), p)),
                pl.BlockSpec((1, 8, block), lambda p, i, o: (p, 0, i)),
            ],
            scratch_shapes=[pltpu.VMEM((128, rows), bf16), pltpu.VMEM((2, rows, 128), f32)],
        ),
        out_shape=[shape_of((rows, 256), bf16), shape_of((2, 8, rows), f32)],
        compiler_params=pltpu.CompilerParams(vmem_limit_bytes=16 << 20),
        cost_estimate=WORK,
    )(order, qkv, qkv, qkv)


def team_back_kernel(
    part, order, q_ref, k_ref, v_ref, g_ref, total_ref, dq_ref, dk_ref, dv_ref, sum_ref,
    kt, su, dk, dv
):
    at = pl.program_id(1)
    block = q_ref.shape[0]
    blocks = k_ref.shape[0] // block

    @pl.when(at == 0)
    def _():
        kt[...] = k_ref[...].T
        set_bias(order[2], head_of(order, part), su)
        dk[...] = jnp.zeros_like(dk)
        dv[...] = jnp.zeros_like(dv)
        sum_ref[...] = jnp.zeros_like(sum_ref)

    def branch(b):
        nk = (b + 1) * block
        q, g = q_ref[...], g_ref[...]
        outs, dks, dvs = [], [], []
        found = [scores(k_ref, q, h, su, nk, block) for h in range(2)]
        halves = [half(g, h) for h in range(2)]
        products = [mm(v_ref[:nk], gm, ACROSS) for gm in halves]
        for h in range(2):
            p = jnp.exp(found[h] - total_ref[0, h : h + 1])
            gm, dp = halves[h], products[h]
            inner = jnp.sum(p * dp, axis=0, keepdims=True)
            ds = (p * (dp - inner)).astype(bf16)
            outs.append(mm(kt[64 * h : 64 * h + 64, :nk], ds, PLAIN))
            dks.append(mm(ds, half(q, h), PLAIN))
            dvs.append(mm(p.astype(bf16), gm, PLAIN))
        low = (jnp.concatenate(outs, axis=0).T * 0.125).astype(bf16)
        dq_ref[...] = low
        sum_ref[0, 0] += rows_of_eight(low.astype(f32))
        dk[:nk] += dks[0] + dks[1]
        dv[:nk] += dvs[0] + dvs[1]

    for b in range(blocks):
        pl.when(at == b)(partial(branch, b))

    @pl.when(at == blocks - 1)
    def _():
        dk_ref[...] = (dk[...] * 0.125).astype(bf16)
        low = dv[...].astype(bf16)
        dv_ref[...] = low
        sum_ref[0, 1] = rows_of_eight(low.astype(f32))


def team_back(order, qkv, grad, totals, part, block):
    rows = qkv.shape[0]
    whole = lambda kind: pl.BlockSpec((rows, 128), lambda p, i, o: (0, 2 * kind + p))
    by_rows = pl.BlockSpec((block, 128), lambda p, i, o: (i, p))
    by_head = pl.BlockSpec((rows, 128), lambda p, i, o: (0, p))
    return pl.pallas_call(
        partial(team_back_kernel, part),
        name="team_back",
        grid_spec=pltpu.PrefetchScalarGridSpec(
            num_scalar_prefetch=1,
            grid=(2, rows // block),
            in_specs=[
                by_rows,
                whole(1),
                whole(2),
                pl.BlockSpec((block, 128), lambda p, i, o: (kept_place(i, o), 2 * part + p)),
                pl.BlockSpec((1, 8, block), lambda p, i, o: (p, 0, i)),
            ],
            out_specs=[
                by_rows,
                by_head,
                by_head,
                pl.BlockSpec((1, 2, 8, 128), lambda p, i, o: (p, 0, 0, 0)),
            ],
            scratch_shapes=[
                pltpu.VMEM((128, rows), bf16),
                pltpu.VMEM((2, rows, 128), f32),
                pltpu.VMEM((rows, 128), f32),
                pltpu.VMEM((rows, 128), f32),
            ],
        ),
        out_shape=[shape_of((rows, 256), bf16)] * 3 + [shape_of((2, 2, 8, 128), f32)],
        compiler_params=pltpu.CompilerParams(vmem_limit_bytes=24 << 20),
        cost_estimate=WORK,
    )(order, qkv, qkv, qkv, grad, totals)


def joined(first, second):
    count, rows, width = first.shape

    def kernel(first_ref, second_ref, out_ref):
        out_ref[:count] = first_ref[...]
        out_ref[count:] = second_ref[...]

    return pl.pallas_call(
        kernel,
        name="joined",
        out_shape=shape_of((2 * count, rows, width), first.dtype),
        compiler_params=pltpu.CompilerParams(vmem_limit_bytes=12 << 20),
        cost_estimate=WORK,
    )(first, second)


def qkv_unit(order, qkv_weight, packed):
    def kernel(order, qkv_ref, packed_ref, unit_ref):
        unit_ref[0, :128] = jnp.concatenate(
            [
                qkv_ref[:, n * 192 + kind * 64 : n * 192 + kind * 64 + 64]
                for kind in range(3)
                for n in range(4)
            ],
            axis=1,
        )
        unit_ref[0, 128:] = jnp.concatenate([packed_ref[...], jnp.zeros((16, 640), bf16)], axis=1)

    share = lambda i, o: (0, member_of(o) * 2 + pair_of(o))
    return grid_call(
        "qkv_unit",
        kernel,
        order,
        (1,),
        [(qkv_weight, pl.BlockSpec((128, 768), share)), (packed, whole_block(packed))],
        [(shape_of((1, 144, 768), bf16), pl.BlockSpec((1, 144, 768), lambda i, o: (0, 0, 0)))],
    )[0]


def other_units(order, out_weight, up_weight, down_weight):
    def kernel(order, out_ref, up_ref, down_ref, out_unit, own_unit, other_unit, down_unit):
        c, x = member_of(order), pair_of(order)
        out_unit[0] = out_ref[...]
        for i in range(8):
            own_unit[0, :, 128 * i : 128 * i + 128] = lanes(up_ref, i * 4 + x * 2 + c)
            other_unit[0, :, 128 * i : 128 * i + 128] = lanes(up_ref, i * 4 + (1 - x) * 2 + c)
        down_unit[0] = down_ref[...]

    shapes = [(1, 128, 512), (1, 128, 1024), (1, 128, 1024), (1, 128, 1024)]
    return grid_call(
        "other_units",
        kernel,
        order,
        (1,),
        [
            (out_weight, pl.BlockSpec((128, 512), lambda i, o: (0, member_of(o)))),
            (up_weight, whole_block(up_weight)),
            (down_weight, pl.BlockSpec((128, 1024), lambda i, o: (o[1], 0))),
        ],
        [(shape_of(s, bf16), pl.BlockSpec(s, lambda i, o: (0, 0, 0))) for s in shapes],
    )


def unpacked(order, mine, came):
    def kernel(order, mine_ref, came_ref, vec_ref, qkv_ref, up_ref, tmp):
        c, x = member_of(order), pair_of(order)
        for i in range(8):
            values = (mine_ref if i < 4 else came_ref)[i % 4].astype(f32)
            start = owner(order, i) * 128
            vec_ref[:, pl.ds(pl.multiple_of(start, 128), 128)] = values
            tmp[i] = values
            for part in range(2):
                row = tmp[i, pl.ds(8 + (x ^ part) * 2 + c, 1)]
                up_ref[part : part + 1, pl.ds(pl.multiple_of(start, 128), 128)] = row
        for part in range(2):
            here = pl.ds(pl.multiple_of(c * 512 + (x ^ part) * 256, 128), 256)
            qkv_ref[part : part + 1] = jnp.concatenate(
                [vec_ref[6:7, here], jnp.zeros((1, 256), f32), vec_ref[7:8, here]], axis=1
            )

    spec = pl.BlockSpec((4, 16, 128), lambda i, o: (0, 8, 0))
    shapes = [(16, 1024), (2, 768), (2, 1024)]
    return grid_call(
        "unpacked",
        kernel,
        order,
        (1,),
        [(mine, spec), (came, spec)],
        [(shape_of(s, f32), pl.BlockSpec(s, lambda i, o: (0, 0))) for s in shapes],
        scratch=[pltpu.VMEM((8, 16, 128), f32)],
    )


def vector_sums(order, middle, pre, heads, first):
    def kernel(order, middle_ref, pre_own, pre_other, own_ref, other_ref, first_ref, out_ref):
        c, x = member_of(order), pair_of(order)
        out_ref[...] = jnp.zeros_like(out_ref)
        for i in range(4):
            out_ref[i : i + 1] = jnp.sum(middle_ref[i], axis=0, keepdims=True)
        for i in range(2):
            out_ref[4 + i : 5 + i] = jnp.sum(first_ref[i], axis=0, keepdims=True)
        for part, ref in enumerate((own_ref, other_ref)):
            for pair in range(2):
                start = (c * 4 + (x ^ part) * 2 + pair) * 128
                here = pl.ds(pl.multiple_of(start, 128), 128)
                for kind in range(2):
                    total = jnp.sum(ref[pair, kind], axis=0, keepdims=True)
                    out_ref[6 + kind : 7 + kind, here] = total
        for part, ref in enumerate((pre_own, pre_other)):
            total = jnp.sum(ref[...], axis=0, keepdims=True)
            for i in range(8):
                start = (i % 2) * 512 + (x ^ part) * 256 + c * 128
                here = pl.ds(pl.multiple_of(start, 128), 128)
                row = 8 + i // 2
                out_ref[row : row + 1, here] = total[:, 128 * i : 128 * i + 128]

    arrays = (middle,) + tuple(pre) + tuple(heads) + (first,)
    return grid_call(
        "vector_sums",
        kernel,
        order,
        (1,),
        [(a, whole_block(a)) for a in arrays],
        [(shape_of((12, 1024), f32), pl.BlockSpec((12, 1024), lambda i, o: (0, 0)))],
    )[0]


def one_of(pair, index):
    return lax.dynamic_index_in_dim(pair, index, 0, keepdims=False)


def flipped(pair, index):
    return jnp.where(index == 0, pair, pair[::-1])


def after(value, *earlier):
    return lax.optimization_barrier((value,) + earlier)[0]


def team_program(
    tokens,
    cotangent,
    lengths,
    first_gain,
    first_shift,
    qkv_weight,
    qv_bias,
    out_weight,
    out_bias,
    second_gain,
    second_shift,
    up_weight,
    up_bias,
    down_weight,
    down_bias,
):
    _, block, width = tokens.shape
    own_rows = 2 * block
    f, s = lax.axis_index("fsdp"), lax.axis_index("seq")
    x, c = s // 2, s % 2
    over_x = lambda v: exchange(v, "seq", 2)
    over_y = lambda v: exchange(v, "fsdp", 1)
    over_z = lambda v, k: exchange(v, "fsdp", 2 * k)

    length = one_of(lengths, x)

    def over_core(value):
        return lax.cond(length > 0, lambda v: exchange(v, "seq", 1), lambda v: v, value)

    order = jnp.stack([f, s, length]).astype(jnp.int32)

    order = [jnp.stack([f, s, length]).astype(jnp.int32)]

    def wait_for(*values):
        order[0] = after(order[0], *values)

    def run(kernel, *operands, **options):
        result = kernel(order[0], *operands, **options)
        wait_for(result[0] if isinstance(result, (list, tuple)) else result)
        return result

    def join(first, second):
        result = joined(after(first, order[0]), second)
        wait_for(result)
        return result

    full = lambda a, b: ((a, 0, a.shape[2], 0), (b, 0, b.shape[2], 0))

    packed = [first_gain, first_shift, second_gain, second_shift, out_bias, down_bias, qv_bias, up_bias]
    packed = jnp.concatenate([v.reshape(-1, 128) for v in packed] + [jnp.zeros((4, 128), bf16)])
    unit_qkv = run(qkv_unit, qkv_weight, packed)
    tokens_came = over_x(one_of(tokens, 1 - x))
    unit_out, unit_up, unit_up_other, unit_down = run(
        other_units, out_weight, up_weight, down_weight
    )
    own_mine = one_of(tokens, x)
    other_mine, other_came = over_core(own_mine), over_core(tokens_came)
    grad_came = over_x(one_of(after(cotangent, tokens_came), 1 - x))
    z_qkv = join(unit_qkv, over_z(unit_qkv, 1))
    z_out = over_z(after(unit_out, z_qkv), 1)
    own_tokens = jnp.concatenate([own_mine, tokens_came])
    wait_for(other_mine, other_came)
    z_qkv = join(z_qkv, over_z(z_qkv, 2))
    y_qkv, xz_qkv = over_y(z_qkv), over_x(z_qkv)
    z_out = join(unit_out, z_out)
    z_out_came = over_z(z_out, 2)
    z_up = over_z(after(unit_up, z_out), 1)

    blocks_at = (jnp.arange(2) ^ x) * 2 + c
    valid = ((blocks_at[:, None] * block + jnp.arange(block)) < length).reshape(own_rows, 1)
    grad_own = jnp.concatenate([one_of(cotangent, x), grad_came])
    grad_own = jnp.where(valid, grad_own, jnp.zeros_like(grad_own))
    grad_other = over_core(grad_own)
    grad_all = jnp.concatenate([grad_own, grad_other])
    wait_for(grad_all)
    z_up = join(unit_up, z_up)
    z_up_came = over_z(z_up, 2)
    z_out = join(z_out, z_out_came)
    y_out = over_y(z_out)
    z_down = over_z(after(unit_down, z_up), 1)
    xy_qkv = over_x(y_qkv)
    qkv_own, qkv_other = full(z_qkv, y_qkv), full(xz_qkv, xy_qkv)
    vectors, bias_qkv, bias_up = run(unpacked, z_qkv, y_qkv)
    normed = run(first_norm, tokens, tokens_came, other_mine, other_came, vectors)
    projected = [None, None]
    mixed, totals = [None, None], [None, None]
    wait_for(xz_qkv)
    projected[0] = run(project, normed, bias_qkv, 0, Weight(qkv_own))
    mixed[0], totals[0] = run(team_attend, projected[0], 0, block)
    z_up = join(z_up, z_up_came)
    y_up = over_y(z_up)
    z_down = join(unit_down, z_down)
    z_down_came = over_z(z_down, 2)
    z_up_other = over_z(after(unit_up_other, z_down), 1)
    projected[1] = run(project, normed, bias_qkv, 1, Weight(qkv_other))
    mixed[1], totals[1] = run(team_attend, projected[1], 1, block)
    z_out_other, y_out_other = over_core(after(z_out, order[0])), over_core(after(y_out, order[0]))
    z_down = join(z_down, z_down_came)
    y_down, xz_down = over_y(z_down), over_x(z_down)
    z_up_other = join(unit_up_other, z_up_other)
    z_up_other_came = over_z(z_up_other, 2)
    out = Weight(full(z_out, y_out), full(z_out_other, y_out_other))
    sent = jnp.concatenate([m[own_rows:] for m in mixed], axis=1)
    mixed_rows = jnp.concatenate([m[:own_rows] for m in mixed] + [over_core(sent)], axis=1)
    middle, norm_own = run(out_and_norm, mixed_rows, own_tokens, vectors, out)
    norm_other = over_core(norm_own)
    wait_for(norm_other)
    norm_all = jnp.concatenate([norm_own, norm_other])

    act, slope, grad_pre, pre_sums = ([None, None] for _ in range(4))
    up_sent, up_kept, up_came = ([None, None] for _ in range(3))

    def up_grad(part, first):
        return run(weight_grad, first, 4, norm_all, [(grad_pre[part], 1024, 0)])

    def down_grad(part, first, count):
        return run(weight_grad, first, count, act[part], [(grad_all, 1024, 0)])

    act[0], slope[0] = run(feed_up, norm_all, bias_up, 0, Weight(full(z_up, y_up)))
    z_up_other = join(z_up_other, z_up_other_came)
    y_up_other = over_y(z_up_other)
    down_kept = down_grad(0, 0, 8)
    up = [full(z_up, y_up), full(z_up_other, y_up_other)]
    xy_down = over_x(y_down)
    down = [full(z_down, y_down), full(xz_down, xy_down)]
    grad_pre[0], pre_sums[0] = run(
        feed_down_back, grad_all, slope[0], Weight(down[0])
    )
    up_sent[0] = up_grad(0, 4)
    up_came[0] = over_y(up_sent[0])
    up_kept[0] = up_grad(0, 0)
    act[1], slope[1] = run(feed_up, norm_all, bias_up, 1, Weight(up[1]))
    down_sent = [None, None]
    for i in (1, 0):
        down_sent[i] = down_grad(1, 4 * i, 4)
    down_came = [over_x(sent) for sent in down_sent]
    grad_pre[1], pre_sums[1] = run(
        feed_down_back, grad_all, slope[1], Weight(down[1])
    )
    wait_for(up_came[0])
    up_sent[1] = up_grad(1, 4)
    up_came[1] = over_y(up_sent[1])
    back_own, back_sent = run(
        feed_up_back,
        grad_pre,
        Weight(*up),
    )
    back_came = over_core(back_sent)
    up_kept[1] = up_grad(1, 0)
    grad_middle, branch, mixed_kept, mixed_sent, middle_sums = run(
        middle_back, back_own, back_came, middle, grad_own, vectors, out
    )
    grad_mixed = jnp.concatenate([mixed_kept, over_core(mixed_sent)])
    out_grad = lambda which: run(
        weight_grad, 0, 8, mixed_rows, [(branch, 512, which)], block_of=mixed_block
    )
    out_sent = out_grad(1)
    out_came = over_core(out_sent)
    out_kept = out_grad(0)

    def added(kept, came):
        return kept.astype(f32) + came.astype(f32)

    def low_sum(kept, came):
        return added(kept, came).astype(bf16)

    def z_pieces(total):
        return [total[k].astype(bf16) for k in (1, 2, 3)]

    def sum_z(total, pieces):
        result = total[0]
        for k, piece in enumerate(pieces):
            result = result + over_z(piece, k + 1).astype(f32)
        return result

    def qkv_grad(grads, first, part):
        rights = [(grad, 256, 0) for grad in grads]
        return run(weight_grad, first, 4, normed, rights, extra=(out_kept, out_came, part))

    def z_far(total):
        return total[2:].astype(bf16)

    def z_near(total, far_came):
        total = added(total[:2], far_came)
        return total[0], total[1].astype(bf16)

    up_x = low_sum(up_kept[1], up_came[1])
    up_x_came = over_x(up_x)
    down_y = low_sum(down_kept[4:], down_came[1])
    down_y_came = over_y(down_y)
    wait_for(up_x, down_y)
    *heads_other, sums_other = run(team_back, projected[1], grad_mixed, totals[1], 1, block)
    other_y_came = over_y(qkv_grad(heads_other, 4, 1))
    down_total = added(low_sum(after(down_kept[:4], order[0]), down_came[0]), down_y_came)
    down_far = z_far(down_total)
    down_far_came = over_z(down_far, 2)
    wait_for(down_far)
    other_kept = qkv_grad(heads_other, 0, 1)
    *heads_own, sums_own = run(team_back, projected[0], grad_mixed, totals[0], 0, block)
    other_x = low_sum(other_kept, other_y_came)
    other_x_came = over_x(other_x)
    wait_for(other_x)
    own_y_came = over_y(qkv_grad(heads_own, 4, 0))
    up_total = added(low_sum(after(up_kept[0], order[0]), up_came[0]), up_x_came)
    up_far = z_far(up_total)
    up_far_came = over_z(up_far, 2)
    wait_for(up_far)
    first_own, first_sent = run(
        project_back, [heads_own, heads_other], Weight(qkv_own, qkv_other)
    )
    first_came = over_core(first_sent)
    fed_own, fed_sent = run(feed_down, act, Weight(*down))
    block_own = jnp.where(
        valid, middle + (fed_own + over_core(fed_sent).astype(f32)) + vectors[5:6], 0.0
    ).astype(bf16)
    down_sum, down_near = z_near(down_total, after(down_far_came, fed_own))
    down_near_came = over_z(down_near, 1)
    wait_for(down_near)
    up_sum, up_near = z_near(up_total, up_far_came)
    up_near_came = over_z(up_near, 1)
    wait_for(up_near, down_near_came)
    own_kept = qkv_grad(heads_own, 0, 0)
    qkv_total = added(own_kept, own_y_came) + other_x_came.astype(f32)
    qkv_pieces = z_pieces(qkv_total)
    wait_for(*qkv_pieces)
    row_grad, first_sums = run(first_back, first_own, first_came, own_tokens, grad_middle, vectors)

    def to_devices(rows):
        return flipped(jnp.stack([rows[:block], over_x(rows[block:])]), x)

    tokens_grad = to_devices(row_grad)
    block_out = to_devices(block_own)

    def over_pair(total):
        pieces = total.reshape(2, 64, -1)
        rows = flipped(jnp.stack([one_of(pieces, x), over_x(one_of(pieces, 1 - x))]), x)
        return jnp.swapaxes(rows, 0, 1)

    def over_team(total):
        pieces = total.reshape((2, 32) + total.shape[1:])
        rows = flipped(jnp.stack([one_of(pieces, c), over_core(one_of(pieces, 1 - c))]), c)
        return jnp.swapaxes(rows, 0, 1)

    down_sum = added(down_sum, down_near_came)
    up_sum = over_team(over_pair(added(up_sum, up_near_came)))
    up_sum = up_sum.reshape(32, 2, 2, 8, 128).transpose(0, 3, 2, 1, 4).reshape(32, 4096)
    qkv_sum = over_team(over_pair(sum_z(qkv_total, qkv_pieces)))
    out_sum = qkv_sum[..., 768:].reshape(32, width)
    qkv_sum = qkv_sum[..., :768].reshape(32, 2, 2, 3, 4, 64)
    qkv_sum = jnp.transpose(qkv_sum, (0, 1, 2, 4, 3, 5)).reshape(32, 3 * width)

    sums = run(vector_sums, middle_sums, pre_sums, (sums_own, sums_other), first_sums)
    for step in (over_core, over_x, over_y, partial(over_z, k=1), partial(over_z, k=2)):
        sums = sums + step(sums)
    place = f * 4 + s
    pieces = lax.dynamic_slice(sums[:8], (0, place * 32), (8, 32))
    up_piece = lax.dynamic_slice(sums[8:].reshape(4096), (place * 128,), (128,))
    return (
        block_out,
        tokens_grad,
        pieces[4],
        pieces[5],
        qkv_sum,
        pieces[6:8],
        out_sum,
        pieces[2],
        pieces[0],
        pieces[1],
        up_sum,
        up_piece,
        down_sum,
        pieces[3],
    )


def local(tokens, *others):
    width = tokens.shape[2]
    shards = (lax.axis_size("fsdp"), lax.axis_size("seq"))
    hidden = others[10].shape[1]
    if tokens.shape[0] == 2 and tokens.shape[1] % 256 == 0 and shards == (8, 4) and tokens.shape[1] * 4 <= 1024 and (width, hidden) == (1024, 4096):
        return team_program(tokens, *others)
    return general_program(tokens, *others)


def solution(mesh):
    return jax.shard_map(
        local,
        mesh=mesh,
        in_specs=(
            P("fsdp", "seq", None),
            P("fsdp", "seq", None),
            P("fsdp"),
            P("fsdp"),
            P("fsdp"),
            P("fsdp", None),
            P(None, "fsdp"),
            P("fsdp", None),
            P("fsdp"),
            P("fsdp"),
            P("fsdp"),
            P("fsdp", None),
            P("fsdp"),
            P("fsdp", None),
            P("fsdp"),
        ),
        out_specs=(
            P("fsdp", "seq", None),
            P("fsdp", "seq", None),
            P(("fsdp", "seq")),
            P(("fsdp", "seq")),
            P(("fsdp", "seq"), None),
            P(None, ("fsdp", "seq")),
            P(("fsdp", "seq"), None),
            P(("fsdp", "seq")),
            P(("fsdp", "seq")),
            P(("fsdp", "seq")),
            P(("fsdp", "seq"), None),
            P(("fsdp", "seq")),
            P(("fsdp", "seq"), None),
            P(("fsdp", "seq")),
        ),
        check_vma=False,
    )
```
